512 devices in a mesh: px: 32 (over x, z_hi, core), lt: 16 (over y, z_lo).
Axes of the slice: x: 4, y: 8, z: 8 (z_hi: 4, z_lo: 2; z = z_hi * 2 + z_lo), core: 2. Of those that a mesh axis runs over, the one named last changes fastest.
Arguments:
- observed: bfloat16 [3, 512, 262144], P(None, 'lt', 'px'), may hold values from 0 to 1
- shadow: int32 [512, 262144], P('lt', 'px'), may hold values from 0 to 1, as said below
- view_ids: int32 [262144], P('px'), may hold values from 0 to 15
- surface_points: float32 [3, 262144], P(None, 'px'), may hold values from -1 to 1
- frame_coords: float32 [2, 262144], P(None, 'px'), may hold values from 0 to 1
- pixel_params: float32 [12, 262144], P(None, 'px'), may hold values from -3.1416 to 3.1416, as said below
- light_power: float32 [3, 512], P(None, 'lt'), may hold values from 4 to 40
- light_pos: float32 [3, 512], P(None, 'lt'), may hold values from -6 to 6, as said below
- camera_pos: float32 [3, 16], replicated, may hold values from -7 to 7, as said below
Outputs:
- new_params: float32 [12, 262144], P(None, 'px')
- new_power: float32 [3, 512], P(None, 'lt')
- new_light_pos: float32 [3, 512], P(None, 'lt')
- loss: float32 [], replicated
The draws below stay inside these ranges and needn't reach their ends.
Inputs may be any that keep to these rules, and one draw needn't show every extreme that they name: `shadow`: 1 where the light reaches the pixel, 0 elsewhere. `pixel_params`: rows 0 to 2 diffuse albedo in 0.05 to 0.9, rows 3 to 5 specular albedo in 0.05 to 1, rows 6 and 7 logarithms of the two roughnesses in -2.5 to -0.7, rows 8 and 9 normal tilts in -0.4 to 0.4, row 10 an angle in -pi to pi, row 11 reflectance at normal incidence in 0.02 to 0.3. `light_pos`: each light lies 4 to 6 from the anchor, at most 1 radian from the third axis. `camera_pos`: each camera lies 5 to 7 from the anchor, at most 0.8 radian from the third axis.
All inputs are finite; a program needn't handle non-finite values.
Results may differ from the reference program's by a relative error of at most 0.0003.
Values sent between devices are 32-bit elements; how exact they have to be, the bound alone decides.
No kernel may reach another device: no remote copies, remote signals or barrier semaphores. Data moves between devices by JAX's collectives and lax.ppermute only.
A program may use at most 64 MiB of HBM per device.

```python
import math
import jax
import jax.numpy as jnp
from jax import lax

PIX_DEV = 8192
VIEWS = 16
PIXELS = 262144
LIGHTS = 512


def draw_shadow(key, part):
    pixel_rank = jnp.arange(PIXELS, dtype=jnp.int32)
    light_rank = jnp.arange(LIGHTS, dtype=jnp.int32)
    pixel_factor = (PIXELS + 2 * pixel_rank) * 90 // PIXELS
    light_factor = (LIGHTS + 2 * light_rank) * 90 // LIGHTS
    threshold = light_factor[:, None] * pixel_factor[None, :]
    drawn = jax.random.randint(jax.random.fold_in(key, 11), (LIGHTS, PIXELS), 0, 72900, dtype=jnp.int32)
    return (drawn < threshold).astype(jnp.int32)


def draw_pixel_params(key, part):
    lower = jnp.array([0.05, 0.05, 0.05, 0.05, 0.05, 0.05, -2.5, -2.5, -0.4, -0.4, -math.pi, 0.02], jnp.float32)
    upper = jnp.array([0.9, 0.9, 0.9, 1.0, 1.0, 1.0, -0.7, -0.7, 0.4, 0.4, math.pi, 0.3], jnp.float32)
    unit = jax.random.uniform(jax.random.fold_in(key, 21), (12, PIXELS), jnp.float32)
    return lower[:, None] + (upper - lower)[:, None] * unit


def sphere_points(key, number, near, far, widest):
    radius = jax.random.uniform(jax.random.fold_in(key, 1), (number,), jnp.float32, near, far)
    polar_angle = jax.random.uniform(jax.random.fold_in(key, 2), (number,), jnp.float32, 0.0, widest)
    azimuth = jax.random.uniform(jax.random.fold_in(key, 3), (number,), jnp.float32, -math.pi, math.pi)
    return jnp.stack([radius * jnp.sin(polar_angle) * jnp.cos(azimuth), radius * jnp.sin(polar_angle) * jnp.sin(azimuth), radius * jnp.cos(polar_angle)])


def draw_light_pos(key, part):
    return sphere_points(jax.random.fold_in(key, 31), LIGHTS, 4.0, 6.0, 1.0)


def draw_camera_pos(key, part):
    return sphere_points(jax.random.fold_in(key, 41), VIEWS, 5.0, 7.0, 0.8)


def with_ends(entries, rng, low, top_value):
    extent = entries.shape
    spot = [jax.random.randint(jax.random.fold_in(rng, axis), (), 0, extent[axis]) for axis in range(len(extent))]
    entries = entries.at[tuple(spot)].set(low)
    longest = extent.index(max(extent))
    spot[longest] = (spot[longest] + 1) % extent[longest]
    return entries.at[tuple(spot)].set(top_value)


def steps_of(own_key, extent, split, least, top_value):
    level = 1.0
    for position, shards_of in split:
        draws = jax.random.uniform(jax.random.fold_in(jax.random.fold_in(own_key, 6), position), (shards_of,), jnp.float32, least / len(split), top_value / len(split))
        level = level * jnp.repeat(jnp.exp(draws), extent[position] // shards_of).reshape((-1,) + (1,) * (len(extent) - 1 - position))
    return level


def setup_inputs(seed: int = 0) -> dict:
    key_of = jax.random.split(jax.random.key(seed), 10)
    observed = jnp.clip(1.0 * jax.random.uniform(key_of[0], (3, LIGHTS, PIXELS), jnp.float32) ** steps_of(key_of[0], (3, LIGHTS, PIXELS), ((1, 16), (2, 32)), -0.2, 0.2), 0.0, 1.0).astype(jnp.bfloat16)
    shadow = draw_shadow(jax.random.fold_in(key_of[9], 71), 0)
    view_ids = with_ends(jax.random.randint(key_of[2], (PIXELS,), 0, VIEWS), jax.random.fold_in(key_of[2], 1), 0, VIEWS - 1).astype(jnp.int32)
    surface_points = jnp.clip(jax.random.uniform(key_of[3], (3, PIXELS), jnp.float32, -1.0, 1.0) * steps_of(key_of[3], (3, PIXELS), ((1, 32),), -0.4, 0.0), -1.0, 1.0)
    frame_coords = jnp.clip(1.0 * jax.random.uniform(key_of[4], (2, PIXELS), jnp.float32) ** steps_of(key_of[4], (2, PIXELS), ((1, 32),), -0.2, 0.2), 0.0, 1.0)
    pixel_params = draw_pixel_params(jax.random.fold_in(key_of[9], 71), 0)
    light_power = jnp.clip(jnp.exp(math.log(40.0) - 2.3025851 * jax.random.uniform(key_of[6], (3, LIGHTS), jnp.float32) ** steps_of(key_of[6], (3, LIGHTS), ((1, 16),), -0.2, 0.2)), 4.0, 40.0)
    light_pos = draw_light_pos(jax.random.fold_in(key_of[9], 71), 0)
    camera_pos = draw_camera_pos(jax.random.fold_in(key_of[9], 71), 0)
    return {"observed": observed, "shadow": shadow, "view_ids": view_ids, "surface_points": surface_points, "frame_coords": frame_coords, "pixel_params": pixel_params, "light_power": light_power, "light_pos": light_pos, "camera_pos": camera_pos}


softness = 0.01
epsilon = 1e-06
stride = 0.2

def inner_three(first, second):
    return first[0] * second[0] + first[1] * second[1] + first[2] * second[2]

def cross_three(first, second):
    return [first[1] * second[2] - first[2] * second[1], first[2] * second[0] - first[0] * second[2], first[0] * second[1] - first[1] * second[0]]

def soft_cosine(value):
    return 0.5 * (value + jnp.sqrt(value * value + softness))

def shade(params, points, frames, cameras, light_power, light_pos, visible, observed):
    polar_angle = frames[0]
    azimuth = 2.0 * math.pi * frames[1]
    cos_polar, sin_polar = (jnp.cos(polar_angle), jnp.sin(polar_angle))
    cos_azimuth, sin_azimuth = (jnp.cos(azimuth), jnp.sin(azimuth))
    base_normal = [sin_polar * cos_azimuth, sin_polar * sin_azimuth, cos_polar]
    base_tangent = [cos_polar * cos_azimuth, cos_polar * sin_azimuth, -sin_polar]
    base_bitangent = [-sin_azimuth, cos_azimuth, jnp.zeros_like(cos_azimuth)]
    tilt_u, tilt_v = (params[8], params[9])
    scaled = lax.rsqrt(1.0 + tilt_u * tilt_u + tilt_v * tilt_v)
    normal = [(base_normal[coord] + tilt_u * base_tangent[coord] + tilt_v * base_bitangent[coord]) * scaled for coord in range(3)]
    spin_angle = params[10]
    turned = [jnp.cos(spin_angle) * base_tangent[coord] + jnp.sin(spin_angle) * base_bitangent[coord] for coord in range(3)]
    along_normal = inner_three(turned, normal)
    raw_tangent = [turned[coord] - along_normal * normal[coord] for coord in range(3)]
    inv_length = lax.rsqrt(inner_three(raw_tangent, raw_tangent))
    tangent = [raw_tangent[coord] * inv_length for coord in range(3)]
    bitangent = cross_three(normal, tangent)
    toward = [cameras[coord] - points[coord] for coord in range(3)]
    view_scale = lax.rsqrt(inner_three(toward, toward))
    view_dir = [toward[coord] * view_scale for coord in range(3)]
    light_offset = [light_pos[coord][:, None] - points[coord][None, :] for coord in range(3)]
    distance_sq = inner_three(light_offset, light_offset)
    light_scale = lax.rsqrt(distance_sq)
    light_dir = [light_offset[coord] * light_scale for coord in range(3)]
    halfway = [light_dir[coord] + view_dir[coord][None, :] for coord in range(3)]
    half_scale = lax.rsqrt(inner_three(halfway, halfway))
    half_dir = [halfway[coord] * half_scale for coord in range(3)]
    alpha_u = jnp.exp(params[6])
    alpha_v = jnp.exp(params[7])
    fresnel_zero = params[11]

    def smith_lambda(direction):
        along = inner_three(direction, tangent)
        across = inner_three(direction, bitangent)
        lifted = soft_cosine(inner_three(direction, normal))
        ratio = (alpha_u * alpha_u * along * along + alpha_v * alpha_v * across * across) / (lifted * lifted)
        return 0.5 * (jnp.sqrt(1.0 + ratio) - 1.0)
    half_along = inner_three(half_dir, tangent) / alpha_u
    half_across = inner_three(half_dir, bitangent) / alpha_v
    half_normal = inner_three(half_dir, normal)
    quadric = half_along * half_along + half_across * half_across + half_normal * half_normal
    microfacet = 1.0 / (math.pi * alpha_u * alpha_v * quadric * quadric)
    shadowing = 1.0 / ((1.0 + smith_lambda(light_dir)) * (1.0 + smith_lambda(view_dir)))
    cos_view_half = inner_three(view_dir, half_dir)
    fresnel = fresnel_zero + (1.0 - fresnel_zero) * (1.0 - cos_view_half) ** 5
    glossy = microfacet * shadowing * fresnel / (4.0 * soft_cosine(inner_three(view_dir, normal)))
    diffuse_term = soft_cosine(inner_three(light_dir, normal)) / math.pi
    energy = jnp.zeros((), params.dtype)
    for channel in range(3):
        reflected = (params[channel] * diffuse_term + params[3 + channel] * glossy) / distance_sq
        residual = visible * (light_power[channel][:, None] * reflected - observed[channel])
        energy = energy + 0.5 * jnp.sum(residual * residual)
    return energy

def reference(observed, shadow, view_ids, surface_points, frame_coords, pixel_params, light_power, light_pos, camera_pos):
    cameras_all = camera_pos[:, view_ids]

    def step_block(carry, block_index):
        power_sum, pos_sum, energy_sum = carry
        offset = block_index * PIX_DEV

        def window(array):
            return lax.dynamic_slice_in_dim(array, offset, PIX_DEV, array.ndim - 1)
        points = window(surface_points)
        frames = window(frame_coords)
        cameras = window(cameras_all)
        visible = window(shadow).astype(jnp.float32)
        measured = window(observed).astype(jnp.float32)

        def energy_of(params, power, positions):
            return shade(params, points, frames, cameras, power, positions, visible, measured)
        energy, pullback = jax.vjp(energy_of, window(pixel_params), light_power, light_pos)
        grad_block, grad_power, grad_pos = pullback(jnp.ones_like(energy))
        return ((power_sum + grad_power, pos_sum + grad_pos, energy_sum + energy), grad_block)
    start_carry = (jnp.zeros_like(light_power), jnp.zeros_like(light_pos), jnp.zeros((), jnp.float32))
    block_ids = jnp.arange(PIXELS // PIX_DEV, dtype=jnp.int32)
    (grad_power, grad_pos, energy_total), grad_blocks = lax.scan(step_block, start_carry, block_ids)
    grad_params = jnp.moveaxis(grad_blocks, 0, 1).reshape(12, PIXELS)
    pixel_scale = jnp.sqrt(jnp.sum(grad_params * grad_params) / (12 * PIXELS) + epsilon)
    light_sq = jnp.sum(grad_power * grad_power) + jnp.sum(grad_pos * grad_pos)
    light_scale = jnp.sqrt(light_sq / (6 * LIGHTS) + epsilon)
    new_params = pixel_params - stride * grad_params / pixel_scale
    new_power = light_power - stride * grad_power / light_scale
    new_light_pos = light_pos - stride * grad_pos / light_scale
    loss = 2.0 * energy_total / (3 * LIGHTS * PIXELS)
    return (new_params, new_power, new_light_pos, loss)
```

```python
import functools
import math

import jax
import jax.numpy as jnp
from jax import lax
from jax.experimental import pallas as pl
from jax.experimental.pallas import tpu as pltpu
from jax.sharding import Mesh
from jax.sharding import PartitionSpec as P

PX = ("px_0", "px_1", "px_2")
LT = ("lt_0", "lt_1")

SOFT = 0.01
EPS = 1e-06
STRIDE = 0.2
LANES = 128
SUBS = 8
ROWS = 12
BLOCK = 1024
CHUNKS = BLOCK // LANES
RAW = 24
GROUP = 1

(TX, TY, TZ, BX, BY, BZ, NX, NY, NZ, PT, PB, PN, VT, VB, VN, AX2, AY2, IX2, IY2, KG, F0, F1, K5,
 KD0, KD1, KD2, KS0, KS1, KS2) = range(29)
TABLE = 29
(SD0, SD1, SD2, SS0, SS1, SS2, SF, SH, V11, V22, V12, V13, V23, U11, U22, U12, U13, U23, WT, WB) = range(20)
SUMS = 20


def inner_three(first, second):
    return first[0] * second[0] + first[1] * second[1] + first[2] * second[2]


def pixel_frame(row, ids, camera_ref):
    azimuth = 2.0 * math.pi * row(17)
    ca, sa = jnp.cos(row(16)), jnp.sin(row(16))
    cz, sz = jnp.cos(azimuth), jnp.sin(azimuth)
    base_n = [sa * cz, sa * sz, ca]
    base_t = [ca * cz, ca * sz, -sa]
    base_b = [-sz, cz]
    u, v, spin = row(8), row(9), row(10)
    cs, sn = jnp.cos(spin), jnp.sin(spin)
    kappa = lax.rsqrt(1.0 + u * u + v * v)
    along = kappa * (u * cs + v * sn)
    inv = lax.rsqrt(1.0 - along * along)
    n_loc = [kappa, kappa * u, kappa * v]
    t_loc = [-along * n_loc[0] * inv, (cs - along * n_loc[1]) * inv, (sn - along * n_loc[2]) * inv]
    kb = kappa * inv
    b_loc = [kb * (u * sn - v * cs), -kb * sn, kb * cs]

    def world(loc):
        return [
            loc[0] * base_n[0] + loc[1] * base_t[0] + loc[2] * base_b[0],
            loc[0] * base_n[1] + loc[1] * base_t[1] + loc[2] * base_b[1],
            loc[0] * base_n[2] + loc[1] * base_t[2],
        ]

    tangent, bitangent, normal = world(t_loc), world(b_loc), world(n_loc)
    point = [row(12), row(13), row(14)]
    camera = [jnp.full_like(u, camera_ref[c, 0]) for c in range(3)]
    for view in range(1, camera_ref.shape[1]):
        chosen = ids == view
        camera = [jnp.where(chosen, camera_ref[c, view], camera[c]) for c in range(3)]
    toward = [camera[c] - point[c] for c in range(3)]
    scale = lax.rsqrt(inner_three(toward, toward))
    view_dir = [toward[c] * scale for c in range(3)]
    vt, vb, vn = (inner_three(view_dir, f) for f in (tangent, bitangent, normal))
    ax, ay = jnp.exp(row(6)), jnp.exp(row(7))
    ax2, ay2 = ax * ax, ay * ay
    ix2, iy2 = 1.0 / ax2, 1.0 / ay2
    vroot = lax.rsqrt(vn * vn + SOFT)
    cv = 0.5 * (vn + (vn * vn + SOFT) * vroot)
    wv2 = cv * cv + ax2 * vt * vt + ay2 * vb * vb
    rwv = lax.rsqrt(wv2)
    rcv = 1.0 / (cv + wv2 * rwv)
    return dict(
        tangent=tangent, bitangent=bitangent, normal=normal, point=point,
        vt=vt, vb=vb, vn=vn, ax=ax, ay=ay, ax2=ax2, ay2=ay2, ix2=ix2, iy2=iy2,
        vroot=vroot, cv=cv, rwv=rwv, rcv=rcv, kappa=kappa, inv=inv, along=along,
        t_loc=t_loc, b_loc=b_loc,
    )


def pair_terms(px, light, visible, measured):
    lx, ly, lz, pw = light[0], light[1], light[2], light[3:6]
    ot = lx * px(TX) + ly * px(TY) + lz * px(TZ) - px(PT)
    ob = lx * px(BX) + ly * px(BY) + lz * px(BZ) - px(PB)
    on = lx * px(NX) + ly * px(NY) + lz * px(NZ) - px(PN)
    r = lax.rsqrt(ot * ot + ob * ob + on * on)
    id2 = r * r
    lt, lb, ln = ot * r, ob * r, on * r
    m = (lt * px(VT) + lb * px(VB)) + (ln * px(VN) + 1.0)
    a1, a2, a3 = lt + px(VT), lb + px(VB), ln + px(VN)
    b1, b2 = a1 * px(IX2), a2 * px(IY2)
    rq = lax.rsqrt(b1 * a1 + b2 * a2 + a3 * a3)
    rq = rq * rq
    rm = lax.rsqrt(m)
    om = 1.0 - (m * rm) * math.sqrt(0.5)
    om2 = om * om
    om4 = om2 * om2
    s5 = om4 * om
    fresnel = px(F0) + px(F1) * s5
    lsq = ln * ln + SOFT
    rs = lax.rsqrt(lsq)
    cn = 0.5 * (ln + lsq * rs)
    xt, xb = lt * px(AX2), lb * px(AY2)
    wsq = cn * cn + (xt * lt + xb * lb)
    rw = lax.rsqrt(wsq)
    rc = lax.rsqrt(cn + wsq * rw)
    rc = rc * rc
    cni = cn * id2
    mq = m * rq
    bi = (mq * mq) * (rc * cni) * px(KG)
    gi = bi * fresnel
    squares = None
    power_terms = []
    ys = []
    for c in range(3):
        refl = px(KD0 + c) * cni + px(KS0 + c) * gi
        res = visible * (pw[c] * refl - measured[c])
        squares = res * res if c == 0 else squares + res * res
        power_terms.append(res * refl)
        ys.append(res * pw[c])
    dcn = ys[0] * px(KD0) + ys[1] * px(KD1) + ys[2] * px(KD2)
    dgl = ys[0] * px(KS0) + ys[1] * px(KS1) + ys[2] * px(KS2)
    h = gi * dgl
    s = cni * dcn + h
    x = dgl * bi
    mm = rm * (2.0 * (h * rm) - (x * om4) * px(K5))
    hw = h * rw
    uu = hw * rc
    ww = rs * (s - hw * cn)
    v4 = (4.0 * h) * rq
    v1, v2, v3 = v4 * a1, v4 * a2, v4 * a3
    u1, u2 = uu * lt, uu * lb
    sums = [None] * SUMS
    for c in range(3):
        sums[SD0 + c] = ys[c] * cni
        sums[SS0 + c] = ys[c] * gi
    sums[SF] = x - x * s5
    sums[SH] = h
    sums[V11], sums[V22], sums[V12] = v1 * a1, v2 * a2, v1 * a2
    sums[V13], sums[V23] = v1 * a3, v2 * a3
    sums[U11], sums[U22], sums[U12] = u1 * lt, u2 * lb, u1 * lb
    sums[U13], sums[U23] = u1 * ln, u2 * ln
    sums[WT], sums[WB] = ww * lt, ww * lb
    gt = mm * px(VT) - uu * xt - v4 * b1
    gb = mm * px(VB) - uu * xb - v4 * b2
    gn = mm * px(VN) + ww - v3
    radial = lt * gt + lb * gb + ln * gn + 2.0 * s
    gt, gb, gn = (gt - lt * radial) * r, (gb - lb * radial) * r, (gn - ln * radial) * r
    light_terms = power_terms + [
        gt * px(TX + c) + gb * px(BX + c) + gn * px(NX + c) for c in range(3)
    ]
    return sums, light_terms, squares


def fold(x):
    total = x[:SUBS]
    for g in range(1, x.shape[0] // SUBS):
        total = total + x[g * SUBS : (g + 1) * SUBS]
    return total


def gradient_kernel(
    camera_ref, observed_ref, shadow_ref, ids_ref, points_ref, frames_ref, params_ref, power_ref, pos_ref,
    grads_ref, light_ref,
    raw, table, sums_ref, light_wide, light_sum, square_sum,
):
    step = pl.program_id(0)
    lights = shadow_ref.shape[0]
    groups = lights // SUBS
    lane = lax.broadcasted_iota(jnp.int32, (SUBS, lights), 1)
    sub = lax.broadcasted_iota(jnp.int32, (SUBS, lights), 0)

    @pl.when(step == 0)
    def _():
        light_sum[...] = jnp.zeros_like(light_sum)
        square_sum[...] = jnp.zeros_like(square_sum)
        for q in range(6):
            source = pos_ref if q < 3 else power_ref
            values = source[q % 3 : q % 3 + 1, :]
            for g in range(groups):
                picked = jnp.where(lane == sub + g * SUBS, values, 0.0)
                column = jnp.sum(picked, axis=1, keepdims=True)
                light_wide[q, g * SUBS : (g + 1) * SUBS, :] = jnp.broadcast_to(column, (SUBS, LANES))

    for k in range(CHUNKS):
        cut = slice(k * LANES, (k + 1) * LANES)
        raw[k * RAW : k * RAW + 12, :] = params_ref[:, cut]
        raw[k * RAW + 12 : k * RAW + 15, :] = points_ref[:, cut]
        raw[k * RAW + 16 : k * RAW + 18, :] = frames_ref[:, cut]

    def row(q):
        return raw[pl.ds(q, CHUNKS, stride=RAW), :]

    f = pixel_frame(row, ids_ref[...], camera_ref)
    entries = {
        AX2: f["ax2"], AY2: f["ay2"], IX2: f["ix2"], IY2: f["iy2"],
        VT: f["vt"], VB: f["vb"], VN: f["vn"],
        PT: inner_three(f["point"], f["tangent"]),
        PB: inner_three(f["point"], f["bitangent"]),
        PN: inner_three(f["point"], f["normal"]),
        KG: 4.0 * f["rcv"] / (math.pi * f["ax"] * f["ay"]),
        F0: row(11), F1: 1.0 - row(11), K5: (1.0 - row(11)) * (5.0 * math.sqrt(2.0) / 4.0),
    }
    for c in range(3):
        entries[TX + c], entries[BX + c], entries[NX + c] = f["tangent"][c], f["bitangent"][c], f["normal"][c]
        entries[KD0 + c] = row(c) * (1.0 / math.pi)
        entries[KS0 + c] = row(3 + c)
    for q, value in entries.items():
        table[q] = value

    rows = SUBS * GROUP

    def chunk(k, _):
        cut = pl.ds(pl.multiple_of(k * LANES, LANES), LANES)

        def px(q):
            return jnp.broadcast_to(table[q, pl.ds(k, 1), :], (rows, LANES))

        total = None
        squares = None
        for g in range(lights // rows):
            at = slice(g * rows, (g + 1) * rows)
            visible = shadow_ref[at, cut].astype(jnp.float32)
            measured = [observed_ref[c, at, cut].astype(jnp.float32) for c in range(3)]
            sums, light_terms, square = pair_terms(
                px, [light_wide[q, at, :] for q in range(6)], visible, measured
            )
            sums = [fold(x) for x in sums]
            square = fold(square)
            total = sums if total is None else [a + b for a, b in zip(total, sums)]
            squares = square if squares is None else squares + square
            for q in range(6):
                light_sum[q, at, :] += light_terms[q]
        square_sum[...] += squares
        for q in range(SUMS):
            sums_ref[pl.ds(pl.multiple_of(q * BLOCK // LANES * SUBS + k * SUBS, SUBS), SUBS), :] = total[q]
        return 0

    lax.fori_loop(0, CHUNKS, chunk, 0)

    def summed(q):
        start = q * CHUNKS * SUBS
        parts = [sums_ref[pl.ds(start + i, CHUNKS, stride=SUBS), :] for i in range(SUBS)]
        while len(parts) > 1:
            parts = [a + b for a, b in zip(parts[::2], parts[1::2])]
        return parts[0]

    z = [summed(q) for q in range(SUMS)]
    vt, vb, vn = f["vt"], f["vb"], f["vn"]
    uv = z[SH] * f["rwv"] * f["rcv"]
    wv = -z[SH] * f["rwv"] * f["cv"] * f["vroot"]
    u11, u22, u12 = z[U11] + uv * vt * vt, z[U22] + uv * vb * vb, z[U12] + uv * vt * vb
    u13, u23 = z[U13] + uv * vt * vn, z[U23] + uv * vb * vn
    wt, wb = z[WT] + wv * vt, z[WB] + wv * vb
    ax2, ay2, ix2, iy2 = f["ax2"], f["ay2"], f["ix2"], f["iy2"]
    tau_x = (1.0 - iy2) * z[V23] - ay2 * u23 - wb
    tau_y = (ix2 - 1.0) * z[V13] + ax2 * u13 + wt
    tau_z = (iy2 - ix2) * z[V12] + (ay2 - ax2) * u12
    turned = tau_x + f["inv"] * f["along"] * tau_z
    grads = [z[SD0 + c] * (1.0 / math.pi) for c in range(3)] + [z[SS0 + c] for c in range(3)]
    grads.append(ix2 * z[V11] - ax2 * u11 - z[SH])
    grads.append(iy2 * z[V22] - ay2 * u22 - z[SH])
    grads.append(f["kappa"] * (f["t_loc"][1] * tau_y - f["b_loc"][1] * turned))
    grads.append(f["kappa"] * (f["t_loc"][2] * tau_y - f["b_loc"][2] * turned))
    grads.append(tau_z * f["inv"] * f["inv"] * f["kappa"])
    grads.append(z[SF])
    for q in range(ROWS):
        grads_ref[pl.ds(q, CHUNKS, stride=ROWS), :] = grads[q]

    @pl.when(step == pl.num_programs(0) - 1)
    def _():
        wide = lax.broadcasted_iota(jnp.int32, (SUBS, LANES), 1)
        deep = lax.broadcasted_iota(jnp.int32, (SUBS, LANES), 0)
        lines = []
        for q in range(6):
            spread = jnp.zeros((SUBS, LANES), jnp.float32)
            for g in range(groups):
                line = jnp.sum(light_sum[q, g * SUBS : (g + 1) * SUBS, :], axis=1, keepdims=True)
                spread = jnp.where(wide == deep + g * SUBS, line, spread)
            lines.append(jnp.sum(spread, axis=0, keepdims=True))
        lines.append(jnp.sum(square_sum[...], axis=0, keepdims=True))
        tile = jnp.zeros((SUBS, LANES), jnp.float32)
        for q, line in enumerate(lines):
            tile = jnp.where(deep == q, line, tile)
        light_ref[...] = tile


def local_gradients(observed, shadow, view_ids, points, frames, params, power, pos, cameras):
    lights, pixels = shadow.shape
    steps = pixels // BLOCK
    return pl.pallas_call(
        gradient_kernel,
        grid=(steps,),
        in_specs=[
            pl.BlockSpec(memory_space=pltpu.SMEM),
            pl.BlockSpec((3, lights, BLOCK), lambda i: (0, 0, i)),
            pl.BlockSpec((lights, BLOCK), lambda i: (0, i)),
            pl.BlockSpec((CHUNKS, LANES), lambda i: (i, 0)),
            pl.BlockSpec((3, BLOCK), lambda i: (0, i)),
            pl.BlockSpec((2, BLOCK), lambda i: (0, i)),
            pl.BlockSpec((ROWS, BLOCK), lambda i: (0, i)),
            pl.BlockSpec((3, lights), lambda i: (0, 0)),
            pl.BlockSpec((3, lights), lambda i: (0, 0)),
        ],
        out_specs=[
            pl.BlockSpec((CHUNKS * ROWS, LANES), lambda i: (i, 0)),
            pl.BlockSpec((SUBS, LANES), lambda i: (0, 0)),
        ],
        out_shape=[
            jax.ShapeDtypeStruct((pixels // LANES * ROWS, LANES), jnp.float32),
            jax.ShapeDtypeStruct((SUBS, LANES), jnp.float32),
        ],
        scratch_shapes=[
            pltpu.VMEM((CHUNKS * RAW, LANES), jnp.float32),
            pltpu.VMEM((TABLE, SUBS, LANES), jnp.float32),
            pltpu.VMEM((SUMS * CHUNKS * SUBS, LANES), jnp.float32),
            pltpu.VMEM((6, lights, LANES), jnp.float32),
            pltpu.VMEM((6, lights, LANES), jnp.float32),
            pltpu.VMEM((SUBS, LANES), jnp.float32),
        ],
        name="pair_gradients",
    )(cameras, observed, shadow, view_ids.reshape(pixels // LANES, LANES), points, frames, params, power, pos)


def share_kernel(arrived_ref, lights_ref, out_ref):
    parts, rows = arrived_ref.shape[:2]
    for at in range(0, rows, SUBS):
        total = arrived_ref[0, at : at + SUBS, :]
        for i in range(1, parts):
            total = total + arrived_ref[i, at : at + SUBS, :]
        for i in range(parts):
            out_ref[i, at : at + SUBS, :] = total
    tile = lights_ref[0]
    for i in range(1, lights_ref.shape[0]):
        tile = tile + lights_ref[i]
    for i in range(parts):
        out_ref[i, rows : rows + SUBS, :] = tile


def square_kernel(gathered_ref, out_ref):
    parts, rows = gathered_ref.shape[0], gathered_ref.shape[1] - SUBS
    lines = []
    for at in range(0, rows, SUBS):
        total = jnp.zeros((SUBS, LANES), jnp.float32)
        for i in range(parts):
            value = gathered_ref[i, at : at + SUBS, :]
            total = total + value * value
        lines.append(total)
    total = functools.reduce(jnp.add, lines)
    for i in range(out_ref.shape[0]):
        out_ref[i] = total


def whole(x):
    return jnp.sum(jnp.sum(x, axis=0, keepdims=True), axis=1, keepdims=True)


def step_kernel(
    pixel_total, light_total, gathered_ref, squares_ref, own_ref, params_ref, power_ref, pos_ref,
    new_params_ref, new_power_ref, new_pos_ref, loss_ref,
):
    parts, rows = gathered_ref.shape[0], gathered_ref.shape[1] - SUBS
    total = squares_ref[0]
    for i in range(1, squares_ref.shape[0]):
        total = total + squares_ref[i]
    pixel_scale = STRIDE * lax.rsqrt(whole(total) / (ROWS * pixel_total) + EPS)
    deep = lax.broadcasted_iota(jnp.int32, (SUBS, LANES), 0)
    light_sq = jnp.zeros((SUBS, LANES), jnp.float32)
    residual_sq = jnp.zeros((SUBS, LANES), jnp.float32)
    for i in range(parts):
        tile = gathered_ref[i, rows : rows + SUBS, :]
        light_sq = light_sq + jnp.where(deep < 6, tile * tile, 0.0)
        residual_sq = residual_sq + jnp.where(deep == 6, tile, 0.0)
    light_scale = STRIDE * lax.rsqrt(whole(light_sq) / (6 * light_total) + EPS)
    loss_ref[...] = whole(residual_sq) / (3.0 * light_total * pixel_total)
    lights = power_ref.shape[1]
    new_power_ref[...] = power_ref[...] - own_ref[0:3, :lights] * light_scale
    new_pos_ref[...] = pos_ref[...] - own_ref[3:6, :lights] * light_scale
    chunks = rows // ROWS
    for i in range(parts):
        for k in range(chunks):
            cut = slice((i * chunks + k) * LANES, (i * chunks + k + 1) * LANES)
            grad = gathered_ref[i, k * ROWS : (k + 1) * ROWS, :]
            new_params_ref[:, cut] = params_ref[:, cut] - grad * pixel_scale


def broadcast_exchange(x, axes):
    return lax.all_to_all(x, axes, split_axis=0, concat_axis=0, tiled=True)


def shards(observed, shadow, view_ids, points, frames, params, power, pos, cameras):
    lights, pixels = shadow.shape
    px_size, lt_size = lax.axis_size(PX), lax.axis_size(LT)
    grads, light_tile = local_gradients(
        observed, shadow, view_ids, points, frames, params, power, pos, cameras
    )
    share_rows = grads.shape[0] // lt_size
    arrived = broadcast_exchange(grads.reshape(lt_size, share_rows, LANES), LT)
    light_parts = broadcast_exchange(
        jnp.broadcast_to(light_tile[None], (px_size, SUBS, LANES)), PX
    )
    spread = pl.pallas_call(
        share_kernel,
        out_shape=jax.ShapeDtypeStruct((lt_size, share_rows + SUBS, LANES), jnp.float32),
        name="share_sum",
    )(arrived, light_parts)
    own_lights = spread[0, share_rows:, :]
    gathered = broadcast_exchange(spread, LT)
    squares = pl.pallas_call(
        square_kernel,
        out_shape=jax.ShapeDtypeStruct((px_size, SUBS, LANES), jnp.float32),
        name="block_squares",
    )(gathered)
    squares = broadcast_exchange(squares, PX)
    new_params, new_power, new_pos, loss = pl.pallas_call(
        functools.partial(step_kernel, pixels * px_size, lights * lt_size),
        out_shape=(
            jax.ShapeDtypeStruct(params.shape, jnp.float32),
            jax.ShapeDtypeStruct(power.shape, jnp.float32),
            jax.ShapeDtypeStruct(pos.shape, jnp.float32),
            jax.ShapeDtypeStruct((1, 1), jnp.float32),
        ),
        name="step",
    )(gathered, squares, own_lights, params, power, pos)
    return new_params, new_power, new_pos, loss.reshape(())


def solution(mesh):
    torus = Mesh(mesh.devices.reshape(4, 4, 2, 8, 2), PX + LT)
    placed = (
        P(None, LT, PX),
        P(LT, PX),
        P(PX),
        P(None, PX),
        P(None, PX),
        P(None, PX),
        P(None, LT),
        P(None, LT),
        P(),
    )
    return jax.shard_map(
        shards,
        mesh=torus,
        in_specs=placed,
        out_specs=(P(None, PX), P(None, LT), P(None, LT), P()),
        check_vma=False,
    )
```

```python
import functools
import math

import jax
import jax.numpy as jnp
from jax import lax
from jax.experimental import pallas as pl
from jax.experimental.pallas import tpu as pltpu
from jax.sharding import Mesh
from jax.sharding import PartitionSpec as P

PX = ("px_0", "px_1", "px_2")
LT = ("lt_0", "lt_1")

SOFT = 0.01
EPS = 1e-06
STRIDE = 0.2
LANES = 128
SUBS = 8
ROWS = 12
BLOCK = 1024
CHUNKS = BLOCK // LANES
RAW = 24
GROUP = 1

(TX, TY, TZ, BX, BY, BZ, NX, NY, NZ, PT, PB, PN, VT, VB, VN, AX2, AY2, IX2, IY2, KG, F0, F1, K5,
 KD0, KD1, KD2, KS0, KS1, KS2) = range(29)
TABLE = 29
(SD0, SD1, SD2, SS0, SS1, SS2, SF, SH, V11, V22, V12, V13, V23, U11, U22, U12, U13, U23, WT, WB) = range(20)
SUMS = 20


def inner_three(first, second):
    return first[0] * second[0] + first[1] * second[1] + first[2] * second[2]


def pixel_frame(row, ids, camera_ref):
    azimuth = 2.0 * math.pi * row(17)
    ca, sa = jnp.cos(row(16)), jnp.sin(row(16))
    cz, sz = jnp.cos(azimuth), jnp.sin(azimuth)
    base_n = [sa * cz, sa * sz, ca]
    base_t = [ca * cz, ca * sz, -sa]
    base_b = [-sz, cz]
    u, v, spin = row(8), row(9), row(10)
    cs, sn = jnp.cos(spin), jnp.sin(spin)
    kappa = lax.rsqrt(1.0 + u * u + v * v)
    along = kappa * (u * cs + v * sn)
    inv = lax.rsqrt(1.0 - along * along)
    n_loc = [kappa, kappa * u, kappa * v]
    t_loc = [-along * n_loc[0] * inv, (cs - along * n_loc[1]) * inv, (sn - along * n_loc[2]) * inv]
    kb = kappa * inv
    b_loc = [kb * (u * sn - v * cs), -kb * sn, kb * cs]

    def world(loc):
        return [
            loc[0] * base_n[0] + loc[1] * base_t[0] + loc[2] * base_b[0],
            loc[0] * base_n[1] + loc[1] * base_t[1] + loc[2] * base_b[1],
            loc[0] * base_n[2] + loc[1] * base_t[2],
        ]

    tangent, bitangent, normal = world(t_loc), world(b_loc), world(n_loc)
    point = [row(12), row(13), row(14)]
    camera = [jnp.full_like(u, camera_ref[c, 0]) for c in range(3)]
    for view in range(1, camera_ref.shape[1]):
        chosen = ids == view
        camera = [jnp.where(chosen, camera_ref[c, view], camera[c]) for c in range(3)]
    toward = [camera[c] - point[c] for c in range(3)]
    scale = lax.rsqrt(inner_three(toward, toward))
    view_dir = [toward[c] * scale for c in range(3)]
    vt, vb, vn = (inner_three(view_dir, f) for f in (tangent, bitangent, normal))
    ax, ay = jnp.exp(row(6)), jnp.exp(row(7))
    ax2, ay2 = ax * ax, ay * ay
    ix2, iy2 = 1.0 / ax2, 1.0 / ay2
    vroot = lax.rsqrt(vn * vn + SOFT)
    cv = 0.5 * (vn + (vn * vn + SOFT) * vroot)
    wv2 = cv * cv + ax2 * vt * vt + ay2 * vb * vb
    rwv = lax.rsqrt(wv2)
    rcv = 1.0 / (cv + wv2 * rwv)
    return dict(
        tangent=tangent, bitangent=bitangent, normal=normal, point=point,
        vt=vt, vb=vb, vn=vn, ax=ax, ay=ay, ax2=ax2, ay2=ay2, ix2=ix2, iy2=iy2,
        vroot=vroot, cv=cv, rwv=rwv, rcv=rcv, kappa=kappa, inv=inv, along=along,
        t_loc=t_loc, b_loc=b_loc,
    )


def pair_terms(px, light, visible, measured):
    lx, ly, lz, pw = light[0], light[1], light[2], light[3:6]
    ot = lx * px(TX) + ly * px(TY) + lz * px(TZ) - px(PT)
    ob = lx * px(BX) + ly * px(BY) + lz * px(BZ) - px(PB)
    on = lx * px(NX) + ly * px(NY) + lz * px(NZ) - px(PN)
    r = lax.rsqrt(ot * ot + ob * ob + on * on)
    id2 = r * r
    lt, lb, ln = ot * r, ob * r, on * r
    m = (lt * px(VT) + lb * px(VB)) + (ln * px(VN) + 1.0)
    a1, a2, a3 = lt + px(VT), lb + px(VB), ln + px(VN)
    b1, b2 = a1 * px(IX2), a2 * px(IY2)
    rq = lax.rsqrt(b1 * a1 + b2 * a2 + a3 * a3)
    rq = rq * rq
    rm = lax.rsqrt(m)
    om = 1.0 - (m * rm) * math.sqrt(0.5)
    om2 = om * om
    om4 = om2 * om2
    s5 = om4 * om
    fresnel = px(F0) + px(F1) * s5
    lsq = ln * ln + SOFT
    rs = lax.rsqrt(lsq)
    cn = 0.5 * (ln + lsq * rs)
    xt, xb = lt * px(AX2), lb * px(AY2)
    wsq = cn * cn + (xt * lt + xb * lb)
    rw = lax.rsqrt(wsq)
    rc = lax.rsqrt(cn + wsq * rw)
    rc = rc * rc
    cni = cn * id2
    mq = m * rq
    bi = (mq * mq) * (rc * cni) * px(KG)
    gi = bi * fresnel
    squares = None
    power_terms = []
    ys = []
    for c in range(3):
        refl = px(KD0 + c) * cni + px(KS0 + c) * gi
        res = visible * (pw[c] * refl - measured[c])
        squares = res * res if c == 0 else squares + res * res
        power_terms.append(res * refl)
        ys.append(res * pw[c])
    dcn = ys[0] * px(KD0) + ys[1] * px(KD1) + ys[2] * px(KD2)
    dgl = ys[0] * px(KS0) + ys[1] * px(KS1) + ys[2] * px(KS2)
    h = gi * dgl
    s = cni * dcn + h
    x = dgl * bi
    mm = rm * (2.0 * (h * rm) - (x * om4) * px(K5))
    hw = h * rw
    uu = hw * rc
    ww = rs * (s - hw * cn)
    v4 = (4.0 * h) * rq
    v1, v2, v3 = v4 * a1, v4 * a2, v4 * a3
    u1, u2 = uu * lt, uu * lb
    sums = [None] * SUMS
    for c in range(3):
        sums[SD0 + c] = ys[c] * cni
        sums[SS0 + c] = ys[c] * gi
    sums[SF] = x - x * s5
    sums[SH] = h
    sums[V11], sums[V22], sums[V12] = v1 * a1, v2 * a2, v1 * a2
    sums[V13], sums[V23] = v1 * a3, v2 * a3
    sums[U11], sums[U22], sums[U12] = u1 * lt, u2 * lb, u1 * lb
    sums[U13], sums[U23] = u1 * ln, u2 * ln
    sums[WT], sums[WB] = ww * lt, ww * lb
    gt = mm * px(VT) - uu * xt - v4 * b1
    gb = mm * px(VB) - uu * xb - v4 * b2
    gn = mm * px(VN) + ww - v3
    radial = lt * gt + lb * gb + ln * gn + 2.0 * s
    gt, gb, gn = (gt - lt * radial) * r, (gb - lb * radial) * r, (gn - ln * radial) * r
    light_terms = power_terms + [
        gt * px(TX + c) + gb * px(BX + c) + gn * px(NX + c) for c in range(3)
    ]
    return sums, light_terms, squares


def whole(x):
    return jnp.sum(jnp.sum(x, axis=0, keepdims=True), axis=1, keepdims=True)


def fold(x):
    total = x[:SUBS]
    for g in range(1, x.shape[0] // SUBS):
        total = total + x[g * SUBS : (g + 1) * SUBS]
    return total


def gradient_kernel(
    camera_ref, observed_ref, shadow_ref, ids_ref, points_ref, frames_ref, params_ref, power_ref, pos_ref,
    grads_ref, light_ref,
    raw, table, sums_ref, light_wide, light_sum, square_sum,
):
    step = pl.program_id(0)
    lights = shadow_ref.shape[0]
    groups = lights // SUBS
    lane = lax.broadcasted_iota(jnp.int32, (SUBS, lights), 1)
    sub = lax.broadcasted_iota(jnp.int32, (SUBS, lights), 0)

    @pl.when(step == 0)
    def _():
        light_sum[...] = jnp.zeros_like(light_sum)
        square_sum[...] = jnp.zeros_like(square_sum)
        for q in range(6):
            source = pos_ref if q < 3 else power_ref
            values = source[q % 3 : q % 3 + 1, :]
            for g in range(groups):
                picked = jnp.where(lane == sub + g * SUBS, values, 0.0)
                column = jnp.sum(picked, axis=1, keepdims=True)
                light_wide[q, g * SUBS : (g + 1) * SUBS, :] = jnp.broadcast_to(column, (SUBS, LANES))

    for k in range(CHUNKS):
        cut = slice(k * LANES, (k + 1) * LANES)
        raw[k * RAW : k * RAW + 12, :] = params_ref[:, cut]
        raw[k * RAW + 12 : k * RAW + 15, :] = points_ref[:, cut]
        raw[k * RAW + 16 : k * RAW + 18, :] = frames_ref[:, cut]

    def row(q):
        return raw[pl.ds(q, CHUNKS, stride=RAW), :]

    f = pixel_frame(row, ids_ref[...], camera_ref)
    entries = {
        AX2: f["ax2"], AY2: f["ay2"], IX2: f["ix2"], IY2: f["iy2"],
        VT: f["vt"], VB: f["vb"], VN: f["vn"],
        PT: inner_three(f["point"], f["tangent"]),
        PB: inner_three(f["point"], f["bitangent"]),
        PN: inner_three(f["point"], f["normal"]),
        KG: 4.0 * f["rcv"] / (math.pi * f["ax"] * f["ay"]),
        F0: row(11), F1: 1.0 - row(11), K5: (1.0 - row(11)) * (5.0 * math.sqrt(2.0) / 4.0),
    }
    for c in range(3):
        entries[TX + c], entries[BX + c], entries[NX + c] = f["tangent"][c], f["bitangent"][c], f["normal"][c]
        entries[KD0 + c] = row(c) * (1.0 / math.pi)
        entries[KS0 + c] = row(3 + c)
    for q, value in entries.items():
        table[q] = value

    rows = SUBS * GROUP

    def chunk(k, _):
        cut = pl.ds(pl.multiple_of(k * LANES, LANES), LANES)

        def px(q):
            return jnp.broadcast_to(table[q, pl.ds(k, 1), :], (rows, LANES))

        total = None
        squares = None
        for g in range(lights // rows):
            at = slice(g * rows, (g + 1) * rows)
            visible = shadow_ref[at, cut].astype(jnp.float32)
            measured = [observed_ref[c, at, cut].astype(jnp.float32) for c in range(3)]
            sums, light_terms, square = pair_terms(
                px, [light_wide[q, at, :] for q in range(6)], visible, measured
            )
            sums = [fold(x) for x in sums]
            square = fold(square)
            total = sums if total is None else [a + b for a, b in zip(total, sums)]
            squares = square if squares is None else squares + square
            for q in range(6):
                light_sum[q, at, :] += light_terms[q]
        square_sum[...] += squares
        for q in range(SUMS):
            sums_ref[pl.ds(pl.multiple_of(q * BLOCK // LANES * SUBS + k * SUBS, SUBS), SUBS), :] = total[q]
        return 0

    lax.fori_loop(0, CHUNKS, chunk, 0)

    def summed(q):
        start = q * CHUNKS * SUBS
        parts = [sums_ref[pl.ds(start + i, CHUNKS, stride=SUBS), :] for i in range(SUBS)]
        while len(parts) > 1:
            parts = [a + b for a, b in zip(parts[::2], parts[1::2])]
        return parts[0]

    z = [summed(q) for q in range(SUMS)]
    vt, vb, vn = f["vt"], f["vb"], f["vn"]
    uv = z[SH] * f["rwv"] * f["rcv"]
    wv = -z[SH] * f["rwv"] * f["cv"] * f["vroot"]
    u11, u22, u12 = z[U11] + uv * vt * vt, z[U22] + uv * vb * vb, z[U12] + uv * vt * vb
    u13, u23 = z[U13] + uv * vt * vn, z[U23] + uv * vb * vn
    wt, wb = z[WT] + wv * vt, z[WB] + wv * vb
    ax2, ay2, ix2, iy2 = f["ax2"], f["ay2"], f["ix2"], f["iy2"]
    tau_x = (1.0 - iy2) * z[V23] - ay2 * u23 - wb
    tau_y = (ix2 - 1.0) * z[V13] + ax2 * u13 + wt
    tau_z = (iy2 - ix2) * z[V12] + (ay2 - ax2) * u12
    turned = tau_x + f["inv"] * f["along"] * tau_z
    grads = [z[SD0 + c] * (1.0 / math.pi) for c in range(3)] + [z[SS0 + c] for c in range(3)]
    grads.append(ix2 * z[V11] - ax2 * u11 - z[SH])
    grads.append(iy2 * z[V22] - ay2 * u22 - z[SH])
    grads.append(f["kappa"] * (f["t_loc"][1] * tau_y - f["b_loc"][1] * turned))
    grads.append(f["kappa"] * (f["t_loc"][2] * tau_y - f["b_loc"][2] * turned))
    grads.append(tau_z * f["inv"] * f["inv"] * f["kappa"])
    grads.append(z[SF])
    for q in range(ROWS):
        grads_ref[pl.ds(q, CHUNKS, stride=ROWS), :] = grads[q]

    @pl.when(step == pl.num_programs(0) - 1)
    def _():
        wide = lax.broadcasted_iota(jnp.int32, (SUBS, LANES), 1)
        deep = lax.broadcasted_iota(jnp.int32, (SUBS, LANES), 0)
        lines = []
        for kind in range(2):
            spread = jnp.zeros((SUBS, LANES), jnp.float32)
            for q in range(3):
                for g in range(groups):
                    line = jnp.sum(light_sum[3 * kind + q, g * SUBS : (g + 1) * SUBS, :], axis=1, keepdims=True)
                    spread = jnp.where(wide == deep + (g * SUBS + q * lights), line, spread)
            lines.append(jnp.sum(spread, axis=0, keepdims=True))
        first = lax.broadcasted_iota(jnp.int32, (1, LANES), 1)
        light_ref[0:1, :] = jnp.where(first == 3 * lights, whole(square_sum[...]), lines[0])
        light_ref[1:2, :] = lines[1]


def local_gradients(observed, shadow, view_ids, points, frames, params, power, pos, cameras):
    lights, pixels = shadow.shape
    steps = pixels // BLOCK
    return pl.pallas_call(
        gradient_kernel,
        grid=(steps,),
        in_specs=[
            pl.BlockSpec(memory_space=pltpu.SMEM),
            pl.BlockSpec((3, lights, BLOCK), lambda i: (0, 0, i)),
            pl.BlockSpec((lights, BLOCK), lambda i: (0, i)),
            pl.BlockSpec((CHUNKS, LANES), lambda i: (i, 0)),
            pl.BlockSpec((3, BLOCK), lambda i: (0, i)),
            pl.BlockSpec((2, BLOCK), lambda i: (0, i)),
            pl.BlockSpec((ROWS, BLOCK), lambda i: (0, i)),
            pl.BlockSpec((3, lights), lambda i: (0, 0)),
            pl.BlockSpec((3, lights), lambda i: (0, 0)),
        ],
        out_specs=[
            pl.BlockSpec((CHUNKS * ROWS, LANES), lambda i: (i, 0)),
            pl.BlockSpec((2, LANES), lambda i: (0, 0)),
        ],
        out_shape=[
            jax.ShapeDtypeStruct((pixels // LANES * ROWS, LANES), jnp.float32),
            jax.ShapeDtypeStruct((2, LANES), jnp.float32),
        ],
        scratch_shapes=[
            pltpu.VMEM((CHUNKS * RAW, LANES), jnp.float32),
            pltpu.VMEM((TABLE, SUBS, LANES), jnp.float32),
            pltpu.VMEM((SUMS * CHUNKS * SUBS, LANES), jnp.float32),
            pltpu.VMEM((6, lights, LANES), jnp.float32),
            pltpu.VMEM((6, lights, LANES), jnp.float32),
            pltpu.VMEM((SUBS, LANES), jnp.float32),
        ],
        compiler_params=pltpu.CompilerParams(vmem_limit_bytes=16 << 20),
        name="pair_gradients",
    )(
        *(
            pltpu.with_memory_space_constraint(x, pltpu.HBM)
            for x in (
                cameras, observed, shadow, view_ids.reshape(pixels // LANES, LANES),
                points, frames, params, power, pos,
            )
        )
    )


def share_kernel(mark, arrived_ref, light_ref, share_ref, spread_ref):
    parts, rows = arrived_ref.shape[:2]
    squares = jnp.zeros((SUBS, LANES), jnp.float32)
    for at in range(0, rows, SUBS):
        pieces = [arrived_ref[i, at : at + SUBS, :] for i in range(parts)]
        while len(pieces) > 1:
            pieces = [a + b for a, b in zip(pieces[::2], pieces[1::2])]
        share_ref[at : at + SUBS, :] = pieces[0]
        squares = squares + pieces[0] * pieces[0]
    lane = lax.broadcasted_iota(jnp.int32, (2, LANES), 1)
    deep = lax.broadcasted_iota(jnp.int32, (2, LANES), 0)
    tile = jnp.where((lane == mark) & (deep == 1), whole(squares), light_ref[...])
    for i in range(spread_ref.shape[0]):
        spread_ref[i] = tile


def join_kernel(mark, share_ref, light_parts_ref, out_ref, light_ref):
    tile = light_parts_ref[0]
    for i in range(1, light_parts_ref.shape[0]):
        tile = tile + light_parts_ref[i]
    light_ref[...] = tile
    lane = lax.broadcasted_iota(jnp.int32, (2, LANES), 1)
    light_sq = whole(jnp.where(lane < mark, tile * tile, 0.0))
    deep = lax.broadcasted_iota(jnp.int32, (SUBS, LANES), 0)
    wide = lax.broadcasted_iota(jnp.int32, (SUBS, LANES), 1)
    tail = jnp.where(wide == 0, light_sq, 0.0)
    tail = jnp.where(wide == 1, tile[0:1, mark : mark + 1], tail)
    tail = jnp.where(wide == 2, tile[1:2, mark : mark + 1], tail)
    tail = jnp.where(deep == 0, tail, 0.0)
    rows = share_ref.shape[0]
    for at in range(0, rows, SUBS):
        value = share_ref[at : at + SUBS, :]
        for i in range(out_ref.shape[0]):
            out_ref[i, at : at + SUBS, :] = value
    for i in range(out_ref.shape[0]):
        out_ref[i, rows : rows + SUBS, :] = tail


def step_kernel(
    pixel_total, light_total, gathered_ref, light_ref, params_ref, power_ref, pos_ref,
    new_params_ref, new_power_ref, new_pos_ref, loss_ref,
):
    parts, rows = gathered_ref.shape[0], gathered_ref.shape[1] - SUBS
    tail = gathered_ref[0, rows : rows + SUBS, :]
    for i in range(1, parts):
        tail = tail + gathered_ref[i, rows : rows + SUBS, :]
    light_scale = STRIDE * lax.rsqrt(tail[0:1, 0:1] / (6 * light_total) + EPS)
    pixel_scale = STRIDE * lax.rsqrt(tail[0:1, 2:3] / (ROWS * pixel_total) + EPS)
    loss_ref[...] = tail[0:1, 1:2] / (3.0 * light_total * pixel_total)
    lights = power_ref.shape[1]
    for c in range(3):
        cut = slice(c * lights, (c + 1) * lights)
        new_power_ref[c : c + 1, :] = power_ref[c : c + 1, :] - light_ref[0:1, cut] * light_scale
        new_pos_ref[c : c + 1, :] = pos_ref[c : c + 1, :] - light_ref[1:2, cut] * light_scale
    chunks = rows // ROWS
    for i in range(parts):
        for k in range(chunks):
            cut = slice((i * chunks + k) * LANES, (i * chunks + k + 1) * LANES)
            grad = gathered_ref[i, k * ROWS : (k + 1) * ROWS, :]
            new_params_ref[:, cut] = params_ref[:, cut] - grad * pixel_scale


def broadcast_exchange(x, axes):
    return lax.all_to_all(x, axes, split_axis=0, concat_axis=0, tiled=True)


def shards(observed, shadow, view_ids, points, frames, params, power, pos, cameras):
    lights, pixels = shadow.shape
    px_size, lt_size = lax.axis_size(PX), lax.axis_size(LT)
    grads, light_tile = local_gradients(
        observed, shadow, view_ids, points, frames, params, power, pos, cameras
    )
    share_rows = grads.shape[0] // lt_size
    mark = 3 * lights
    small = pltpu.CompilerParams(vmem_limit_bytes=8 << 20)
    arrived = broadcast_exchange(grads.reshape(lt_size, share_rows, LANES), LT)
    share, spread = pl.pallas_call(
        functools.partial(share_kernel, mark),
        out_shape=(
            jax.ShapeDtypeStruct((share_rows, LANES), jnp.float32),
            jax.ShapeDtypeStruct((px_size, 2, LANES), jnp.float32),
        ),
        compiler_params=small,
        name="share_sum",
    )(arrived, light_tile)
    light_parts = broadcast_exchange(spread, PX)
    joined, own_lights = pl.pallas_call(
        functools.partial(join_kernel, mark),
        out_shape=(
            jax.ShapeDtypeStruct((lt_size, share_rows + SUBS, LANES), jnp.float32),
            jax.ShapeDtypeStruct((2, LANES), jnp.float32),
        ),
        compiler_params=small,
        name="join",
    )(share, light_parts)
    gathered = broadcast_exchange(joined, LT)
    new_params, new_power, new_pos, loss = pl.pallas_call(
        functools.partial(step_kernel, pixels * px_size, lights * lt_size),
        out_shape=(
            jax.ShapeDtypeStruct(params.shape, jnp.float32),
            jax.ShapeDtypeStruct(power.shape, jnp.float32),
            jax.ShapeDtypeStruct(pos.shape, jnp.float32),
            jax.ShapeDtypeStruct((1, 1), jnp.float32),
        ),
        compiler_params=small,
        name="step",
    )(gathered, own_lights, params, power, pos)
    return new_params, new_power, new_pos, loss.reshape(())


def solution(mesh):
    torus = Mesh(mesh.devices.reshape(4, 4, 2, 8, 2), PX + LT)
    placed = (
        P(None, LT, PX),
        P(LT, PX),
        P(PX),
        P(None, PX),
        P(None, PX),
        P(None, PX),
        P(None, LT),
        P(None, LT),
        P(),
    )
    return jax.shard_map(
        shards,
        mesh=torus,
        in_specs=placed,
        out_specs=(P(None, PX), P(None, LT), P(None, LT), P()),
        check_vma=False,
    )
```

```python
import functools
import math

import jax
import jax.numpy as jnp
from jax import lax
from jax.experimental import pallas as pl
from jax.experimental.pallas import tpu as pltpu
from jax.sharding import Mesh
from jax.sharding import PartitionSpec as P

PX = ("px_0", "px_1", "px_2")
LT = ("lt_0", "lt_1")

SOFT = 0.01
EPS = 1e-06
STRIDE = 0.2
LANES = 128
SUBS = 8
ROWS = 12
BLOCK = 2048
CHUNKS = BLOCK // LANES
RAW = 25
DEPTH = 32
PITCH = 33
SUM_PITCH = 9
UNROLL = 8

(VT, VB, VN, AX2, AY2, IX2, IY2, F0, F1, K5, KD0, KD1, KD2, KS0, KS1, KS2) = range(16)
TABLE = 16
(SD0, SD1, SD2, SS0, SS1, SS2, SF, SH, V11, V22, V12, V13, V23, U11, U22, U12, TX, TY) = range(18)
SUMS = 18
LEFT = (0, 0, 1, 1, 0, 2)
RIGHT = (0, 1, 0, 1, 2, 0)
COMPS = 5
BLOCKS = 5
SQUARED = 3


def inner_three(first, second):
    return first[0] * second[0] + first[1] * second[1] + first[2] * second[2]


def pixel_frame(row, ids, camera_ref):
    azimuth = 2.0 * math.pi * row(17)
    ca, sa = jnp.cos(row(16)), jnp.sin(row(16))
    cz, sz = jnp.cos(azimuth), jnp.sin(azimuth)
    base_n = [sa * cz, sa * sz, ca]
    base_t = [ca * cz, ca * sz, -sa]
    base_b = [-sz, cz]
    u, v, spin = row(8), row(9), row(10)
    cs, sn = jnp.cos(spin), jnp.sin(spin)
    kappa = lax.rsqrt(1.0 + u * u + v * v)
    along = kappa * (u * cs + v * sn)
    inv = lax.rsqrt(1.0 - along * along)
    n_loc = [kappa, kappa * u, kappa * v]
    t_loc = [-along * n_loc[0] * inv, (cs - along * n_loc[1]) * inv, (sn - along * n_loc[2]) * inv]
    kb = kappa * inv
    b_loc = [kb * (u * sn - v * cs), -kb * sn, kb * cs]

    def world(loc):
        return [
            loc[0] * base_n[0] + loc[1] * base_t[0] + loc[2] * base_b[0],
            loc[0] * base_n[1] + loc[1] * base_t[1] + loc[2] * base_b[1],
            loc[0] * base_n[2] + loc[1] * base_t[2],
        ]

    tangent, bitangent, normal = world(t_loc), world(b_loc), world(n_loc)
    point = [row(12), row(13), row(14)]
    camera = [jnp.full_like(u, camera_ref[c, 0]) for c in range(3)]
    for view in range(1, camera_ref.shape[1]):
        chosen = ids == view
        camera = [jnp.where(chosen, camera_ref[c, view], camera[c]) for c in range(3)]
    toward = [camera[c] - point[c] for c in range(3)]
    scale = lax.rsqrt(inner_three(toward, toward))
    view_dir = [toward[c] * scale for c in range(3)]
    vt, vb, vn = (inner_three(view_dir, f) for f in (tangent, bitangent, normal))
    ax, ay = jnp.exp(row(6)), jnp.exp(row(7))
    ax2, ay2 = ax * ax, ay * ay
    ix2, iy2 = 1.0 / ax2, 1.0 / ay2
    vroot = lax.rsqrt(vn * vn + SOFT)
    cv = 0.5 * (vn + (vn * vn + SOFT) * vroot)
    wv2 = cv * cv + ax2 * vt * vt + ay2 * vb * vb
    rwv = lax.rsqrt(wv2)
    rcv = 1.0 / (cv + wv2 * rwv)
    return dict(
        tangent=tangent, bitangent=bitangent, normal=normal, point=point, view_dir=view_dir,
        vt=vt, vb=vb, vn=vn, ax=ax, ay=ay, ax2=ax2, ay2=ay2, ix2=ix2, iy2=iy2,
        inv_f1=1.0 / (1.0 - row(11)), lobe=16.0 * rcv / (math.pi * ax * ay), vroot=vroot, cv=cv, rwv=rwv, rcv=rcv, kappa=kappa, inv=inv, along=along,
        t_loc=t_loc, b_loc=b_loc,
    )


def pair_terms(px, offsets, pw, visible, measured):
    ot, ob, on, d2, ov = offsets
    r = lax.rsqrt(d2)
    id2 = r * r
    lt, lb, ln, lv = ot * r, ob * r, on * r, ov * r
    m = 0.5 * lv + 0.5
    a1, a2, a3 = lt + px(VT), lb + px(VB), ln + px(VN)
    b1, b2 = a1 * px(IX2), a2 * px(IY2)
    rq = lax.rsqrt(b1 * a1 + b2 * a2 + a3 * a3)
    rq = rq * rq
    rm = lax.rsqrt(m)
    om = 1.0 - m * rm
    om2 = om * om
    om4 = om2 * om2
    s5 = om4 * om
    fresnel = px(F0) + px(F1) * s5
    rf = lax.rsqrt(fresnel)
    lsq = ln * ln + SOFT
    rs = lax.rsqrt(lsq)
    cn = ln + lsq * rs
    xt, xb = lt * px(AX2), lb * px(AY2)
    wsq = cn * cn + (xt * lt + xb * lb)
    rw = lax.rsqrt(wsq)
    rc = lax.rsqrt(cn + wsq * rw)
    rc = rc * rc
    cni = cn * (id2 * visible)
    mq = m * rq
    gi = (mq * mq) * (rc * cni) * fresnel
    sums = [None] * SUMS
    power_terms = []
    squares = h = s = None
    for c in range(3):
        diffuse, glossy = pw[c] * cni, pw[c] * gi
        res = px(KD0 + c) * diffuse + px(KS0 + c) * glossy - measured[c]
        squares = res * res if c == 0 else squares + res * res
        sums[SD0 + c], sums[SS0 + c] = res * diffuse, res * glossy
        part = px(KS0 + c) * sums[SS0 + c]
        term = px(KD0 + c) * sums[SD0 + c] + part
        power_terms.append(term)
        h = part if c == 0 else h + part
        s = term if c == 0 else s + term
    squares = squares * visible
    x = (h * rf) * rf
    nm = rm * ((x * om4) * px(K5) - h * rm)
    hw = h * rw
    uu = hw * rc
    ww = rs * (s - hw * cn)
    v4 = (4.0 * h) * rq
    p1, p2 = uu * xt, uu * xb
    q1, q2, q3 = v4 * b1, v4 * b2, v4 * a3
    sums[SF] = x
    sums[SH] = h
    sums[V11], sums[V22], sums[V12] = q1 * a1, q2 * a2, q1 * a2
    sums[V13], sums[V23] = q1 * a3, q2 * a3
    sums[U11], sums[U22], sums[U12] = p1 * lt, p2 * lb, p1 * lb
    sums[TX], sums[TY] = p2 * ln + ww * lb, p1 * ln + ww * lt
    g1, g2, g3 = p1 + q1, p2 + q2, q3 - ww
    inner = (lt * g1 + lb * g2) + (ln * g3 + lv * nm)
    cots = [r * g1, r * g2, r * g3, id2 * (s - 0.5 * inner), r * nm]
    return sums, power_terms, squares, cots


def whole(x):
    return jnp.sum(jnp.sum(x, axis=0, keepdims=True), axis=1, keepdims=True)


def rounded(x):
    return x.astype(jnp.bfloat16).astype(jnp.float32)


def split_three(x):
    first = rounded(x)
    second = rounded(x - first)
    return [first, second, x - first - second]


def gradient_kernel(
    camera_ref, observed_hbm, shadow_hbm, ids_hbm, points_hbm, frames_hbm, params_hbm, power_ref, pos_ref,
    grads_ref, light_ref,
    observed_ref, shadow_ref, ids_ref, points_ref, frames_ref, params_ref,
    raw, table, sums_ref, left, right, offsets, spread_ref, frame_ref, power_wide, power_sum, pos_sum,
    square_sum, sems,
):
    lights, pixels = shadow_hbm.shape
    groups = lights // SUBS
    steps = pixels // BLOCK

    def copies(first, count):
        cut = slice(first * BLOCK, (first + count) * BLOCK)
        tile = slice(first * CHUNKS, (first + count) * CHUNKS)
        slot = min(first, 1)
        pairs = [
            (params_hbm.at[:, cut], params_ref.at[:, cut]),
            (points_hbm.at[:, cut], points_ref.at[:, cut]),
            (frames_hbm.at[:, cut], frames_ref.at[:, cut]),
            (ids_hbm.at[tile, :], ids_ref.at[tile, :]),
            (shadow_hbm.at[:, cut], shadow_ref.at[:, cut]),
            (observed_hbm.at[:, :, cut], observed_ref.at[:, :, cut]),
        ]
        return [pltpu.make_async_copy(a, b, sems.at[slot, i]) for i, (a, b) in enumerate(pairs)]

    stages = [copies(0, 1), copies(1, steps - 1)]
    for copy in stages[0]:
        copy.start()

    power_sum[...] = jnp.zeros_like(power_sum)
    pos_sum[...] = jnp.zeros_like(pos_sum)
    square_sum[...] = jnp.zeros_like(square_sum)
    spread_ref[...] = jnp.zeros_like(spread_ref)
    frame_ref[...] = jnp.zeros_like(frame_ref)
    right[...] = jnp.zeros_like(right)

    def piece(b):
        return slice(b * LANES, (b + 1) * LANES)

    def right_rows(b, q):
        return pl.ds(b * CHUNKS * PITCH + q, CHUNKS, stride=PITCH)

    for i, part in enumerate(RIGHT):
        if part == 0:
            right[right_rows(SQUARED, i * COMPS + 4), :] = jnp.ones((CHUNKS, LANES), jnp.float32)
    lane = lax.broadcasted_iota(jnp.int32, (SUBS, lights), 1)
    sub = lax.broadcasted_iota(jnp.int32, (SUBS, lights), 0)

    def column(source, c, g):
        picked = jnp.where(lane == sub + g * SUBS, source[c : c + 1, :], 0.0)
        return jnp.sum(picked, axis=1, keepdims=True)

    deep_lane = lax.broadcasted_iota(jnp.int32, (SUBS, DEPTH), 1)
    one = jnp.ones((SUBS, DEPTH), jnp.float32)
    zero = jnp.zeros((SUBS, DEPTH), jnp.float32)
    tiles = []
    for g in range(groups):
        at = slice(g * SUBS, (g + 1) * SUBS)
        for c in range(3):
            power_wide[c, at, :] = jnp.broadcast_to(column(power_ref, c, g), (SUBS, LANES))
        pos = [jnp.broadcast_to(column(pos_ref, c, g), (SUBS, DEPTH)) for c in range(3)]
        splits = [split_three(x) for x in pos] + [[one, zero, zero], split_three(inner_three(pos, pos))]
        tile = zero
        for i, part in enumerate(LEFT):
            for c in range(COMPS):
                tile = jnp.where(deep_lane == i * COMPS + c, splits[c][part], tile)
        tiles.append(tile)
    left[...] = jnp.concatenate(tiles, axis=0).astype(jnp.bfloat16)

    def frame(k, depth):
        return jnp.concatenate(
            [right[pl.ds((b * CHUNKS + k) * PITCH, depth), :] for b in range(BLOCKS)], axis=1
        ).astype(jnp.bfloat16)

    def product(k):
        return jnp.dot(left[...], frame(k, DEPTH), preferred_element_type=jnp.float32)

    def gather_positions():
        pos_sum[...] += lax.dot_general(
            spread_ref[...].astype(jnp.bfloat16), frame_ref[...], (((1,), (1,)), ((), ())),
            preferred_element_type=jnp.float32,
        )

    for copy in stages[0][:4]:
        copy.wait()
    for stage in stages[1:]:
        for copy in stage:
            copy.start()

    def arrive(step, first, some):
        for i, stage in enumerate(stages[first:], first):

            @pl.when(step == i)
            def _(stage=stage):
                for copy in stage[some]:
                    copy.wait()

    def block(step, _):
        arrive(step, 1, slice(0, 4))

        base = pl.multiple_of(step * BLOCK, BLOCK)
        for k in range(CHUNKS):
            cut = pl.ds(pl.multiple_of(base + k * LANES, LANES), LANES)
            raw[k * RAW : k * RAW + 12, :] = params_ref[:, cut]
            raw[k * RAW + 12 : k * RAW + 15, :] = points_ref[:, cut]
            raw[k * RAW + 16 : k * RAW + 18, :] = frames_ref[:, cut]

        def row(q):
            return raw[pl.ds(q, CHUNKS, stride=RAW), :]

        ids = ids_ref[pl.ds(pl.multiple_of(step * CHUNKS, CHUNKS), CHUNKS), :]
        f = pixel_frame(row, ids, camera_ref)
        point = f["point"]
        columns = [
            [*vec, -inner_three(point, vec)] for vec in (f["tangent"], f["bitangent"], f["normal"])
        ]
        columns.append([-2.0 * point[c] for c in range(3)] + [inner_three(point, point)])
        columns.append([*f["view_dir"], -inner_three(point, f["view_dir"])])
        for b, column_of in enumerate(columns):
            for c, value in enumerate(column_of):
                rest = value - rounded(value)
                parts = [value, rest, rest - rounded(rest)]
                for i, part in enumerate(RIGHT):
                    right[right_rows(b, i * COMPS + c), :] = parts[part]
        entries = {
            AX2: 4.0 * f["ax2"], AY2: 4.0 * f["ay2"], IX2: f["ix2"], IY2: f["iy2"],
            VT: f["vt"], VB: f["vb"], VN: f["vn"],
            F0: row(11), F1: 1.0 - row(11), K5: 1.25 - 1.25 * row(11),
        }
        for c in range(3):
            entries[KD0 + c] = row(c) * (0.5 / math.pi)
            entries[KS0 + c] = row(3 + c) * f["lobe"]
        for q, value in entries.items():
            table[q] = value
        offsets[...] = product(0)

        def chunk(k, _):
            cut = pl.ds(pl.multiple_of(base + k * LANES, LANES), LANES)

            def px(q):
                return jnp.broadcast_to(table[q, pl.ds(k, 1), :], (SUBS, LANES))

            following = product(jnp.minimum(k + 1, CHUNKS - 1))
            gather_positions()
            total = squares = None
            for g in range(groups):
                at = slice(g * SUBS, (g + 1) * SUBS)
                visible = shadow_ref[at, cut].astype(jnp.float32)
                measured = [observed_ref[c, at, cut].astype(jnp.float32) for c in range(3)]
                sums, power_terms, square, cot = pair_terms(
                    px, [offsets[at, piece(b)] for b in range(BLOCKS)],
                    [power_wide[c, at, :] for c in range(3)], visible, measured,
                )
                total = sums if total is None else [a + b for a, b in zip(total, sums)]
                squares = square if squares is None else squares + square
                for b in range(BLOCKS):
                    spread_ref[at, piece(b)] = cot[b]
                for c in range(3):
                    power_sum[c, at, :] += power_terms[c]
            square_sum[...] += squares
            for q in range(SUMS):
                sums_ref[pl.ds((q * CHUNKS + k) * SUM_PITCH, SUBS), :] = total[q]
            frame_ref[...] = frame(k, 16)
            offsets[...] = following
            return 0

        arrive(step, 0, slice(4, 6))
        lax.fori_loop(0, CHUNKS, chunk, 0, unroll=UNROLL)
        grads = block_gradients(f, sums_ref)
        for q in range(ROWS):
            grads_ref[pl.ds(step * (CHUNKS * ROWS) + q, CHUNKS, stride=ROWS), :] = grads[q]
        return 0

    lax.fori_loop(0, steps, block, 0)

    gather_positions()
    wide = lax.broadcasted_iota(jnp.int32, (SUBS, LANES), 1)
    deep = lax.broadcasted_iota(jnp.int32, (SUBS, LANES), 0)
    lines = []
    for kind in range(2):
        spread = jnp.zeros((SUBS, LANES), jnp.float32)
        for c in range(3):
            for g in range(groups):
                at = slice(g * SUBS, (g + 1) * SUBS)
                if kind == 0:
                    line = jnp.sum(power_sum[c, at, :], axis=1, keepdims=True) / column(power_ref, c, g)
                else:
                    line = -pos_sum[at, c : c + 1] - 2.0 * column(pos_ref, c, g) * pos_sum[at, 4:5]
                spread = jnp.where(wide == deep + (g * SUBS + c * lights), line, spread)
        lines.append(jnp.sum(spread, axis=0, keepdims=True))
    first = lax.broadcasted_iota(jnp.int32, (1, LANES), 1)
    light_ref[0:1, :] = jnp.where(first == 3 * lights, whole(square_sum[...]), lines[0])
    light_ref[1:2, :] = lines[1]


def block_gradients(f, sums_ref):
    def summed(q):
        start = q * CHUNKS * SUM_PITCH
        parts = [sums_ref[pl.ds(start + i, CHUNKS, stride=SUM_PITCH), :] for i in range(SUBS)]
        while len(parts) > 1:
            parts = [a + b for a, b in zip(parts[::2], parts[1::2])]
        return parts[0]

    z = [summed(q) for q in range(SUMS)]
    vt, vb, vn = f["vt"], f["vb"], f["vn"]
    uv = z[SH] * f["rwv"] * f["rcv"]
    wv = -z[SH] * f["rwv"] * f["cv"] * f["vroot"]
    ax2, ay2, ix2, iy2 = f["ax2"], f["ay2"], f["ix2"], f["iy2"]
    pt, pb = uv * vt * ax2, uv * vb * ay2
    tau_x = (ay2 - 1.0) * z[V23] - z[TX] - (pb * vn + wv * vb)
    tau_y = (1.0 - ax2) * z[V13] + z[TY] + (pt * vn + wv * vt)
    tau_z = (iy2 * ax2 - 1.0) * z[V12] + (ay2 * ix2 - 1.0) * (z[U12] + pt * vb)
    turned = tau_x + f["inv"] * f["along"] * tau_z
    grads = [z[SD0 + c] * (0.5 / math.pi) for c in range(3)]
    grads += [z[SS0 + c] * f["lobe"] for c in range(3)]
    grads.append(z[V11] - (z[U11] + pt * vt) - z[SH])
    grads.append(z[V22] - (z[U22] + pb * vb) - z[SH])
    grads.append(f["kappa"] * (f["t_loc"][1] * tau_y - f["b_loc"][1] * turned))
    grads.append(f["kappa"] * (f["t_loc"][2] * tau_y - f["b_loc"][2] * turned))
    grads.append(tau_z * f["inv"] * f["inv"] * f["kappa"])
    grads.append((z[SF] - z[SH]) * f["inv_f1"])
    return grads


def local_gradients(observed, shadow, view_ids, points, frames, params, power, pos, cameras):
    lights, pixels = shadow.shape
    hbm = pl.BlockSpec(memory_space=pltpu.HBM)
    vmem = pl.BlockSpec(memory_space=pltpu.VMEM)
    return pl.pallas_call(
        gradient_kernel,
        in_specs=[pl.BlockSpec(memory_space=pltpu.SMEM)] + [hbm] * 6 + [vmem] * 2,
        out_specs=[vmem, vmem],
        out_shape=[
            jax.ShapeDtypeStruct((pixels // LANES * ROWS, LANES), jnp.float32),
            jax.ShapeDtypeStruct((2, LANES), jnp.float32),
        ],
        scratch_shapes=[
            pltpu.VMEM(observed.shape, observed.dtype),
            pltpu.VMEM(shadow.shape, jnp.int32),
            pltpu.VMEM((pixels // LANES, LANES), jnp.int32),
            pltpu.VMEM(points.shape, jnp.float32),
            pltpu.VMEM(frames.shape, jnp.float32),
            pltpu.VMEM(params.shape, jnp.float32),
            pltpu.VMEM((CHUNKS * RAW, LANES), jnp.float32),
            pltpu.VMEM((TABLE, CHUNKS, LANES), jnp.float32),
            pltpu.VMEM((SUMS * CHUNKS * SUM_PITCH, LANES), jnp.float32),
            pltpu.VMEM((lights, DEPTH), jnp.bfloat16),
            pltpu.VMEM((BLOCKS * CHUNKS * PITCH, LANES), jnp.float32),
            pltpu.VMEM((lights, BLOCKS * LANES), jnp.float32),
            pltpu.VMEM((lights, BLOCKS * LANES), jnp.float32),
            pltpu.VMEM((16, BLOCKS * LANES), jnp.bfloat16),
            pltpu.VMEM((3, lights, LANES), jnp.float32),
            pltpu.VMEM((3, lights, LANES), jnp.float32),
            pltpu.VMEM((lights, 16), jnp.float32),
            pltpu.VMEM((SUBS, LANES), jnp.float32),
            pltpu.SemaphoreType.DMA((2, 6)),
        ],
        compiler_params=pltpu.CompilerParams(vmem_limit_bytes=16 << 20),
        name="pair_gradients",
    )(
        *(
            pltpu.with_memory_space_constraint(x, pltpu.HBM)
            for x in (
                cameras, observed, shadow, view_ids.reshape(pixels // LANES, LANES),
                points, frames, params, power, pos,
            )
        )
    )


def share_kernel(mark, arrived_ref, light_ref, share_ref, spread_ref):
    parts, rows = arrived_ref.shape[:2]
    squares = jnp.zeros((SUBS, LANES), jnp.float32)
    for at in range(0, rows, SUBS):
        pieces = [arrived_ref[i, at : at + SUBS, :] for i in range(parts)]
        while len(pieces) > 1:
            pieces = [a + b for a, b in zip(pieces[::2], pieces[1::2])]
        share_ref[at : at + SUBS, :] = pieces[0]
        squares = squares + pieces[0] * pieces[0]
    lane = lax.broadcasted_iota(jnp.int32, (2, LANES), 1)
    deep = lax.broadcasted_iota(jnp.int32, (2, LANES), 0)
    tile = jnp.where((lane == mark) & (deep == 1), whole(squares), light_ref[...])
    for i in range(spread_ref.shape[0]):
        spread_ref[i] = tile


def join_kernel(mark, share_ref, light_parts_ref, out_ref, light_ref):
    tile = light_parts_ref[0]
    for i in range(1, light_parts_ref.shape[0]):
        tile = tile + light_parts_ref[i]
    light_ref[...] = tile
    lane = lax.broadcasted_iota(jnp.int32, (2, LANES), 1)
    light_sq = whole(jnp.where(lane < mark, tile * tile, 0.0))
    deep = lax.broadcasted_iota(jnp.int32, (SUBS, LANES), 0)
    wide = lax.broadcasted_iota(jnp.int32, (SUBS, LANES), 1)
    tail = jnp.where(wide == 0, light_sq, 0.0)
    tail = jnp.where(wide == 1, tile[0:1, mark : mark + 1], tail)
    tail = jnp.where(wide == 2, tile[1:2, mark : mark + 1], tail)
    tail = jnp.where(deep == 0, tail, 0.0)
    rows = share_ref.shape[0]
    for at in range(0, rows, SUBS):
        value = share_ref[at : at + SUBS, :]
        for i in range(out_ref.shape[0]):
            out_ref[i, at : at + SUBS, :] = value
    for i in range(out_ref.shape[0]):
        out_ref[i, rows : rows + SUBS, :] = tail


def step_kernel(
    pixel_total, light_total, gathered_ref, light_ref, params_ref, power_ref, pos_ref,
    new_params_ref, new_power_ref, new_pos_ref, loss_ref,
):
    parts, rows = gathered_ref.shape[0], gathered_ref.shape[1] - SUBS
    tail = gathered_ref[0, rows : rows + SUBS, :]
    for i in range(1, parts):
        tail = tail + gathered_ref[i, rows : rows + SUBS, :]
    light_scale = STRIDE * lax.rsqrt(tail[0:1, 0:1] / (6 * light_total) + EPS)
    pixel_scale = STRIDE * lax.rsqrt(tail[0:1, 2:3] / (ROWS * pixel_total) + EPS)
    loss_ref[...] = tail[0:1, 1:2] / (3.0 * light_total * pixel_total)
    lights = power_ref.shape[1]
    for c in range(3):
        cut = slice(c * lights, (c + 1) * lights)
        new_power_ref[c : c + 1, :] = power_ref[c : c + 1, :] - light_ref[0:1, cut] * light_scale
        new_pos_ref[c : c + 1, :] = pos_ref[c : c + 1, :] - light_ref[1:2, cut] * light_scale
    chunks = rows // ROWS
    for i in range(parts):
        for k in range(chunks):
            cut = slice((i * chunks + k) * LANES, (i * chunks + k + 1) * LANES)
            grad = gathered_ref[i, k * ROWS : (k + 1) * ROWS, :]
            new_params_ref[:, cut] = params_ref[:, cut] - grad * pixel_scale


def broadcast_exchange(x, axes):
    return lax.all_to_all(x, axes, split_axis=0, concat_axis=0, tiled=True)


def shards(observed, shadow, view_ids, points, frames, params, power, pos, cameras):
    lights, pixels = shadow.shape
    px_size, lt_size = lax.axis_size(PX), lax.axis_size(LT)
    grads, light_tile = local_gradients(
        observed, shadow, view_ids, points, frames, params, power, pos, cameras
    )
    share_rows = grads.shape[0] // lt_size
    mark = 3 * lights
    small = pltpu.CompilerParams(vmem_limit_bytes=8 << 20)
    arrived = broadcast_exchange(grads.reshape(lt_size, share_rows, LANES), LT)
    share, spread = pl.pallas_call(
        functools.partial(share_kernel, mark),
        out_shape=(
            jax.ShapeDtypeStruct((share_rows, LANES), jnp.float32),
            jax.ShapeDtypeStruct((px_size, 2, LANES), jnp.float32),
        ),
        compiler_params=small,
        name="share_sum",
    )(arrived, light_tile)
    light_parts = broadcast_exchange(spread, PX)
    joined, own_lights = pl.pallas_call(
        functools.partial(join_kernel, mark),
        out_shape=(
            jax.ShapeDtypeStruct((lt_size, share_rows + SUBS, LANES), jnp.float32),
            jax.ShapeDtypeStruct((2, LANES), jnp.float32),
        ),
        compiler_params=small,
        name="join",
    )(share, light_parts)
    gathered = broadcast_exchange(joined, LT)
    new_params, new_power, new_pos, loss = pl.pallas_call(
        functools.partial(step_kernel, pixels * px_size, lights * lt_size),
        out_shape=(
            jax.ShapeDtypeStruct(params.shape, jnp.float32),
            jax.ShapeDtypeStruct(power.shape, jnp.float32),
            jax.ShapeDtypeStruct(pos.shape, jnp.float32),
            jax.ShapeDtypeStruct((1, 1), jnp.float32),
        ),
        compiler_params=small,
        name="step",
    )(gathered, own_lights, params, power, pos)
    return new_params, new_power, new_pos, loss.reshape(())


def solution(mesh):
    torus = Mesh(mesh.devices.reshape(4, 4, 2, 8, 2), PX + LT)
    placed = (
        P(None, LT, PX),
        P(LT, PX),
        P(PX),
        P(None, PX),
        P(None, PX),
        P(None, PX),
        P(None, LT),
        P(None, LT),
        P(),
    )
    return jax.shard_map(
        shards,
        mesh=torus,
        in_specs=placed,
        out_specs=(P(None, PX), P(None, LT), P(None, LT), P()),
        check_vma=False,
    )
```

```python
import functools
import math

import jax
import jax.numpy as jnp
from jax import lax
from jax.experimental import pallas as pl
from jax.experimental.pallas import tpu as pltpu
from jax.sharding import Mesh
from jax.sharding import PartitionSpec as P

PX = ("px_0", "px_1", "px_2")
LT = ("lt_0", "lt_1")

SOFT = 0.01
EPS = 1e-06
STRIDE = 0.2
LANES = 128
SUBS = 8
ROWS = 12
BLOCK = 2048
CHUNKS = BLOCK // LANES
RAW = 25
DEPTH = 16
PITCH = 17
SUM_PITCH = 9
UNROLL = 16
PIECES = 4

(VT, VB, VN, AX2, AY2, IX2, IY2, F0, F1, K5, KD0, KD1, KD2, KS0, KS1, KS2) = range(16)
TABLE = 16
(SD0, SD1, SD2, SS0, SS1, SS2, SF, SH, V11, V22, V12, V13, V23, U11, U22, U12, TX, TY) = range(18)
SUMS = 18
LEFT = (0, 0, 1)
RIGHT = (0, 1, 0)
COMPS = 5
BLOCKS = 5
SQUARED = 3


def inner_three(first, second):
    return first[0] * second[0] + first[1] * second[1] + first[2] * second[2]


def pixel_frame(row, ids, camera_ref):
    azimuth = 2.0 * math.pi * row(17)
    ca, sa = jnp.cos(row(16)), jnp.sin(row(16))
    cz, sz = jnp.cos(azimuth), jnp.sin(azimuth)
    base_n = [sa * cz, sa * sz, ca]
    base_t = [ca * cz, ca * sz, -sa]
    base_b = [-sz, cz]
    u, v, spin = row(8), row(9), row(10)
    cs, sn = jnp.cos(spin), jnp.sin(spin)
    kappa = lax.rsqrt(1.0 + u * u + v * v)
    along = kappa * (u * cs + v * sn)
    inv = lax.rsqrt(1.0 - along * along)
    n_loc = [kappa, kappa * u, kappa * v]
    t_loc = [-along * n_loc[0] * inv, (cs - along * n_loc[1]) * inv, (sn - along * n_loc[2]) * inv]
    kb = kappa * inv
    b_loc = [kb * (u * sn - v * cs), -kb * sn, kb * cs]

    def world(loc):
        return [
            loc[0] * base_n[0] + loc[1] * base_t[0] + loc[2] * base_b[0],
            loc[0] * base_n[1] + loc[1] * base_t[1] + loc[2] * base_b[1],
            loc[0] * base_n[2] + loc[1] * base_t[2],
        ]

    tangent, bitangent, normal = world(t_loc), world(b_loc), world(n_loc)
    point = [row(12), row(13), row(14)]
    camera = [jnp.full_like(u, camera_ref[c, 0]) for c in range(3)]
    for view in range(1, camera_ref.shape[1]):
        chosen = ids == view
        camera = [jnp.where(chosen, camera_ref[c, view], camera[c]) for c in range(3)]
    toward = [camera[c] - point[c] for c in range(3)]
    scale = lax.rsqrt(inner_three(toward, toward))
    view_dir = [toward[c] * scale for c in range(3)]
    vt, vb, vn = (inner_three(view_dir, f) for f in (tangent, bitangent, normal))
    ax, ay = jnp.exp(row(6)), jnp.exp(row(7))
    ax2, ay2 = ax * ax, ay * ay
    ix2, iy2 = 1.0 / ax2, 1.0 / ay2
    vroot = lax.rsqrt(vn * vn + SOFT)
    cv = 0.5 * (vn + (vn * vn + SOFT) * vroot)
    wv2 = cv * cv + ax2 * vt * vt + ay2 * vb * vb
    rwv = lax.rsqrt(wv2)
    rcv = 1.0 / (cv + wv2 * rwv)
    return dict(
        tangent=tangent, bitangent=bitangent, normal=normal, point=point, view_dir=view_dir,
        vt=vt, vb=vb, vn=vn, ax=ax, ay=ay, ax2=ax2, ay2=ay2, ix2=ix2, iy2=iy2,
        inv_f1=1.0 / (1.0 - row(11)), lobe=16.0 * rcv / (math.pi * ax * ay), vroot=vroot, cv=cv, rwv=rwv, rcv=rcv, kappa=kappa, inv=inv, along=along,
        t_loc=t_loc, b_loc=b_loc,
    )


def pair_terms(px, offsets, pw, visible, measured):
    ot, ob, on, d2, ov = offsets
    r = lax.rsqrt(d2)
    id2 = r * r
    lt, lb, ln, lv = ot * r, ob * r, on * r, ov * r
    m = 0.5 * lv + 0.5
    a1, a2, a3 = lt + px(VT), lb + px(VB), ln + px(VN)
    b1, b2 = a1 * px(IX2), a2 * px(IY2)
    rq = lax.rsqrt(b1 * a1 + b2 * a2 + a3 * a3)
    rq = rq * rq
    rm = lax.rsqrt(m)
    om = 1.0 - m * rm
    om2 = om * om
    om4 = om2 * om2
    s5 = om4 * om
    fresnel = px(F0) + px(F1) * s5
    rf = lax.rsqrt(fresnel)
    lsq = ln * ln + SOFT
    rs = lax.rsqrt(lsq)
    cn = ln + lsq * rs
    xt, xb = lt * px(AX2), lb * px(AY2)
    wsq = cn * cn + (xt * lt + xb * lb)
    rw = lax.rsqrt(wsq)
    rc = lax.rsqrt(cn + wsq * rw)
    rc = rc * rc
    cni = cn * (id2 * visible)
    mq = m * rq
    gi = (mq * mq) * (rc * cni) * fresnel
    sums = [None] * SUMS
    power_terms = []
    squares = h = s = None
    for c in range(3):
        diffuse, glossy = pw[c] * cni, pw[c] * gi
        res = px(KD0 + c) * diffuse + px(KS0 + c) * glossy - measured[c]
        squares = res * res if c == 0 else squares + res * res
        sums[SD0 + c], sums[SS0 + c] = res * diffuse, res * glossy
        part = px(KS0 + c) * sums[SS0 + c]
        term = px(KD0 + c) * sums[SD0 + c] + part
        power_terms.append(term)
        h = part if c == 0 else h + part
        s = term if c == 0 else s + term
    squares = squares * visible
    x = (h * rf) * rf
    nm = rm * ((x * om4) * px(K5) - h * rm)
    hw = h * rw
    uu = hw * rc
    ww = rs * (s - hw * cn)
    v4 = (4.0 * h) * rq
    p1, p2 = uu * xt, uu * xb
    q1, q2, q3 = v4 * b1, v4 * b2, v4 * a3
    sums[SF] = x
    sums[SH] = h
    sums[V11], sums[V22], sums[V12] = q1 * a1, q2 * a2, q1 * a2
    sums[V13], sums[V23] = q1 * a3, q2 * a3
    sums[U11], sums[U22], sums[U12] = p1 * lt, p2 * lb, p1 * lb
    sums[TX], sums[TY] = p2 * ln + ww * lb, p1 * ln + ww * lt
    g1, g2, g3 = p1 + q1, p2 + q2, q3 - ww
    inner = (lt * g1 + lb * g2) + (ln * g3 + lv * nm)
    cots = [r * g1, r * g2, r * g3, id2 * (s - 0.5 * inner), r * nm]
    return sums, power_terms, squares, cots


def whole(x):
    return jnp.sum(jnp.sum(x, axis=0, keepdims=True), axis=1, keepdims=True)


def rounded(x):
    return x.astype(jnp.bfloat16).astype(jnp.float32)


def split_two(x):
    first = rounded(x)
    return [first, x - first]


def gradient_kernel(
    camera_ref, observed_hbm, shadow_hbm, ids_hbm, points_hbm, frames_hbm, params_hbm, power_ref, pos_ref,
    grads_ref, light_ref,
    observed_ref, shadow_ref, ids_ref, points_ref, frames_ref, params_ref,
    raw, table, sums_ref, left, right, offsets, spread_ref, frames_packed, power_wide, power_sum, pos_sum,
    square_sum, sems,
):
    lights, pixels = shadow_hbm.shape
    groups = lights // SUBS
    steps = pixels // BLOCK

    def copies(first, count):
        cut = slice(first * BLOCK, (first + count) * BLOCK)
        tile = slice(first * CHUNKS, (first + count) * CHUNKS)
        slot = min(first, 1)
        pairs = [
            (params_hbm.at[:, cut], params_ref.at[:, cut]),
            (points_hbm.at[:, cut], points_ref.at[:, cut]),
            (frames_hbm.at[:, cut], frames_ref.at[:, cut]),
            (ids_hbm.at[tile, :], ids_ref.at[tile, :]),
            (shadow_hbm.at[:, cut], shadow_ref.at[:, cut]),
            (observed_hbm.at[:, :, cut], observed_ref.at[:, :, cut]),
        ]
        return [pltpu.make_async_copy(a, b, sems.at[slot, i]) for i, (a, b) in enumerate(pairs)]

    stages = [copies(0, 1), copies(1, steps - 1)]
    for copy in stages[0]:
        copy.start()

    power_sum[...] = jnp.zeros_like(power_sum)
    pos_sum[...] = jnp.zeros_like(pos_sum)
    square_sum[...] = jnp.zeros_like(square_sum)
    spread_ref[...] = jnp.zeros_like(spread_ref)
    frames_packed[...] = jnp.zeros_like(frames_packed)
    right[...] = jnp.zeros_like(right)

    def piece(b):
        return slice(b * LANES, (b + 1) * LANES)

    def right_rows(b, q):
        return pl.ds(b * CHUNKS * PITCH + q, CHUNKS, stride=PITCH)

    for i, part in enumerate(RIGHT):
        if part == 0:
            right[right_rows(SQUARED, i * COMPS + 4), :] = jnp.ones((CHUNKS, LANES), jnp.float32)
    lane = lax.broadcasted_iota(jnp.int32, (SUBS, lights), 1)
    sub = lax.broadcasted_iota(jnp.int32, (SUBS, lights), 0)

    def column(source, c, g):
        picked = jnp.where(lane == sub + g * SUBS, source[c : c + 1, :], 0.0)
        return jnp.sum(picked, axis=1, keepdims=True)

    deep_lane = lax.broadcasted_iota(jnp.int32, (SUBS, DEPTH), 1)
    one = jnp.ones((SUBS, DEPTH), jnp.float32)
    zero = jnp.zeros((SUBS, DEPTH), jnp.float32)
    tiles = []
    for g in range(groups):
        at = slice(g * SUBS, (g + 1) * SUBS)
        for c in range(3):
            power_wide[c, at, :] = jnp.broadcast_to(column(power_ref, c, g), (SUBS, LANES))
        pos = [jnp.broadcast_to(column(pos_ref, c, g), (SUBS, DEPTH)) for c in range(3)]
        splits = [split_two(x) for x in pos] + [[one, zero], split_two(inner_three(pos, pos))]
        tile = zero
        for i, part in enumerate(LEFT):
            for c in range(COMPS):
                tile = jnp.where(deep_lane == i * COMPS + c, splits[c][part], tile)
        tiles.append(tile)
    left[...] = jnp.concatenate(tiles, axis=0).astype(jnp.bfloat16)

    def product(k):
        frame = jnp.concatenate(
            [right[pl.ds((b * CHUNKS + k) * PITCH, DEPTH), :] for b in range(BLOCKS)], axis=1
        ).astype(jnp.bfloat16)
        frames_packed[k] = frame
        return jnp.dot(left[...], frame, preferred_element_type=jnp.float32)

    def gather_positions(k):
        pos_sum[...] += lax.dot_general(
            spread_ref[...].astype(jnp.bfloat16), frames_packed[k], (((1,), (1,)), ((), ())),
            preferred_element_type=jnp.float32,
        )

    for copy in stages[0][:4]:
        copy.wait()
    for stage in stages[1:]:
        for copy in stage:
            copy.start()

    def arrive(step, first, some):
        for i, stage in enumerate(stages[first:], first):

            @pl.when(step == i)
            def _(stage=stage):
                for copy in stage[some]:
                    copy.wait()

    def block(step, _):
        arrive(step, 1, slice(0, 4))

        base = pl.multiple_of(step * BLOCK, BLOCK)
        for k in range(CHUNKS):
            cut = pl.ds(pl.multiple_of(base + k * LANES, LANES), LANES)
            raw[k * RAW : k * RAW + 12, :] = params_ref[:, cut]
            raw[k * RAW + 12 : k * RAW + 15, :] = points_ref[:, cut]
            raw[k * RAW + 16 : k * RAW + 18, :] = frames_ref[:, cut]

        def row(q):
            return raw[pl.ds(q, CHUNKS, stride=RAW), :]

        ids = ids_ref[pl.ds(pl.multiple_of(step * CHUNKS, CHUNKS), CHUNKS), :]
        f = pixel_frame(row, ids, camera_ref)
        point = f["point"]
        columns = [
            [*vec, -inner_three(point, vec)] for vec in (f["tangent"], f["bitangent"], f["normal"])
        ]
        columns.append([-2.0 * point[c] for c in range(3)] + [inner_three(point, point)])
        columns.append([*f["view_dir"], -inner_three(point, f["view_dir"])])
        for b, column_of in enumerate(columns):
            for c, value in enumerate(column_of):
                parts = [value, value - rounded(value)]
                for i, part in enumerate(RIGHT):
                    right[right_rows(b, i * COMPS + c), :] = parts[part]
        entries = {
            AX2: 4.0 * f["ax2"], AY2: 4.0 * f["ay2"], IX2: f["ix2"], IY2: f["iy2"],
            VT: f["vt"], VB: f["vb"], VN: f["vn"],
            F0: row(11), F1: 1.0 - row(11), K5: 1.25 - 1.25 * row(11),
        }
        for c in range(3):
            entries[KD0 + c] = row(c) * (0.5 / math.pi)
            entries[KS0 + c] = row(3 + c) * f["lobe"]
        for q, value in entries.items():
            table[q] = value
        offsets[...] = product(0)

        def chunk(k, _):
            cut = pl.ds(pl.multiple_of(base + k * LANES, LANES), LANES)

            def px(q):
                return jnp.broadcast_to(table[q, pl.ds(k, 1), :], (SUBS, LANES))

            following = product(jnp.minimum(k + 1, CHUNKS - 1))
            gather_positions(jnp.where(k == 0, CHUNKS, k) - 1)
            total = squares = None
            for g in range(groups):
                at = slice(g * SUBS, (g + 1) * SUBS)
                visible = shadow_ref[at, cut].astype(jnp.float32)
                measured = [observed_ref[c, at, cut].astype(jnp.float32) for c in range(3)]
                sums, power_terms, square, cot = pair_terms(
                    px, [offsets[at, piece(b)] for b in range(BLOCKS)],
                    [power_wide[c, at, :] for c in range(3)], visible, measured,
                )
                total = sums if total is None else [a + b for a, b in zip(total, sums)]
                squares = square if squares is None else squares + square
                for b in range(BLOCKS):
                    spread_ref[at, piece(b)] = cot[b]
                for c in range(3):
                    power_sum[c, at, :] += power_terms[c]
            square_sum[...] += squares
            for q in range(SUMS):
                sums_ref[pl.ds((q * CHUNKS + k) * SUM_PITCH, SUBS), :] = total[q]
            offsets[...] = following
            return 0

        arrive(step, 0, slice(4, 6))
        lax.fori_loop(0, CHUNKS, chunk, 0, unroll=UNROLL)
        grads = block_gradients(f, sums_ref)
        for q in range(ROWS):
            grads_ref[pl.ds(step * (CHUNKS * ROWS) + q, CHUNKS, stride=ROWS), :] = grads[q]
        return 0

    lax.fori_loop(0, steps, block, 0)

    gather_positions(CHUNKS - 1)
    wide = lax.broadcasted_iota(jnp.int32, (SUBS, LANES), 1)
    deep = lax.broadcasted_iota(jnp.int32, (SUBS, LANES), 0)
    lines = []
    for kind in range(2):
        spread = jnp.zeros((SUBS, LANES), jnp.float32)
        for c in range(3):
            for g in range(groups):
                at = slice(g * SUBS, (g + 1) * SUBS)
                if kind == 0:
                    line = jnp.sum(power_sum[c, at, :], axis=1, keepdims=True) / column(power_ref, c, g)
                else:
                    line = -pos_sum[at, c : c + 1] - 2.0 * column(pos_ref, c, g) * pos_sum[at, 4:5]
                spread = jnp.where(wide == deep + (g * SUBS + c * lights), line, spread)
        lines.append(jnp.sum(spread, axis=0, keepdims=True))
    first = lax.broadcasted_iota(jnp.int32, (1, LANES), 1)
    light_ref[0:1, :] = jnp.where(first == 3 * lights, whole(square_sum[...]), lines[0])
    light_ref[1:2, :] = lines[1]


def block_gradients(f, sums_ref):
    def summed(q):
        start = q * CHUNKS * SUM_PITCH
        parts = [sums_ref[pl.ds(start + i, CHUNKS, stride=SUM_PITCH), :] for i in range(SUBS)]
        while len(parts) > 1:
            parts = [a + b for a, b in zip(parts[::2], parts[1::2])]
        return parts[0]

    z = [summed(q) for q in range(SUMS)]
    vt, vb, vn = f["vt"], f["vb"], f["vn"]
    uv = z[SH] * f["rwv"] * f["rcv"]
    wv = -z[SH] * f["rwv"] * f["cv"] * f["vroot"]
    ax2, ay2, ix2, iy2 = f["ax2"], f["ay2"], f["ix2"], f["iy2"]
    pt, pb = uv * vt * ax2, uv * vb * ay2
    tau_x = (ay2 - 1.0) * z[V23] - z[TX] - (pb * vn + wv * vb)
    tau_y = (1.0 - ax2) * z[V13] + z[TY] + (pt * vn + wv * vt)
    tau_z = (iy2 * ax2 - 1.0) * z[V12] + (ay2 * ix2 - 1.0) * (z[U12] + pt * vb)
    turned = tau_x + f["inv"] * f["along"] * tau_z
    grads = [z[SD0 + c] * (0.5 / math.pi) for c in range(3)]
    grads += [z[SS0 + c] * f["lobe"] for c in range(3)]
    grads.append(z[V11] - (z[U11] + pt * vt) - z[SH])
    grads.append(z[V22] - (z[U22] + pb * vb) - z[SH])
    grads.append(f["kappa"] * (f["t_loc"][1] * tau_y - f["b_loc"][1] * turned))
    grads.append(f["kappa"] * (f["t_loc"][2] * tau_y - f["b_loc"][2] * turned))
    grads.append(tau_z * f["inv"] * f["inv"] * f["kappa"])
    grads.append((z[SF] - z[SH]) * f["inv_f1"])
    return grads


def local_gradients(observed, shadow, view_ids, points, frames, params, power, pos, cameras):
    lights, pixels = shadow.shape
    hbm = pl.BlockSpec(memory_space=pltpu.HBM)
    vmem = pl.BlockSpec(memory_space=pltpu.VMEM)
    return pl.pallas_call(
        gradient_kernel,
        in_specs=[pl.BlockSpec(memory_space=pltpu.SMEM)] + [hbm] * 6 + [vmem] * 2,
        out_specs=[vmem, vmem],
        out_shape=[
            jax.ShapeDtypeStruct((pixels // LANES * ROWS, LANES), jnp.float32),
            jax.ShapeDtypeStruct((2, LANES), jnp.float32),
        ],
        scratch_shapes=[
            pltpu.VMEM(observed.shape, observed.dtype),
            pltpu.VMEM(shadow.shape, jnp.int32),
            pltpu.VMEM((pixels // LANES, LANES), jnp.int32),
            pltpu.VMEM(points.shape, jnp.float32),
            pltpu.VMEM(frames.shape, jnp.float32),
            pltpu.VMEM(params.shape, jnp.float32),
            pltpu.VMEM((CHUNKS * RAW, LANES), jnp.float32),
            pltpu.VMEM((TABLE, CHUNKS, LANES), jnp.float32),
            pltpu.VMEM((SUMS * CHUNKS * SUM_PITCH, LANES), jnp.float32),
            pltpu.VMEM((lights, DEPTH), jnp.bfloat16),
            pltpu.VMEM((BLOCKS * CHUNKS * PITCH, LANES), jnp.float32),
            pltpu.VMEM((lights, BLOCKS * LANES), jnp.float32),
            pltpu.VMEM((lights, BLOCKS * LANES), jnp.float32),
            pltpu.VMEM((CHUNKS, DEPTH, BLOCKS * LANES), jnp.bfloat16),
            pltpu.VMEM((3, lights, LANES), jnp.float32),
            pltpu.VMEM((3, lights, LANES), jnp.float32),
            pltpu.VMEM((lights, 16), jnp.float32),
            pltpu.VMEM((SUBS, LANES), jnp.float32),
            pltpu.SemaphoreType.DMA((2, 6)),
        ],
        compiler_params=pltpu.CompilerParams(vmem_limit_bytes=16 << 20),
        name="pair_gradients",
    )(
        *(
            pltpu.with_memory_space_constraint(x, pltpu.HBM)
            for x in (
                cameras, observed, shadow, view_ids.reshape(pixels // LANES, LANES),
                points, frames, params, power, pos,
            )
        )
    )


def share_kernel(mark, arrived_ref, light_ref, share_ref, spread_ref):
    parts, rows = arrived_ref.shape[:2]
    squares = jnp.zeros((SUBS, LANES), jnp.float32)
    for at in range(0, rows, SUBS):
        pieces = [arrived_ref[i, at : at + SUBS, :] for i in range(parts)]
        while len(pieces) > 1:
            pieces = [a + b for a, b in zip(pieces[::2], pieces[1::2])]
        share_ref[at : at + SUBS, :] = pieces[0]
        squares = squares + pieces[0] * pieces[0]
    lane = lax.broadcasted_iota(jnp.int32, (2, LANES), 1)
    deep = lax.broadcasted_iota(jnp.int32, (2, LANES), 0)
    tile = jnp.where((lane == mark) & (deep == 1), whole(squares), light_ref[...])
    for i in range(spread_ref.shape[0]):
        spread_ref[i] = tile


def join_kernel(mark, share_ref, light_parts_ref, out_ref, light_ref):
    tile = light_parts_ref[0]
    for i in range(1, light_parts_ref.shape[0]):
        tile = tile + light_parts_ref[i]
    light_ref[...] = tile
    lane = lax.broadcasted_iota(jnp.int32, (2, LANES), 1)
    light_sq = whole(jnp.where(lane < mark, tile * tile, 0.0))
    deep = lax.broadcasted_iota(jnp.int32, (SUBS, LANES), 0)
    wide = lax.broadcasted_iota(jnp.int32, (SUBS, LANES), 1)
    tail = jnp.where(wide == 0, light_sq, 0.0)
    tail = jnp.where(wide == 1, tile[0:1, mark : mark + 1], tail)
    tail = jnp.where(wide == 2, tile[1:2, mark : mark + 1], tail)
    tail = jnp.where(deep == 0, tail, 0.0)
    rows = share_ref.shape[0]
    for at in range(0, rows, SUBS):
        value = share_ref[at : at + SUBS, :]
        for i in range(out_ref.shape[0]):
            out_ref[i, at : at + SUBS, :] = value
    for i in range(out_ref.shape[0]):
        out_ref[i, rows : rows + SUBS, :] = tail


def step_kernel(
    pixel_total, light_total, gathered_ref, light_ref, params_ref, power_ref, pos_ref,
    new_params_hbm, new_power_ref, new_pos_ref, loss_ref, stepped, sems,
):
    parts, rows = gathered_ref.shape[0], gathered_ref.shape[1] - SUBS
    tail = gathered_ref[0, rows : rows + SUBS, :]
    for i in range(1, parts):
        tail = tail + gathered_ref[i, rows : rows + SUBS, :]
    pixel_scale = STRIDE * lax.rsqrt(tail[0:1, 2:3] / (ROWS * pixel_total) + EPS)
    pixel_scale = jnp.broadcast_to(pixel_scale, (ROWS, LANES))
    chunks = rows // ROWS
    each = parts // PIECES
    copies = []
    for piece in range(PIECES):
        for i in range(piece * each, (piece + 1) * each):
            for k in range(chunks):
                cut = slice((i * chunks + k) * LANES, (i * chunks + k + 1) * LANES)
                grad = gathered_ref[i, k * ROWS : (k + 1) * ROWS, :]
                stepped[:, cut] = params_ref[:, cut] - grad * pixel_scale
        span = slice(piece * each * chunks * LANES, (piece + 1) * each * chunks * LANES)
        copies.append(
            pltpu.make_async_copy(stepped.at[:, span], new_params_hbm.at[:, span], sems.at[piece])
        )
        copies[-1].start()
    light_scale = STRIDE * lax.rsqrt(tail[0:1, 0:1] / (6 * light_total) + EPS)
    loss_ref[...] = tail[0:1, 1:2] / (3.0 * light_total * pixel_total)
    lights = power_ref.shape[1]
    for c in range(3):
        cut = slice(c * lights, (c + 1) * lights)
        new_power_ref[c : c + 1, :] = power_ref[c : c + 1, :] - light_ref[0:1, cut] * light_scale
        new_pos_ref[c : c + 1, :] = pos_ref[c : c + 1, :] - light_ref[1:2, cut] * light_scale
    for copy in copies:
        copy.wait()


def broadcast_exchange(x, axes):
    return lax.all_to_all(x, axes, split_axis=0, concat_axis=0, tiled=True)


def shards(observed, shadow, view_ids, points, frames, params, power, pos, cameras):
    lights, pixels = shadow.shape
    px_size, lt_size = lax.axis_size(PX), lax.axis_size(LT)
    grads, light_tile = local_gradients(
        observed, shadow, view_ids, points, frames, params, power, pos, cameras
    )
    share_rows = grads.shape[0] // lt_size
    mark = 3 * lights
    small = pltpu.CompilerParams(vmem_limit_bytes=8 << 20)
    arrived = broadcast_exchange(grads.reshape(lt_size, share_rows, LANES), LT)
    share, spread = pl.pallas_call(
        functools.partial(share_kernel, mark),
        out_shape=(
            jax.ShapeDtypeStruct((share_rows, LANES), jnp.float32),
            jax.ShapeDtypeStruct((px_size, 2, LANES), jnp.float32),
        ),
        compiler_params=small,
        name="share_sum",
    )(arrived, light_tile)
    light_parts = broadcast_exchange(spread, PX)
    joined, own_lights = pl.pallas_call(
        functools.partial(join_kernel, mark),
        out_shape=(
            jax.ShapeDtypeStruct((lt_size, share_rows + SUBS, LANES), jnp.float32),
            jax.ShapeDtypeStruct((2, LANES), jnp.float32),
        ),
        compiler_params=small,
        name="join",
    )(share, light_parts)
    gathered = broadcast_exchange(joined, LT)
    new_params, new_power, new_pos, loss = pl.pallas_call(
        functools.partial(step_kernel, pixels * px_size, lights * lt_size),
        out_shape=(
            jax.ShapeDtypeStruct(params.shape, jnp.float32),
            jax.ShapeDtypeStruct(power.shape, jnp.float32),
            jax.ShapeDtypeStruct(pos.shape, jnp.float32),
            jax.ShapeDtypeStruct((1, 1), jnp.float32),
        ),
        out_specs=(pl.BlockSpec(memory_space=pltpu.HBM),) + (pl.BlockSpec(memory_space=pltpu.VMEM),) * 3,
        scratch_shapes=[
            pltpu.VMEM(params.shape, jnp.float32),
            pltpu.SemaphoreType.DMA((PIECES,)),
        ],
        compiler_params=small,
        name="step",
    )(gathered, own_lights, params, power, pos)
    return new_params, new_power, new_pos, loss.reshape(())


def solution(mesh):
    torus = Mesh(mesh.devices.reshape(4, 4, 2, 8, 2), PX + LT)
    placed = (
        P(None, LT, PX),
        P(LT, PX),
        P(PX),
        P(None, PX),
        P(None, PX),
        P(None, PX),
        P(None, LT),
        P(None, LT),
        P(),
    )
    return jax.shard_map(
        shards,
        mesh=torus,
        in_specs=placed,
        out_specs=(P(None, PX), P(None, LT), P(None, LT), P()),
        check_vma=False,
    )
```

```python
import functools
import math

import jax
import jax.numpy as jnp
from jax import lax
from jax.experimental import pallas as pl
from jax.experimental.pallas import tpu as pltpu
from jax.sharding import Mesh
from jax.sharding import PartitionSpec as P

PX = ("px_0", "px_1", "px_2")
LT = ("lt_0", "lt_1")
SHARES = ("lt_1", "lt_0")

SOFT = 0.01
EPS = 1e-06
STRIDE = 0.2
LANES = 128
SUBS = 8
ROWS = 12
BLOCK = 2048
CHUNKS = BLOCK // LANES
RAW = 25
DEPTH = 16
PITCH = 17
SUM_PITCH = 9
UNROLL = 16

(VT, VB, VN, AX2, AY2, IX2, IY2, F0, F1, K5, KD0, KD1, KD2, KS0, KS1, KS2) = range(16)
TABLE = 16
(SD0, SD1, SD2, SS0, SS1, SS2, SF, SH, V11, V22, V12, V13, V23, U11, U22, U12, TX, TY) = range(18)
SUMS = 18
LEFT = (0, 0, 1)
RIGHT = (0, 1, 0)
COMPS = 5
BLOCKS = 5
SQUARED = 3


def inner_three(first, second):
    return first[0] * second[0] + first[1] * second[1] + first[2] * second[2]


def pixel_frame(row, ids, camera_ref):
    azimuth = 2.0 * math.pi * row(17)
    ca, sa = jnp.cos(row(16)), jnp.sin(row(16))
    cz, sz = jnp.cos(azimuth), jnp.sin(azimuth)
    base_n = [sa * cz, sa * sz, ca]
    base_t = [ca * cz, ca * sz, -sa]
    base_b = [-sz, cz]
    u, v, spin = row(8), row(9), row(10)
    cs, sn = jnp.cos(spin), jnp.sin(spin)
    kappa = lax.rsqrt(1.0 + u * u + v * v)
    along = kappa * (u * cs + v * sn)
    inv = lax.rsqrt(1.0 - along * along)
    n_loc = [kappa, kappa * u, kappa * v]
    t_loc = [-along * n_loc[0] * inv, (cs - along * n_loc[1]) * inv, (sn - along * n_loc[2]) * inv]
    kb = kappa * inv
    b_loc = [kb * (u * sn - v * cs), -kb * sn, kb * cs]

    def world(loc):
        return [
            loc[0] * base_n[0] + loc[1] * base_t[0] + loc[2] * base_b[0],
            loc[0] * base_n[1] + loc[1] * base_t[1] + loc[2] * base_b[1],
            loc[0] * base_n[2] + loc[1] * base_t[2],
        ]

    tangent, bitangent, normal = world(t_loc), world(b_loc), world(n_loc)
    point = [row(12), row(13), row(14)]
    camera = [jnp.full_like(u, camera_ref[c, 0]) for c in range(3)]
    for view in range(1, camera_ref.shape[1]):
        chosen = ids == view
        camera = [jnp.where(chosen, camera_ref[c, view], camera[c]) for c in range(3)]
    toward = [camera[c] - point[c] for c in range(3)]
    scale = lax.rsqrt(inner_three(toward, toward))
    view_dir = [toward[c] * scale for c in range(3)]
    vt, vb, vn = (inner_three(view_dir, f) for f in (tangent, bitangent, normal))
    ax, ay = jnp.exp(row(6)), jnp.exp(row(7))
    ax2, ay2 = ax * ax, ay * ay
    ix2, iy2 = 1.0 / ax2, 1.0 / ay2
    vroot = lax.rsqrt(vn * vn + SOFT)
    cv = 0.5 * (vn + (vn * vn + SOFT) * vroot)
    wv2 = cv * cv + ax2 * vt * vt + ay2 * vb * vb
    rwv = lax.rsqrt(wv2)
    rcv = 1.0 / (cv + wv2 * rwv)
    return dict(
        tangent=tangent, bitangent=bitangent, normal=normal, point=point, view_dir=view_dir,
        vt=vt, vb=vb, vn=vn, ax=ax, ay=ay, ax2=ax2, ay2=ay2, ix2=ix2, iy2=iy2,
        inv_f1=1.0 / (1.0 - row(11)), lobe=16.0 * rcv / (math.pi * ax * ay), vroot=vroot, cv=cv, rwv=rwv, rcv=rcv, kappa=kappa, inv=inv, along=along,
        t_loc=t_loc, b_loc=b_loc,
    )


def pair_terms(px, offsets, pw, visible, measured):
    ot, ob, on, d2, ov = offsets
    r = lax.rsqrt(d2)
    id2 = r * r
    lt, lb, ln, lv = ot * r, ob * r, on * r, ov * r
    m = 0.5 * lv + 0.5
    a1, a2, a3 = lt + px(VT), lb + px(VB), ln + px(VN)
    b1, b2 = a1 * px(IX2), a2 * px(IY2)
    rq = lax.rsqrt(b1 * a1 + b2 * a2 + a3 * a3)
    rq = rq * rq
    rm = lax.rsqrt(m)
    om = 1.0 - m * rm
    om2 = om * om
    om4 = om2 * om2
    s5 = om4 * om
    fresnel = px(F0) + px(F1) * s5
    rf = lax.rsqrt(fresnel)
    lsq = ln * ln + SOFT
    rs = lax.rsqrt(lsq)
    cn = ln + lsq * rs
    xt, xb = lt * px(AX2), lb * px(AY2)
    wsq = cn * cn + (xt * lt + xb * lb)
    rw = lax.rsqrt(wsq)
    rc = lax.rsqrt(cn + wsq * rw)
    rc = rc * rc
    cni = cn * (id2 * visible)
    mq = m * rq
    gi = (mq * mq) * (rc * cni) * fresnel
    sums = [None] * SUMS
    power_terms = []
    squares = h = s = None
    for c in range(3):
        diffuse, glossy = pw[c] * cni, pw[c] * gi
        res = px(KD0 + c) * diffuse + px(KS0 + c) * glossy - measured[c]
        squares = res * res if c == 0 else squares + res * res
        sums[SD0 + c], sums[SS0 + c] = res * diffuse, res * glossy
        part = px(KS0 + c) * sums[SS0 + c]
        term = px(KD0 + c) * sums[SD0 + c] + part
        power_terms.append(term)
        h = part if c == 0 else h + part
        s = term if c == 0 else s + term
    squares = squares * visible
    x = (h * rf) * rf
    nm = rm * ((x * om4) * px(K5) - h * rm)
    hw = h * rw
    uu = hw * rc
    ww = rs * (s - hw * cn)
    v4 = (4.0 * h) * rq
    p1, p2 = uu * xt, uu * xb
    q1, q2, q3 = v4 * b1, v4 * b2, v4 * a3
    sums[SF] = x
    sums[SH] = h
    sums[V11], sums[V22], sums[V12] = q1 * a1, q2 * a2, q1 * a2
    sums[V13], sums[V23] = q1 * a3, q2 * a3
    sums[U11], sums[U22], sums[U12] = p1 * lt, p2 * lb, p1 * lb
    sums[TX], sums[TY] = p2 * ln + ww * lb, p1 * ln + ww * lt
    g1, g2, g3 = p1 + q1, p2 + q2, q3 - ww
    inner = (lt * g1 + lb * g2) + (ln * g3 + lv * nm)
    cots = [r * g1, r * g2, r * g3, id2 * (s - 0.5 * inner), r * nm]
    return sums, power_terms, squares, cots


def whole(x):
    return jnp.sum(jnp.sum(x, axis=0, keepdims=True), axis=1, keepdims=True)


def rounded(x):
    return x.astype(jnp.bfloat16).astype(jnp.float32)


def split_two(x):
    first = rounded(x)
    return [first, x - first]


def gradient_kernel(
    camera_ref, observed_hbm, shadow_hbm, ids_hbm, points_hbm, frames_hbm, params_hbm, power_ref, pos_ref,
    grads_ref, light_ref,
    observed_ref, shadow_ref, ids_ref, points_ref, frames_ref, params_ref,
    raw, table, sums_ref, left, right, offsets, spread_ref, frames_packed, power_wide, power_sum, pos_sum,
    square_sum, sems,
):
    lights, pixels = shadow_hbm.shape
    groups = lights // SUBS
    steps = pixels // BLOCK

    def copies(first, count):
        cut = slice(first * BLOCK, (first + count) * BLOCK)
        tile = slice(first * CHUNKS, (first + count) * CHUNKS)
        slot = min(first, 1)
        pairs = [
            (params_hbm.at[:, cut], params_ref.at[:, cut]),
            (points_hbm.at[:, cut], points_ref.at[:, cut]),
            (frames_hbm.at[:, cut], frames_ref.at[:, cut]),
            (ids_hbm.at[tile, :], ids_ref.at[tile, :]),
            (shadow_hbm.at[:, cut], shadow_ref.at[:, cut]),
            (observed_hbm.at[:, :, cut], observed_ref.at[:, :, cut]),
        ]
        return [pltpu.make_async_copy(a, b, sems.at[slot, i]) for i, (a, b) in enumerate(pairs)]

    stages = [copies(0, 1), copies(1, steps - 1)]
    for copy in stages[0]:
        copy.start()

    power_sum[...] = jnp.zeros_like(power_sum)
    pos_sum[...] = jnp.zeros_like(pos_sum)
    square_sum[...] = jnp.zeros_like(square_sum)
    spread_ref[...] = jnp.zeros_like(spread_ref)
    frames_packed[...] = jnp.zeros_like(frames_packed)
    right[...] = jnp.zeros_like(right)

    def piece(b):
        return slice(b * LANES, (b + 1) * LANES)

    def right_rows(b, q):
        return pl.ds(b * CHUNKS * PITCH + q, CHUNKS, stride=PITCH)

    for i, part in enumerate(RIGHT):
        if part == 0:
            right[right_rows(SQUARED, i * COMPS + 4), :] = jnp.ones((CHUNKS, LANES), jnp.float32)
    lane = lax.broadcasted_iota(jnp.int32, (SUBS, lights), 1)
    sub = lax.broadcasted_iota(jnp.int32, (SUBS, lights), 0)

    def column(source, c, g):
        picked = jnp.where(lane == sub + g * SUBS, source[c : c + 1, :], 0.0)
        return jnp.sum(picked, axis=1, keepdims=True)

    deep_lane = lax.broadcasted_iota(jnp.int32, (SUBS, DEPTH), 1)
    one = jnp.ones((SUBS, DEPTH), jnp.float32)
    zero = jnp.zeros((SUBS, DEPTH), jnp.float32)
    tiles = []
    for g in range(groups):
        at = slice(g * SUBS, (g + 1) * SUBS)
        for c in range(3):
            power_wide[c, at, :] = jnp.broadcast_to(column(power_ref, c, g), (SUBS, LANES))
        pos = [jnp.broadcast_to(column(pos_ref, c, g), (SUBS, DEPTH)) for c in range(3)]
        splits = [split_two(x) for x in pos] + [[one, zero], split_two(inner_three(pos, pos))]
        tile = zero
        for i, part in enumerate(LEFT):
            for c in range(COMPS):
                tile = jnp.where(deep_lane == i * COMPS + c, splits[c][part], tile)
        tiles.append(tile)
    left[...] = jnp.concatenate(tiles, axis=0).astype(jnp.bfloat16)

    def product(k):
        frame = jnp.concatenate(
            [right[pl.ds((b * CHUNKS + k) * PITCH, DEPTH), :] for b in range(BLOCKS)], axis=1
        ).astype(jnp.bfloat16)
        frames_packed[k] = frame
        return jnp.dot(left[...], frame, preferred_element_type=jnp.float32)

    def gather_positions(k):
        pos_sum[...] += lax.dot_general(
            spread_ref[...].astype(jnp.bfloat16), frames_packed[k], (((1,), (1,)), ((), ())),
            preferred_element_type=jnp.float32,
        )

    for copy in stages[0][:4]:
        copy.wait()
    for stage in stages[1:]:
        for copy in stage:
            copy.start()

    def arrive(step, first, some):
        for i, stage in enumerate(stages[first:], first):

            @pl.when(step == i)
            def _(stage=stage):
                for copy in stage[some]:
                    copy.wait()

    def block(step, _):
        arrive(step, 1, slice(0, 4))

        base = pl.multiple_of(step * BLOCK, BLOCK)
        for k in range(CHUNKS):
            cut = pl.ds(pl.multiple_of(base + k * LANES, LANES), LANES)
            raw[k * RAW : k * RAW + 12, :] = params_ref[:, cut]
            raw[k * RAW + 12 : k * RAW + 15, :] = points_ref[:, cut]
            raw[k * RAW + 16 : k * RAW + 18, :] = frames_ref[:, cut]

        def row(q):
            return raw[pl.ds(q, CHUNKS, stride=RAW), :]

        ids = ids_ref[pl.ds(pl.multiple_of(step * CHUNKS, CHUNKS), CHUNKS), :]
        f = pixel_frame(row, ids, camera_ref)
        point = f["point"]
        columns = [
            [*vec, -inner_three(point, vec)] for vec in (f["tangent"], f["bitangent"], f["normal"])
        ]
        columns.append([-2.0 * point[c] for c in range(3)] + [inner_three(point, point)])
        columns.append([*f["view_dir"], -inner_three(point, f["view_dir"])])
        for b, column_of in enumerate(columns):
            for c, value in enumerate(column_of):
                parts = [value, value - rounded(value)]
                for i, part in enumerate(RIGHT):
                    right[right_rows(b, i * COMPS + c), :] = parts[part]
        entries = {
            AX2: 4.0 * f["ax2"], AY2: 4.0 * f["ay2"], IX2: f["ix2"], IY2: f["iy2"],
            VT: f["vt"], VB: f["vb"], VN: f["vn"],
            F0: row(11), F1: 1.0 - row(11), K5: 1.25 - 1.25 * row(11),
        }
        for c in range(3):
            entries[KD0 + c] = row(c) * (0.5 / math.pi)
            entries[KS0 + c] = row(3 + c) * f["lobe"]
        for q, value in entries.items():
            table[q] = value
        offsets[...] = product(0)

        def chunk(k, _):
            cut = pl.ds(pl.multiple_of(base + k * LANES, LANES), LANES)

            def px(q):
                return jnp.broadcast_to(table[q, pl.ds(k, 1), :], (SUBS, LANES))

            following = product(jnp.minimum(k + 1, CHUNKS - 1))
            gather_positions(jnp.where(k == 0, CHUNKS, k) - 1)
            total = squares = None
            for g in range(groups):
                at = slice(g * SUBS, (g + 1) * SUBS)
                visible = shadow_ref[at, cut].astype(jnp.float32)
                measured = [observed_ref[c, at, cut].astype(jnp.float32) for c in range(3)]
                sums, power_terms, square, cot = pair_terms(
                    px, [offsets[at, piece(b)] for b in range(BLOCKS)],
                    [power_wide[c, at, :] for c in range(3)], visible, measured,
                )
                total = sums if total is None else [a + b for a, b in zip(total, sums)]
                squares = square if squares is None else squares + square
                for b in range(BLOCKS):
                    spread_ref[at, piece(b)] = cot[b]
                for c in range(3):
                    power_sum[c, at, :] += power_terms[c]
            square_sum[...] += squares
            for q in range(SUMS):
                sums_ref[pl.ds((q * CHUNKS + k) * SUM_PITCH, SUBS), :] = total[q]
            offsets[...] = following
            return 0

        arrive(step, 0, slice(4, 6))
        lax.fori_loop(0, CHUNKS, chunk, 0, unroll=UNROLL)
        grads = block_gradients(f, sums_ref)
        for q in range(ROWS):
            grads_ref[pl.ds(step * (CHUNKS * ROWS) + q, CHUNKS, stride=ROWS), :] = grads[q]
        return 0

    lax.fori_loop(0, steps, block, 0)

    gather_positions(CHUNKS - 1)
    wide = lax.broadcasted_iota(jnp.int32, (SUBS, LANES), 1)
    deep = lax.broadcasted_iota(jnp.int32, (SUBS, LANES), 0)
    lines = []
    for kind in range(2):
        spread = jnp.zeros((SUBS, LANES), jnp.float32)
        for c in range(3):
            for g in range(groups):
                at = slice(g * SUBS, (g + 1) * SUBS)
                if kind == 0:
                    line = jnp.sum(power_sum[c, at, :], axis=1, keepdims=True) / column(power_ref, c, g)
                else:
                    line = -pos_sum[at, c : c + 1] - 2.0 * column(pos_ref, c, g) * pos_sum[at, 4:5]
                spread = jnp.where(wide == deep + (g * SUBS + c * lights), line, spread)
        lines.append(jnp.sum(spread, axis=0, keepdims=True))
    first = lax.broadcasted_iota(jnp.int32, (1, LANES), 1)
    light_ref[0:1, :] = jnp.where(first == 3 * lights, whole(square_sum[...]), lines[0])
    light_ref[1:2, :] = lines[1]


def block_gradients(f, sums_ref):
    def summed(q):
        start = q * CHUNKS * SUM_PITCH
        parts = [sums_ref[pl.ds(start + i, CHUNKS, stride=SUM_PITCH), :] for i in range(SUBS)]
        while len(parts) > 1:
            parts = [a + b for a, b in zip(parts[::2], parts[1::2])]
        return parts[0]

    z = [summed(q) for q in range(SUMS)]
    vt, vb, vn = f["vt"], f["vb"], f["vn"]
    uv = z[SH] * f["rwv"] * f["rcv"]
    wv = -z[SH] * f["rwv"] * f["cv"] * f["vroot"]
    ax2, ay2, ix2, iy2 = f["ax2"], f["ay2"], f["ix2"], f["iy2"]
    pt, pb = uv * vt * ax2, uv * vb * ay2
    tau_x = (ay2 - 1.0) * z[V23] - z[TX] - (pb * vn + wv * vb)
    tau_y = (1.0 - ax2) * z[V13] + z[TY] + (pt * vn + wv * vt)
    tau_z = (iy2 * ax2 - 1.0) * z[V12] + (ay2 * ix2 - 1.0) * (z[U12] + pt * vb)
    turned = tau_x + f["inv"] * f["along"] * tau_z
    grads = [z[SD0 + c] * (0.5 / math.pi) for c in range(3)]
    grads += [z[SS0 + c] * f["lobe"] for c in range(3)]
    grads.append(z[V11] - (z[U11] + pt * vt) - z[SH])
    grads.append(z[V22] - (z[U22] + pb * vb) - z[SH])
    grads.append(f["kappa"] * (f["t_loc"][1] * tau_y - f["b_loc"][1] * turned))
    grads.append(f["kappa"] * (f["t_loc"][2] * tau_y - f["b_loc"][2] * turned))
    grads.append(tau_z * f["inv"] * f["inv"] * f["kappa"])
    grads.append((z[SF] - z[SH]) * f["inv_f1"])
    return grads


def local_gradients(observed, shadow, view_ids, points, frames, params, power, pos, cameras):
    lights, pixels = shadow.shape
    hbm = pl.BlockSpec(memory_space=pltpu.HBM)
    vmem = pl.BlockSpec(memory_space=pltpu.VMEM)
    return pl.pallas_call(
        gradient_kernel,
        in_specs=[pl.BlockSpec(memory_space=pltpu.SMEM)] + [hbm] * 6 + [vmem] * 2,
        out_specs=[vmem, vmem],
        out_shape=[
            jax.ShapeDtypeStruct((pixels // LANES * ROWS, LANES), jnp.float32),
            jax.ShapeDtypeStruct((2, LANES), jnp.float32),
        ],
        scratch_shapes=[
            pltpu.VMEM(observed.shape, observed.dtype),
            pltpu.VMEM(shadow.shape, jnp.int32),
            pltpu.VMEM((pixels // LANES, LANES), jnp.int32),
            pltpu.VMEM(points.shape, jnp.float32),
            pltpu.VMEM(frames.shape, jnp.float32),
            pltpu.VMEM(params.shape, jnp.float32),
            pltpu.VMEM((CHUNKS * RAW, LANES), jnp.float32),
            pltpu.VMEM((TABLE, CHUNKS, LANES), jnp.float32),
            pltpu.VMEM((SUMS * CHUNKS * SUM_PITCH, LANES), jnp.float32),
            pltpu.VMEM((lights, DEPTH), jnp.bfloat16),
            pltpu.VMEM((BLOCKS * CHUNKS * PITCH, LANES), jnp.float32),
            pltpu.VMEM((lights, BLOCKS * LANES), jnp.float32),
            pltpu.VMEM((lights, BLOCKS * LANES), jnp.float32),
            pltpu.VMEM((CHUNKS, DEPTH, BLOCKS * LANES), jnp.bfloat16),
            pltpu.VMEM((3, lights, LANES), jnp.float32),
            pltpu.VMEM((3, lights, LANES), jnp.float32),
            pltpu.VMEM((lights, 16), jnp.float32),
            pltpu.VMEM((SUBS, LANES), jnp.float32),
            pltpu.SemaphoreType.DMA((2, 6)),
        ],
        compiler_params=pltpu.CompilerParams(vmem_limit_bytes=16 << 20),
        name="pair_gradients",
    )(
        *(
            pltpu.with_memory_space_constraint(x, pltpu.HBM)
            for x in (
                cameras, observed, shadow, view_ids.reshape(pixels // LANES, LANES),
                points, frames, params, power, pos,
            )
        )
    )


def share_kernel(mark, arrived_ref, light_ref, share_ref, spread_ref):
    parts, rows = arrived_ref.shape[:2]
    squares = jnp.zeros((SUBS, LANES), jnp.float32)
    for at in range(0, rows, SUBS):
        pieces = [arrived_ref[i, at : at + SUBS, :] for i in range(parts)]
        while len(pieces) > 1:
            pieces = [a + b for a, b in zip(pieces[::2], pieces[1::2])]
        share_ref[at : at + SUBS, :] = pieces[0]
        squares = squares + pieces[0] * pieces[0]
    lane = lax.broadcasted_iota(jnp.int32, (2, LANES), 1)
    deep = lax.broadcasted_iota(jnp.int32, (2, LANES), 0)
    tile = jnp.where((lane == mark) & (deep == 1), whole(squares), light_ref[...])
    for i in range(spread_ref.shape[0]):
        spread_ref[i] = tile


def join_kernel(mark, share_ref, light_parts_ref, out_ref, light_ref):
    tile = light_parts_ref[0]
    for i in range(1, light_parts_ref.shape[0]):
        tile = tile + light_parts_ref[i]
    light_ref[...] = tile
    lane = lax.broadcasted_iota(jnp.int32, (2, LANES), 1)
    light_sq = whole(jnp.where(lane < mark, tile * tile, 0.0))
    deep = lax.broadcasted_iota(jnp.int32, (SUBS, LANES), 0)
    wide = lax.broadcasted_iota(jnp.int32, (SUBS, LANES), 1)
    tail = jnp.where(wide == 0, light_sq, 0.0)
    tail = jnp.where(wide == 1, tile[0:1, mark : mark + 1], tail)
    tail = jnp.where(wide == 2, tile[1:2, mark : mark + 1], tail)
    tail = jnp.where(deep == 0, tail, 0.0)
    rows = share_ref.shape[0]
    for at in range(0, rows, SUBS):
        value = share_ref[at : at + SUBS, :]
        for i in range(out_ref.shape[0]):
            out_ref[i, at : at + SUBS, :] = value
    for i in range(out_ref.shape[0]):
        out_ref[i, rows : rows + SUBS, :] = tail


def step_kernel(
    pixel_total, light_total, gathered_ref, light_ref, params_ref, power_ref, pos_ref,
    new_params_ref, new_power_ref, new_pos_ref, loss_ref,
):
    parts, rows = gathered_ref.shape[0], gathered_ref.shape[1] - SUBS
    tail = gathered_ref[0, rows : rows + SUBS, :]
    for i in range(1, parts):
        tail = tail + gathered_ref[i, rows : rows + SUBS, :]
    light_scale = STRIDE * lax.rsqrt(tail[0:1, 0:1] / (6 * light_total) + EPS)
    pixel_scale = STRIDE * lax.rsqrt(tail[0:1, 2:3] / (ROWS * pixel_total) + EPS)
    loss_ref[...] = tail[0:1, 1:2] / (3.0 * light_total * pixel_total)
    lights = power_ref.shape[1]
    for c in range(3):
        cut = slice(c * lights, (c + 1) * lights)
        new_power_ref[c : c + 1, :] = power_ref[c : c + 1, :] - light_ref[0:1, cut] * light_scale
        new_pos_ref[c : c + 1, :] = pos_ref[c : c + 1, :] - light_ref[1:2, cut] * light_scale
    chunks = rows // ROWS
    for i in range(parts):
        for k in range(chunks):
            cut = slice((i * chunks + k) * LANES, (i * chunks + k + 1) * LANES)
            grad = gathered_ref[i, k * ROWS : (k + 1) * ROWS, :]
            new_params_ref[:, cut] = params_ref[:, cut] - grad * pixel_scale


def broadcast_exchange(x, axes):
    return lax.all_to_all(x, axes, split_axis=0, concat_axis=0, tiled=True)


def shards(observed, shadow, view_ids, points, frames, params, power, pos, cameras):
    lights, pixels = shadow.shape
    px_size, lt_size = lax.axis_size(PX), lax.axis_size(LT)
    grads, light_tile = local_gradients(
        observed, shadow, view_ids, points, frames, params, power, pos, cameras
    )
    share_rows = grads.shape[0] // lt_size
    mark = 3 * lights
    small = pltpu.CompilerParams(vmem_limit_bytes=8 << 20)
    arrived = broadcast_exchange(grads.reshape(lt_size, share_rows, LANES), SHARES)
    share, spread = pl.pallas_call(
        functools.partial(share_kernel, mark),
        out_shape=(
            jax.ShapeDtypeStruct((share_rows, LANES), jnp.float32),
            jax.ShapeDtypeStruct((px_size, 2, LANES), jnp.float32),
        ),
        compiler_params=small,
        name="share_sum",
    )(arrived, light_tile)
    light_parts = broadcast_exchange(spread, PX)
    joined, own_lights = pl.pallas_call(
        functools.partial(join_kernel, mark),
        out_shape=(
            jax.ShapeDtypeStruct((lt_size, share_rows + SUBS, LANES), jnp.float32),
            jax.ShapeDtypeStruct((2, LANES), jnp.float32),
        ),
        compiler_params=small,
        name="join",
    )(share, light_parts)
    gathered = broadcast_exchange(joined, SHARES)
    new_params, new_power, new_pos, loss = pl.pallas_call(
        functools.partial(step_kernel, pixels * px_size, lights * lt_size),
        out_shape=(
            jax.ShapeDtypeStruct(params.shape, jnp.float32),
            jax.ShapeDtypeStruct(power.shape, jnp.float32),
            jax.ShapeDtypeStruct(pos.shape, jnp.float32),
            jax.ShapeDtypeStruct((1, 1), jnp.float32),
        ),
        compiler_params=small,
        name="step",
    )(gathered, own_lights, params, power, pos)
    return new_params, new_power, new_pos, loss.reshape(())


def solution(mesh):
    torus = Mesh(mesh.devices.reshape(4, 4, 2, 8, 2), PX + LT)
    placed = (
        P(None, LT, PX),
        P(LT, PX),
        P(PX),
        P(None, PX),
        P(None, PX),
        P(None, PX),
        P(None, LT),
        P(None, LT),
        P(),
    )
    return jax.shard_map(
        shards,
        mesh=torus,
        in_specs=placed,
        out_specs=(P(None, PX), P(None, LT), P(None, LT), P()),
        check_vma=False,
    )
```

```python
import functools
import math

import jax
import jax.numpy as jnp
from jax import lax
from jax.experimental import pallas as pl
from jax.experimental.pallas import tpu as pltpu
from jax.sharding import Mesh
from jax.sharding import PartitionSpec as P

PX = ("px_0", "px_1", "px_2")
LT = ("y_2", "y_1", "y_0", "z_0")
SHARES = ("z_0", "y_0", "y_1", "y_2")

SOFT = 0.01
EPS = 1e-06
STRIDE = 0.2
LANES = 128
SUBS = 8
ROWS = 12
BLOCK = 2048
CHUNKS = BLOCK // LANES
RAW = 25
DEPTH = 16
PITCH = 17
SUM_PITCH = 9
UNROLL = 16

(VT, VB, VN, AX2, AY2, IX2, IY2, F0, F1, K5, KD0, KD1, KD2, KS0, KS1, KS2) = range(16)
TABLE = 16
(SD0, SD1, SD2, SS0, SS1, SS2, SF, SH, V11, V22, V12, V13, V23, U11, U22, U12, TX, TY) = range(18)
SUMS = 18
LEFT = (0, 0, 1)
RIGHT = (0, 1, 0)
COMPS = 5
BLOCKS = 5
SQUARED = 3


def inner_three(first, second):
    return first[0] * second[0] + first[1] * second[1] + first[2] * second[2]


def pixel_frame(row, ids, camera_ref):
    azimuth = 2.0 * math.pi * row(17)
    ca, sa = jnp.cos(row(16)), jnp.sin(row(16))
    cz, sz = jnp.cos(azimuth), jnp.sin(azimuth)
    base_n = [sa * cz, sa * sz, ca]
    base_t = [ca * cz, ca * sz, -sa]
    base_b = [-sz, cz]
    u, v, spin = row(8), row(9), row(10)
    cs, sn = jnp.cos(spin), jnp.sin(spin)
    kappa = lax.rsqrt(1.0 + u * u + v * v)
    along = kappa * (u * cs + v * sn)
    inv = lax.rsqrt(1.0 - along * along)
    n_loc = [kappa, kappa * u, kappa * v]
    t_loc = [-along * n_loc[0] * inv, (cs - along * n_loc[1]) * inv, (sn - along * n_loc[2]) * inv]
    kb = kappa * inv
    b_loc = [kb * (u * sn - v * cs), -kb * sn, kb * cs]

    def world(loc):
        return [
            loc[0] * base_n[0] + loc[1] * base_t[0] + loc[2] * base_b[0],
            loc[0] * base_n[1] + loc[1] * base_t[1] + loc[2] * base_b[1],
            loc[0] * base_n[2] + loc[1] * base_t[2],
        ]

    tangent, bitangent, normal = world(t_loc), world(b_loc), world(n_loc)
    point = [row(12), row(13), row(14)]
    camera = [jnp.full_like(u, camera_ref[c, 0]) for c in range(3)]
    for view in range(1, camera_ref.shape[1]):
        chosen = ids == view
        camera = [jnp.where(chosen, camera_ref[c, view], camera[c]) for c in range(3)]
    toward = [camera[c] - point[c] for c in range(3)]
    scale = lax.rsqrt(inner_three(toward, toward))
    view_dir = [toward[c] * scale for c in range(3)]
    vt, vb, vn = (inner_three(view_dir, f) for f in (tangent, bitangent, normal))
    ax, ay = jnp.exp(row(6)), jnp.exp(row(7))
    ax2, ay2 = ax * ax, ay * ay
    ix2, iy2 = 1.0 / ax2, 1.0 / ay2
    vroot = lax.rsqrt(vn * vn + SOFT)
    cv = 0.5 * (vn + (vn * vn + SOFT) * vroot)
    wv2 = cv * cv + ax2 * vt * vt + ay2 * vb * vb
    rwv = lax.rsqrt(wv2)
    rcv = 1.0 / (cv + wv2 * rwv)
    return dict(
        tangent=tangent, bitangent=bitangent, normal=normal, point=point, view_dir=view_dir,
        vt=vt, vb=vb, vn=vn, ax=ax, ay=ay, ax2=ax2, ay2=ay2, ix2=ix2, iy2=iy2,
        inv_f1=1.0 / (1.0 - row(11)), lobe=16.0 * rcv / (math.pi * ax * ay), vroot=vroot, cv=cv, rwv=rwv, rcv=rcv, kappa=kappa, inv=inv, along=along,
        t_loc=t_loc, b_loc=b_loc,
    )


def pair_terms(px, offsets, pw, visible, measured):
    ot, ob, on, d2, ov = offsets
    r = lax.rsqrt(d2)
    id2 = r * r
    lt, lb, ln, lv = ot * r, ob * r, on * r, ov * r
    m = 0.5 * lv + 0.5
    a1, a2, a3 = lt + px(VT), lb + px(VB), ln + px(VN)
    b1, b2 = a1 * px(IX2), a2 * px(IY2)
    rq = lax.rsqrt(b1 * a1 + b2 * a2 + a3 * a3)
    rq = rq * rq
    rm = lax.rsqrt(m)
    om = 1.0 - m * rm
    om2 = om * om
    om4 = om2 * om2
    s5 = om4 * om
    fresnel = px(F0) + px(F1) * s5
    rf = lax.rsqrt(fresnel)
    lsq = ln * ln + SOFT
    rs = lax.rsqrt(lsq)
    cn = ln + lsq * rs
    xt, xb = lt * px(AX2), lb * px(AY2)
    wsq = cn * cn + (xt * lt + xb * lb)
    rw = lax.rsqrt(wsq)
    rc = lax.rsqrt(cn + wsq * rw)
    rc = rc * rc
    cni = cn * (id2 * visible)
    mq = m * rq
    gi = (mq * mq) * (rc * cni) * fresnel
    sums = [None] * SUMS
    power_terms = []
    squares = h = s = None
    for c in range(3):
        diffuse, glossy = pw[c] * cni, pw[c] * gi
        res = px(KD0 + c) * diffuse + px(KS0 + c) * glossy - measured[c]
        squares = res * res if c == 0 else squares + res * res
        sums[SD0 + c], sums[SS0 + c] = res * diffuse, res * glossy
        part = px(KS0 + c) * sums[SS0 + c]
        term = px(KD0 + c) * sums[SD0 + c] + part
        power_terms.append(term)
        h = part if c == 0 else h + part
        s = term if c == 0 else s + term
    squares = squares * visible
    x = (h * rf) * rf
    nm = rm * ((x * om4) * px(K5) - h * rm)
    hw = h * rw
    uu = hw * rc
    ww = rs * (s - hw * cn)
    v4 = (4.0 * h) * rq
    p1, p2 = uu * xt, uu * xb
    q1, q2, q3 = v4 * b1, v4 * b2, v4 * a3
    sums[SF] = x
    sums[SH] = h
    sums[V11], sums[V22], sums[V12] = q1 * a1, q2 * a2, q1 * a2
    sums[V13], sums[V23] = q1 * a3, q2 * a3
    sums[U11], sums[U22], sums[U12] = p1 * lt, p2 * lb, p1 * lb
    sums[TX], sums[TY] = p2 * ln + ww * lb, p1 * ln + ww * lt
    g1, g2, g3 = p1 + q1, p2 + q2, q3 - ww
    inner = (lt * g1 + lb * g2) + (ln * g3 + lv * nm)
    cots = [r * g1, r * g2, r * g3, id2 * (s - 0.5 * inner), r * nm]
    return sums, power_terms, squares, cots


def whole(x):
    return jnp.sum(jnp.sum(x, axis=0, keepdims=True), axis=1, keepdims=True)


def rounded(x):
    return x.astype(jnp.bfloat16).astype(jnp.float32)


def split_two(x):
    first = rounded(x)
    return [first, x - first]


def gradient_kernel(
    camera_ref, observed_hbm, shadow_hbm, ids_hbm, points_hbm, frames_hbm, params_hbm, power_ref, pos_ref,
    grads_ref, light_ref,
    observed_ref, shadow_ref, ids_ref, points_ref, frames_ref, params_ref,
    raw, table, sums_ref, left, right, offsets, spread_ref, frames_packed, power_wide, power_sum, pos_sum,
    square_sum, sems,
):
    lights, pixels = shadow_hbm.shape
    groups = lights // SUBS
    steps = pixels // BLOCK

    def copies(first, count):
        cut = slice(first * BLOCK, (first + count) * BLOCK)
        tile = slice(first * CHUNKS, (first + count) * CHUNKS)
        slot = min(first, 1)
        pairs = [
            (params_hbm.at[:, cut], params_ref.at[:, cut]),
            (points_hbm.at[:, cut], points_ref.at[:, cut]),
            (frames_hbm.at[:, cut], frames_ref.at[:, cut]),
            (ids_hbm.at[tile, :], ids_ref.at[tile, :]),
            (shadow_hbm.at[:, cut], shadow_ref.at[:, cut]),
            (observed_hbm.at[:, :, cut], observed_ref.at[:, :, cut]),
        ]
        return [pltpu.make_async_copy(a, b, sems.at[slot, i]) for i, (a, b) in enumerate(pairs)]

    stages = [copies(0, 1), copies(1, steps - 1)]
    for copy in stages[0]:
        copy.start()

    power_sum[...] = jnp.zeros_like(power_sum)
    pos_sum[...] = jnp.zeros_like(pos_sum)
    square_sum[...] = jnp.zeros_like(square_sum)
    spread_ref[...] = jnp.zeros_like(spread_ref)
    frames_packed[...] = jnp.zeros_like(frames_packed)
    right[...] = jnp.zeros_like(right)

    def piece(b):
        return slice(b * LANES, (b + 1) * LANES)

    def right_rows(b, q):
        return pl.ds(b * CHUNKS * PITCH + q, CHUNKS, stride=PITCH)

    for i, part in enumerate(RIGHT):
        if part == 0:
            right[right_rows(SQUARED, i * COMPS + 4), :] = jnp.ones((CHUNKS, LANES), jnp.float32)
    lane = lax.broadcasted_iota(jnp.int32, (SUBS, lights), 1)
    sub = lax.broadcasted_iota(jnp.int32, (SUBS, lights), 0)

    def column(source, c, g):
        picked = jnp.where(lane == sub + g * SUBS, source[c : c + 1, :], 0.0)
        return jnp.sum(picked, axis=1, keepdims=True)

    deep_lane = lax.broadcasted_iota(jnp.int32, (SUBS, DEPTH), 1)
    one = jnp.ones((SUBS, DEPTH), jnp.float32)
    zero = jnp.zeros((SUBS, DEPTH), jnp.float32)
    tiles = []
    for g in range(groups):
        at = slice(g * SUBS, (g + 1) * SUBS)
        for c in range(3):
            power_wide[c, at, :] = jnp.broadcast_to(column(power_ref, c, g), (SUBS, LANES))
        pos = [jnp.broadcast_to(column(pos_ref, c, g), (SUBS, DEPTH)) for c in range(3)]
        splits = [split_two(x) for x in pos] + [[one, zero], split_two(inner_three(pos, pos))]
        tile = zero
        for i, part in enumerate(LEFT):
            for c in range(COMPS):
                tile = jnp.where(deep_lane == i * COMPS + c, splits[c][part], tile)
        tiles.append(tile)
    left[...] = jnp.concatenate(tiles, axis=0).astype(jnp.bfloat16)

    def product(k):
        frame = jnp.concatenate(
            [right[pl.ds((b * CHUNKS + k) * PITCH, DEPTH), :] for b in range(BLOCKS)], axis=1
        ).astype(jnp.bfloat16)
        frames_packed[k] = frame
        return jnp.dot(left[...], frame, preferred_element_type=jnp.float32)

    def gather_positions(k):
        pos_sum[...] += lax.dot_general(
            spread_ref[...].astype(jnp.bfloat16), frames_packed[k], (((1,), (1,)), ((), ())),
            preferred_element_type=jnp.float32,
        )

    for copy in stages[0][:4]:
        copy.wait()
    for stage in stages[1:]:
        for copy in stage:
            copy.start()

    def arrive(step, first, some):
        for i, stage in enumerate(stages[first:], first):

            @pl.when(step == i)
            def _(stage=stage):
                for copy in stage[some]:
                    copy.wait()

    def block(step, _):
        arrive(step, 1, slice(0, 4))

        base = pl.multiple_of(step * BLOCK, BLOCK)
        for k in range(CHUNKS):
            cut = pl.ds(pl.multiple_of(base + k * LANES, LANES), LANES)
            raw[k * RAW : k * RAW + 12, :] = params_ref[:, cut]
            raw[k * RAW + 12 : k * RAW + 15, :] = points_ref[:, cut]
            raw[k * RAW + 16 : k * RAW + 18, :] = frames_ref[:, cut]

        def row(q):
            return raw[pl.ds(q, CHUNKS, stride=RAW), :]

        ids = ids_ref[pl.ds(pl.multiple_of(step * CHUNKS, CHUNKS), CHUNKS), :]
        f = pixel_frame(row, ids, camera_ref)
        point = f["point"]
        columns = [
            [*vec, -inner_three(point, vec)] for vec in (f["tangent"], f["bitangent"], f["normal"])
        ]
        columns.append([-2.0 * point[c] for c in range(3)] + [inner_three(point, point)])
        columns.append([*f["view_dir"], -inner_three(point, f["view_dir"])])
        for b, column_of in enumerate(columns):
            for c, value in enumerate(column_of):
                parts = [value, value - rounded(value)]
                for i, part in enumerate(RIGHT):
                    right[right_rows(b, i * COMPS + c), :] = parts[part]
        entries = {
            AX2: 4.0 * f["ax2"], AY2: 4.0 * f["ay2"], IX2: f["ix2"], IY2: f["iy2"],
            VT: f["vt"], VB: f["vb"], VN: f["vn"],
            F0: row(11), F1: 1.0 - row(11), K5: 1.25 - 1.25 * row(11),
        }
        for c in range(3):
            entries[KD0 + c] = row(c) * (0.5 / math.pi)
            entries[KS0 + c] = row(3 + c) * f["lobe"]
        for q, value in entries.items():
            table[q] = value
        offsets[...] = product(0)

        def chunk(k, _):
            cut = pl.ds(pl.multiple_of(base + k * LANES, LANES), LANES)

            def px(q):
                return jnp.broadcast_to(table[q, pl.ds(k, 1), :], (SUBS, LANES))

            following = product(jnp.minimum(k + 1, CHUNKS - 1))
            gather_positions(jnp.where(k == 0, CHUNKS, k) - 1)
            total = squares = None
            for g in range(groups):
                at = slice(g * SUBS, (g + 1) * SUBS)
                visible = shadow_ref[at, cut].astype(jnp.float32)
                measured = [observed_ref[c, at, cut].astype(jnp.float32) for c in range(3)]
                sums, power_terms, square, cot = pair_terms(
                    px, [offsets[at, piece(b)] for b in range(BLOCKS)],
                    [power_wide[c, at, :] for c in range(3)], visible, measured,
                )
                total = sums if total is None else [a + b for a, b in zip(total, sums)]
                squares = square if squares is None else squares + square
                for b in range(BLOCKS):
                    spread_ref[at, piece(b)] = cot[b]
                for c in range(3):
                    power_sum[c, at, :] += power_terms[c]
            square_sum[...] += squares
            for q in range(SUMS):
                sums_ref[pl.ds((q * CHUNKS + k) * SUM_PITCH, SUBS), :] = total[q]
            offsets[...] = following
            return 0

        arrive(step, 0, slice(4, 6))
        lax.fori_loop(0, CHUNKS, chunk, 0, unroll=UNROLL)
        grads = block_gradients(f, sums_ref)
        for q in range(ROWS):
            grads_ref[pl.ds(step * (CHUNKS * ROWS) + q, CHUNKS, stride=ROWS), :] = grads[q]
        return 0

    lax.fori_loop(0, steps, block, 0)

    gather_positions(CHUNKS - 1)
    wide = lax.broadcasted_iota(jnp.int32, (SUBS, LANES), 1)
    deep = lax.broadcasted_iota(jnp.int32, (SUBS, LANES), 0)
    lines = []
    for kind in range(2):
        spread = jnp.zeros((SUBS, LANES), jnp.float32)
        for c in range(3):
            for g in range(groups):
                at = slice(g * SUBS, (g + 1) * SUBS)
                if kind == 0:
                    line = jnp.sum(power_sum[c, at, :], axis=1, keepdims=True) / column(power_ref, c, g)
                else:
                    line = -pos_sum[at, c : c + 1] - 2.0 * column(pos_ref, c, g) * pos_sum[at, 4:5]
                spread = jnp.where(wide == deep + (g * SUBS + c * lights), line, spread)
        lines.append(jnp.sum(spread, axis=0, keepdims=True))
    first = lax.broadcasted_iota(jnp.int32, (1, LANES), 1)
    light_ref[0:1, :] = jnp.where(first == 3 * lights, whole(square_sum[...]), lines[0])
    light_ref[1:2, :] = lines[1]


def block_gradients(f, sums_ref):
    def summed(q):
        start = q * CHUNKS * SUM_PITCH
        parts = [sums_ref[pl.ds(start + i, CHUNKS, stride=SUM_PITCH), :] for i in range(SUBS)]
        while len(parts) > 1:
            parts = [a + b for a, b in zip(parts[::2], parts[1::2])]
        return parts[0]

    z = [summed(q) for q in range(SUMS)]
    vt, vb, vn = f["vt"], f["vb"], f["vn"]
    uv = z[SH] * f["rwv"] * f["rcv"]
    wv = -z[SH] * f["rwv"] * f["cv"] * f["vroot"]
    ax2, ay2, ix2, iy2 = f["ax2"], f["ay2"], f["ix2"], f["iy2"]
    pt, pb = uv * vt * ax2, uv * vb * ay2
    tau_x = (ay2 - 1.0) * z[V23] - z[TX] - (pb * vn + wv * vb)
    tau_y = (1.0 - ax2) * z[V13] + z[TY] + (pt * vn + wv * vt)
    tau_z = (iy2 * ax2 - 1.0) * z[V12] + (ay2 * ix2 - 1.0) * (z[U12] + pt * vb)
    turned = tau_x + f["inv"] * f["along"] * tau_z
    grads = [z[SD0 + c] * (0.5 / math.pi) for c in range(3)]
    grads += [z[SS0 + c] * f["lobe"] for c in range(3)]
    grads.append(z[V11] - (z[U11] + pt * vt) - z[SH])
    grads.append(z[V22] - (z[U22] + pb * vb) - z[SH])
    grads.append(f["kappa"] * (f["t_loc"][1] * tau_y - f["b_loc"][1] * turned))
    grads.append(f["kappa"] * (f["t_loc"][2] * tau_y - f["b_loc"][2] * turned))
    grads.append(tau_z * f["inv"] * f["inv"] * f["kappa"])
    grads.append((z[SF] - z[SH]) * f["inv_f1"])
    return grads


def local_gradients(observed, shadow, view_ids, points, frames, params, power, pos, cameras):
    lights, pixels = shadow.shape
    hbm = pl.BlockSpec(memory_space=pltpu.HBM)
    vmem = pl.BlockSpec(memory_space=pltpu.VMEM)
    return pl.pallas_call(
        gradient_kernel,
        in_specs=[pl.BlockSpec(memory_space=pltpu.SMEM)] + [hbm] * 6 + [vmem] * 2,
        out_specs=[vmem, vmem],
        out_shape=[
            jax.ShapeDtypeStruct((pixels // LANES * ROWS, LANES), jnp.float32),
            jax.ShapeDtypeStruct((2, LANES), jnp.float32),
        ],
        scratch_shapes=[
            pltpu.VMEM(observed.shape, observed.dtype),
            pltpu.VMEM(shadow.shape, jnp.int32),
            pltpu.VMEM((pixels // LANES, LANES), jnp.int32),
            pltpu.VMEM(points.shape, jnp.float32),
            pltpu.VMEM(frames.shape, jnp.float32),
            pltpu.VMEM(params.shape, jnp.float32),
            pltpu.VMEM((CHUNKS * RAW, LANES), jnp.float32),
            pltpu.VMEM((TABLE, CHUNKS, LANES), jnp.float32),
            pltpu.VMEM((SUMS * CHUNKS * SUM_PITCH, LANES), jnp.float32),
            pltpu.VMEM((lights, DEPTH), jnp.bfloat16),
            pltpu.VMEM((BLOCKS * CHUNKS * PITCH, LANES), jnp.float32),
            pltpu.VMEM((lights, BLOCKS * LANES), jnp.float32),
            pltpu.VMEM((lights, BLOCKS * LANES), jnp.float32),
            pltpu.VMEM((CHUNKS, DEPTH, BLOCKS * LANES), jnp.bfloat16),
            pltpu.VMEM((3, lights, LANES), jnp.float32),
            pltpu.VMEM((3, lights, LANES), jnp.float32),
            pltpu.VMEM((lights, 16), jnp.float32),
            pltpu.VMEM((SUBS, LANES), jnp.float32),
            pltpu.SemaphoreType.DMA((2, 6)),
        ],
        compiler_params=pltpu.CompilerParams(vmem_limit_bytes=16 << 20),
        name="pair_gradients",
    )(
        *(
            pltpu.with_memory_space_constraint(x, pltpu.HBM)
            for x in (
                cameras, observed, shadow, view_ids.reshape(pixels // LANES, LANES),
                points, frames, params, power, pos,
            )
        )
    )


def share_kernel(mark, arrived_ref, light_ref, share_ref, spread_ref):
    parts, rows = arrived_ref.shape[:2]
    squares = jnp.zeros((SUBS, LANES), jnp.float32)
    for at in range(0, rows, SUBS):
        pieces = [arrived_ref[i, at : at + SUBS, :] for i in range(parts)]
        while len(pieces) > 1:
            pieces = [a + b for a, b in zip(pieces[::2], pieces[1::2])]
        share_ref[at : at + SUBS, :] = pieces[0]
        squares = squares + pieces[0] * pieces[0]
    lane = lax.broadcasted_iota(jnp.int32, (2, LANES), 1)
    deep = lax.broadcasted_iota(jnp.int32, (2, LANES), 0)
    tile = jnp.where((lane == mark) & (deep == 1), whole(squares), light_ref[...])
    for i in range(spread_ref.shape[0]):
        spread_ref[i] = tile


def join_kernel(mark, share_ref, light_parts_ref, out_ref, light_ref):
    tile = light_parts_ref[0]
    for i in range(1, light_parts_ref.shape[0]):
        tile = tile + light_parts_ref[i]
    light_ref[...] = tile
    lane = lax.broadcasted_iota(jnp.int32, (2, LANES), 1)
    light_sq = whole(jnp.where(lane < mark, tile * tile, 0.0))
    deep = lax.broadcasted_iota(jnp.int32, (SUBS, LANES), 0)
    wide = lax.broadcasted_iota(jnp.int32, (SUBS, LANES), 1)
    tail = jnp.where(wide == 0, light_sq, 0.0)
    tail = jnp.where(wide == 1, tile[0:1, mark : mark + 1], tail)
    tail = jnp.where(wide == 2, tile[1:2, mark : mark + 1], tail)
    tail = jnp.where(deep == 0, tail, 0.0)
    rows = share_ref.shape[0]
    for at in range(0, rows, SUBS):
        value = share_ref[at : at + SUBS, :]
        for i in range(out_ref.shape[0]):
            out_ref[i, at : at + SUBS, :] = value
    for i in range(out_ref.shape[0]):
        out_ref[i, rows : rows + SUBS, :] = tail


def step_kernel(
    pixel_total, light_total, gathered_ref, light_ref, params_ref, power_ref, pos_ref,
    new_params_ref, new_power_ref, new_pos_ref, loss_ref,
):
    parts, rows = gathered_ref.shape[0], gathered_ref.shape[1] - SUBS
    tail = gathered_ref[0, rows : rows + SUBS, :]
    for i in range(1, parts):
        tail = tail + gathered_ref[i, rows : rows + SUBS, :]
    light_scale = STRIDE * lax.rsqrt(tail[0:1, 0:1] / (6 * light_total) + EPS)
    pixel_scale = STRIDE * lax.rsqrt(tail[0:1, 2:3] / (ROWS * pixel_total) + EPS)
    loss_ref[...] = tail[0:1, 1:2] / (3.0 * light_total * pixel_total)
    lights = power_ref.shape[1]
    for c in range(3):
        cut = slice(c * lights, (c + 1) * lights)
        new_power_ref[c : c + 1, :] = power_ref[c : c + 1, :] - light_ref[0:1, cut] * light_scale
        new_pos_ref[c : c + 1, :] = pos_ref[c : c + 1, :] - light_ref[1:2, cut] * light_scale
    chunks = rows // ROWS
    for i in range(parts):
        for k in range(chunks):
            cut = slice((i * chunks + k) * LANES, (i * chunks + k + 1) * LANES)
            grad = gathered_ref[i, k * ROWS : (k + 1) * ROWS, :]
            new_params_ref[:, cut] = params_ref[:, cut] - grad * pixel_scale


def broadcast_exchange(x, axes):
    return lax.all_to_all(x, axes, split_axis=0, concat_axis=0, tiled=True)


def shards(observed, shadow, view_ids, points, frames, params, power, pos, cameras):
    lights, pixels = shadow.shape
    px_size, lt_size = lax.axis_size(PX), lax.axis_size(LT)
    grads, light_tile = local_gradients(
        observed, shadow, view_ids, points, frames, params, power, pos, cameras
    )
    share_rows = grads.shape[0] // lt_size
    mark = 3 * lights
    small = pltpu.CompilerParams(vmem_limit_bytes=8 << 20)
    arrived = broadcast_exchange(grads.reshape(lt_size, share_rows, LANES), SHARES)
    share, spread = pl.pallas_call(
        functools.partial(share_kernel, mark),
        out_shape=(
            jax.ShapeDtypeStruct((share_rows, LANES), jnp.float32),
            jax.ShapeDtypeStruct((px_size, 2, LANES), jnp.float32),
        ),
        compiler_params=small,
        name="share_sum",
    )(arrived, light_tile)
    light_parts = broadcast_exchange(spread, PX)
    joined, own_lights = pl.pallas_call(
        functools.partial(join_kernel, mark),
        out_shape=(
            jax.ShapeDtypeStruct((lt_size, share_rows + SUBS, LANES), jnp.float32),
            jax.ShapeDtypeStruct((2, LANES), jnp.float32),
        ),
        compiler_params=small,
        name="join",
    )(share, light_parts)
    gathered = broadcast_exchange(joined, SHARES)
    new_params, new_power, new_pos, loss = pl.pallas_call(
        functools.partial(step_kernel, pixels * px_size, lights * lt_size),
        out_shape=(
            jax.ShapeDtypeStruct(params.shape, jnp.float32),
            jax.ShapeDtypeStruct(power.shape, jnp.float32),
            jax.ShapeDtypeStruct(pos.shape, jnp.float32),
            jax.ShapeDtypeStruct((1, 1), jnp.float32),
        ),
        compiler_params=small,
        name="step",
    )(gathered, own_lights, params, power, pos)
    return new_params, new_power, new_pos, loss.reshape(())


def solution(mesh):
    torus = Mesh(mesh.devices.reshape(4, 4, 2, 2, 2, 2, 2), PX + LT)
    placed = (
        P(None, LT, PX),
        P(LT, PX),
        P(PX),
        P(None, PX),
        P(None, PX),
        P(None, PX),
        P(None, LT),
        P(None, LT),
        P(),
    )
    return jax.shard_map(
        shards,
        mesh=torus,
        in_specs=placed,
        out_specs=(P(None, PX), P(None, LT), P(None, LT), P()),
        check_vma=False,
    )
```

```python
import functools
import math

import jax
import jax.numpy as jnp
from jax import lax
from jax.experimental import pallas as pl
from jax.experimental.pallas import tpu as pltpu
from jax.sharding import Mesh
from jax.sharding import PartitionSpec as P

PX = ("px_0", "px_1", "px_2")
LT = ("lt_0", "lt_1")
SHARES = ("lt_1", "lt_0")
BLOCK_SUMS = ("px_2", "px_0", "px_1")

SOFT = 0.01
EPS = 1e-06
STRIDE = 0.2
LANES = 128
SUBS = 8
ROWS = 12
BLOCK = 2048
CHUNKS = BLOCK // LANES
RAW = 25
DEPTH = 16
PITCH = 17
SUM_PITCH = 9
UNROLL = 16

(VT, VB, VN, AX2, AY2, IX2, IY2, F0, F1, K5, KD0, KD1, KD2, KS0, KS1, KS2) = range(16)
TABLE = 16
(SD0, SD1, SD2, SS0, SS1, SS2, SF, SH, V11, V22, V12, V13, V23, U11, U22, U12, TX, TY) = range(18)
SUMS = 18
LEFT = (0, 0, 1)
RIGHT = (0, 1, 0)
COMPS = 5
BLOCKS = 5
SQUARED = 3


def inner_three(first, second):
    return first[0] * second[0] + first[1] * second[1] + first[2] * second[2]


def pixel_frame(row, ids, camera_ref):
    azimuth = 2.0 * math.pi * row(17)
    ca, sa = jnp.cos(row(16)), jnp.sin(row(16))
    cz, sz = jnp.cos(azimuth), jnp.sin(azimuth)
    base_n = [sa * cz, sa * sz, ca]
    base_t = [ca * cz, ca * sz, -sa]
    base_b = [-sz, cz]
    u, v, spin = row(8), row(9), row(10)
    cs, sn = jnp.cos(spin), jnp.sin(spin)
    kappa = lax.rsqrt(1.0 + u * u + v * v)
    along = kappa * (u * cs + v * sn)
    inv = lax.rsqrt(1.0 - along * along)
    n_loc = [kappa, kappa * u, kappa * v]
    t_loc = [-along * n_loc[0] * inv, (cs - along * n_loc[1]) * inv, (sn - along * n_loc[2]) * inv]
    kb = kappa * inv
    b_loc = [kb * (u * sn - v * cs), -kb * sn, kb * cs]

    def world(loc):
        return [
            loc[0] * base_n[0] + loc[1] * base_t[0] + loc[2] * base_b[0],
            loc[0] * base_n[1] + loc[1] * base_t[1] + loc[2] * base_b[1],
            loc[0] * base_n[2] + loc[1] * base_t[2],
        ]

    tangent, bitangent, normal = world(t_loc), world(b_loc), world(n_loc)
    point = [row(12), row(13), row(14)]
    camera = [jnp.full_like(u, camera_ref[c, 0]) for c in range(3)]
    for view in range(1, camera_ref.shape[1]):
        chosen = ids == view
        camera = [jnp.where(chosen, camera_ref[c, view], camera[c]) for c in range(3)]
    toward = [camera[c] - point[c] for c in range(3)]
    scale = lax.rsqrt(inner_three(toward, toward))
    view_dir = [toward[c] * scale for c in range(3)]
    vt, vb, vn = (inner_three(view_dir, f) for f in (tangent, bitangent, normal))
    ax, ay = jnp.exp(row(6)), jnp.exp(row(7))
    ax2, ay2 = ax * ax, ay * ay
    ix2, iy2 = 1.0 / ax2, 1.0 / ay2
    vroot = lax.rsqrt(vn * vn + SOFT)
    cv = 0.5 * (vn + (vn * vn + SOFT) * vroot)
    wv2 = cv * cv + ax2 * vt * vt + ay2 * vb * vb
    rwv = lax.rsqrt(wv2)
    rcv = 1.0 / (cv + wv2 * rwv)
    return dict(
        tangent=tangent, bitangent=bitangent, normal=normal, point=point, view_dir=view_dir,
        vt=vt, vb=vb, vn=vn, ax=ax, ay=ay, ax2=ax2, ay2=ay2, ix2=ix2, iy2=iy2,
        inv_f1=1.0 / (1.0 - row(11)), lobe=16.0 * rcv / (math.pi * ax * ay), vroot=vroot, cv=cv, rwv=rwv, rcv=rcv, kappa=kappa, inv=inv, along=along,
        t_loc=t_loc, b_loc=b_loc,
    )


def pair_terms(px, offsets, pw, visible, measured):
    ot, ob, on, d2, ov = offsets
    r = lax.rsqrt(d2)
    id2 = r * r
    lt, lb, ln, lv = ot * r, ob * r, on * r, ov * r
    m = 0.5 * lv + 0.5
    a1, a2, a3 = lt + px(VT), lb + px(VB), ln + px(VN)
    b1, b2 = a1 * px(IX2), a2 * px(IY2)
    rq = lax.rsqrt(b1 * a1 + b2 * a2 + a3 * a3)
    rq = rq * rq
    rm = lax.rsqrt(m)
    om = 1.0 - m * rm
    om2 = om * om
    om4 = om2 * om2
    s5 = om4 * om
    fresnel = px(F0) + px(F1) * s5
    rf = lax.rsqrt(fresnel)
    lsq = ln * ln + SOFT
    rs = lax.rsqrt(lsq)
    cn = ln + lsq * rs
    xt, xb = lt * px(AX2), lb * px(AY2)
    wsq = cn * cn + (xt * lt + xb * lb)
    rw = lax.rsqrt(wsq)
    rc = lax.rsqrt(cn + wsq * rw)
    rc = rc * rc
    cni = cn * (id2 * visible)
    mq = m * rq
    gi = (mq * mq) * (rc * cni) * fresnel
    sums = [None] * SUMS
    power_terms = []
    squares = h = s = None
    for c in range(3):
        diffuse, glossy = pw[c] * cni, pw[c] * gi
        res = px(KD0 + c) * diffuse + px(KS0 + c) * glossy - measured[c]
        squares = res * res if c == 0 else squares + res * res
        sums[SD0 + c], sums[SS0 + c] = res * diffuse, res * glossy
        part = px(KS0 + c) * sums[SS0 + c]
        term = px(KD0 + c) * sums[SD0 + c] + part
        power_terms.append(term)
        h = part if c == 0 else h + part
        s = term if c == 0 else s + term
    squares = squares * visible
    x = (h * rf) * rf
    nm = rm * ((x * om4) * px(K5) - h * rm)
    hw = h * rw
    uu = hw * rc
    ww = rs * (s - hw * cn)
    v4 = (4.0 * h) * rq
    p1, p2 = uu * xt, uu * xb
    q1, q2, q3 = v4 * b1, v4 * b2, v4 * a3
    sums[SF] = x
    sums[SH] = h
    sums[V11], sums[V22], sums[V12] = q1 * a1, q2 * a2, q1 * a2
    sums[V13], sums[V23] = q1 * a3, q2 * a3
    sums[U11], sums[U22], sums[U12] = p1 * lt, p2 * lb, p1 * lb
    sums[TX], sums[TY] = p2 * ln + ww * lb, p1 * ln + ww * lt
    g1, g2, g3 = p1 + q1, p2 + q2, q3 - ww
    inner = (lt * g1 + lb * g2) + (ln * g3 + lv * nm)
    cots = [r * g1, r * g2, r * g3, id2 * (s - 0.5 * inner), r * nm]
    return sums, power_terms, squares, cots


def whole(x):
    return jnp.sum(jnp.sum(x, axis=0, keepdims=True), axis=1, keepdims=True)


def rounded(x):
    return x.astype(jnp.bfloat16).astype(jnp.float32)


def split_two(x):
    first = rounded(x)
    return [first, x - first]


def gradient_kernel(
    camera_ref, observed_hbm, shadow_hbm, ids_hbm, points_hbm, frames_hbm, params_hbm, power_ref, pos_ref,
    grads_ref, light_ref,
    observed_ref, shadow_ref, ids_ref, points_ref, frames_ref, params_ref,
    raw, table, sums_ref, left, right, offsets, spread_ref, frames_packed, power_wide, power_sum, pos_sum,
    square_sum, sems,
):
    lights, pixels = shadow_hbm.shape
    groups = lights // SUBS
    steps = pixels // BLOCK

    def copies(first, count):
        cut = slice(first * BLOCK, (first + count) * BLOCK)
        tile = slice(first * CHUNKS, (first + count) * CHUNKS)
        slot = min(first, 1)
        pairs = [
            (params_hbm.at[:, cut], params_ref.at[:, cut]),
            (points_hbm.at[:, cut], points_ref.at[:, cut]),
            (frames_hbm.at[:, cut], frames_ref.at[:, cut]),
            (ids_hbm.at[tile, :], ids_ref.at[tile, :]),
            (shadow_hbm.at[:, cut], shadow_ref.at[:, cut]),
            (observed_hbm.at[:, :, cut], observed_ref.at[:, :, cut]),
        ]
        return [pltpu.make_async_copy(a, b, sems.at[slot, i]) for i, (a, b) in enumerate(pairs)]

    stages = [copies(0, 1), copies(1, steps - 1)]
    for copy in stages[0]:
        copy.start()

    power_sum[...] = jnp.zeros_like(power_sum)
    pos_sum[...] = jnp.zeros_like(pos_sum)
    square_sum[...] = jnp.zeros_like(square_sum)
    spread_ref[...] = jnp.zeros_like(spread_ref)
    frames_packed[...] = jnp.zeros_like(frames_packed)
    right[...] = jnp.zeros_like(right)

    def piece(b):
        return slice(b * LANES, (b + 1) * LANES)

    def right_rows(b, q):
        return pl.ds(b * CHUNKS * PITCH + q, CHUNKS, stride=PITCH)

    for i, part in enumerate(RIGHT):
        if part == 0:
            right[right_rows(SQUARED, i * COMPS + 4), :] = jnp.ones((CHUNKS, LANES), jnp.float32)
    lane = lax.broadcasted_iota(jnp.int32, (SUBS, lights), 1)
    sub = lax.broadcasted_iota(jnp.int32, (SUBS, lights), 0)

    def column(source, c, g):
        picked = jnp.where(lane == sub + g * SUBS, source[c : c + 1, :], 0.0)
        return jnp.sum(picked, axis=1, keepdims=True)

    deep_lane = lax.broadcasted_iota(jnp.int32, (SUBS, DEPTH), 1)
    one = jnp.ones((SUBS, DEPTH), jnp.float32)
    zero = jnp.zeros((SUBS, DEPTH), jnp.float32)
    tiles = []
    for g in range(groups):
        at = slice(g * SUBS, (g + 1) * SUBS)
        for c in range(3):
            power_wide[c, at, :] = jnp.broadcast_to(column(power_ref, c, g), (SUBS, LANES))
        pos = [jnp.broadcast_to(column(pos_ref, c, g), (SUBS, DEPTH)) for c in range(3)]
        splits = [split_two(x) for x in pos] + [[one, zero], split_two(inner_three(pos, pos))]
        tile = zero
        for i, part in enumerate(LEFT):
            for c in range(COMPS):
                tile = jnp.where(deep_lane == i * COMPS + c, splits[c][part], tile)
        tiles.append(tile)
    left[...] = jnp.concatenate(tiles, axis=0).astype(jnp.bfloat16)

    def product(k):
        frame = jnp.concatenate(
            [right[pl.ds((b * CHUNKS + k) * PITCH, DEPTH), :] for b in range(BLOCKS)], axis=1
        ).astype(jnp.bfloat16)
        frames_packed[k] = frame
        return jnp.dot(left[...], frame, preferred_element_type=jnp.float32)

    def gather_positions(k):
        pos_sum[...] += lax.dot_general(
            spread_ref[...].astype(jnp.bfloat16), frames_packed[k], (((1,), (1,)), ((), ())),
            preferred_element_type=jnp.float32,
        )

    for copy in stages[0][:4]:
        copy.wait()
    for stage in stages[1:]:
        for copy in stage:
            copy.start()

    def arrive(step, first, some):
        for i, stage in enumerate(stages[first:], first):

            @pl.when(step == i)
            def _(stage=stage):
                for copy in stage[some]:
                    copy.wait()

    def block(step, _):
        arrive(step, 1, slice(0, 4))

        base = pl.multiple_of(step * BLOCK, BLOCK)
        for k in range(CHUNKS):
            cut = pl.ds(pl.multiple_of(base + k * LANES, LANES), LANES)
            raw[k * RAW : k * RAW + 12, :] = params_ref[:, cut]
            raw[k * RAW + 12 : k * RAW + 15, :] = points_ref[:, cut]
            raw[k * RAW + 16 : k * RAW + 18, :] = frames_ref[:, cut]

        def row(q):
            return raw[pl.ds(q, CHUNKS, stride=RAW), :]

        ids = ids_ref[pl.ds(pl.multiple_of(step * CHUNKS, CHUNKS), CHUNKS), :]
        f = pixel_frame(row, ids, camera_ref)
        point = f["point"]
        columns = [
            [*vec, -inner_three(point, vec)] for vec in (f["tangent"], f["bitangent"], f["normal"])
        ]
        columns.append([-2.0 * point[c] for c in range(3)] + [inner_three(point, point)])
        columns.append([*f["view_dir"], -inner_three(point, f["view_dir"])])
        for b, column_of in enumerate(columns):
            for c, value in enumerate(column_of):
                parts = [value, value - rounded(value)]
                for i, part in enumerate(RIGHT):
                    right[right_rows(b, i * COMPS + c), :] = parts[part]
        entries = {
            AX2: 4.0 * f["ax2"], AY2: 4.0 * f["ay2"], IX2: f["ix2"], IY2: f["iy2"],
            VT: f["vt"], VB: f["vb"], VN: f["vn"],
            F0: row(11), F1: 1.0 - row(11), K5: 1.25 - 1.25 * row(11),
        }
        for c in range(3):
            entries[KD0 + c] = row(c) * (0.5 / math.pi)
            entries[KS0 + c] = row(3 + c) * f["lobe"]
        for q, value in entries.items():
            table[q] = value
        offsets[...] = product(0)

        def chunk(k, _):
            cut = pl.ds(pl.multiple_of(base + k * LANES, LANES), LANES)

            def px(q):
                return jnp.broadcast_to(table[q, pl.ds(k, 1), :], (SUBS, LANES))

            following = product(jnp.minimum(k + 1, CHUNKS - 1))
            gather_positions(jnp.where(k == 0, CHUNKS, k) - 1)
            total = squares = None
            for g in range(groups):
                at = slice(g * SUBS, (g + 1) * SUBS)
                visible = shadow_ref[at, cut].astype(jnp.float32)
                measured = [observed_ref[c, at, cut].astype(jnp.float32) for c in range(3)]
                sums, power_terms, square, cot = pair_terms(
                    px, [offsets[at, piece(b)] for b in range(BLOCKS)],
                    [power_wide[c, at, :] for c in range(3)], visible, measured,
                )
                total = sums if total is None else [a + b for a, b in zip(total, sums)]
                squares = square if squares is None else squares + square
                for b in range(BLOCKS):
                    spread_ref[at, piece(b)] = cot[b]
                for c in range(3):
                    power_sum[c, at, :] += power_terms[c]
            square_sum[...] += squares
            for q in range(SUMS):
                sums_ref[pl.ds((q * CHUNKS + k) * SUM_PITCH, SUBS), :] = total[q]
            offsets[...] = following
            return 0

        arrive(step, 0, slice(4, 6))
        lax.fori_loop(0, CHUNKS, chunk, 0, unroll=UNROLL)
        grads = block_gradients(f, sums_ref)
        for q in range(ROWS):
            grads_ref[pl.ds(step * (CHUNKS * ROWS) + q, CHUNKS, stride=ROWS), :] = grads[q]
        return 0

    lax.fori_loop(0, steps, block, 0)

    gather_positions(CHUNKS - 1)
    wide = lax.broadcasted_iota(jnp.int32, (SUBS, LANES), 1)
    deep = lax.broadcasted_iota(jnp.int32, (SUBS, LANES), 0)
    lines = []
    for kind in range(2):
        spread = jnp.zeros((SUBS, LANES), jnp.float32)
        for c in range(3):
            for g in range(groups):
                at = slice(g * SUBS, (g + 1) * SUBS)
                if kind == 0:
                    line = jnp.sum(power_sum[c, at, :], axis=1, keepdims=True) / column(power_ref, c, g)
                else:
                    line = -pos_sum[at, c : c + 1] - 2.0 * column(pos_ref, c, g) * pos_sum[at, 4:5]
                spread = jnp.where(wide == deep + (g * SUBS + c * lights), line, spread)
        lines.append(jnp.sum(spread, axis=0, keepdims=True))
    first = lax.broadcasted_iota(jnp.int32, (1, LANES), 1)
    light_ref[0:1, :] = jnp.where(first == 3 * lights, whole(square_sum[...]), lines[0])
    light_ref[1:2, :] = lines[1]


def block_gradients(f, sums_ref):
    def summed(q):
        start = q * CHUNKS * SUM_PITCH
        parts = [sums_ref[pl.ds(start + i, CHUNKS, stride=SUM_PITCH), :] for i in range(SUBS)]
        while len(parts) > 1:
            parts = [a + b for a, b in zip(parts[::2], parts[1::2])]
        return parts[0]

    z = [summed(q) for q in range(SUMS)]
    vt, vb, vn = f["vt"], f["vb"], f["vn"]
    uv = z[SH] * f["rwv"] * f["rcv"]
    wv = -z[SH] * f["rwv"] * f["cv"] * f["vroot"]
    ax2, ay2, ix2, iy2 = f["ax2"], f["ay2"], f["ix2"], f["iy2"]
    pt, pb = uv * vt * ax2, uv * vb * ay2
    tau_x = (ay2 - 1.0) * z[V23] - z[TX] - (pb * vn + wv * vb)
    tau_y = (1.0 - ax2) * z[V13] + z[TY] + (pt * vn + wv * vt)
    tau_z = (iy2 * ax2 - 1.0) * z[V12] + (ay2 * ix2 - 1.0) * (z[U12] + pt * vb)
    turned = tau_x + f["inv"] * f["along"] * tau_z
    grads = [z[SD0 + c] * (0.5 / math.pi) for c in range(3)]
    grads += [z[SS0 + c] * f["lobe"] for c in range(3)]
    grads.append(z[V11] - (z[U11] + pt * vt) - z[SH])
    grads.append(z[V22] - (z[U22] + pb * vb) - z[SH])
    grads.append(f["kappa"] * (f["t_loc"][1] * tau_y - f["b_loc"][1] * turned))
    grads.append(f["kappa"] * (f["t_loc"][2] * tau_y - f["b_loc"][2] * turned))
    grads.append(tau_z * f["inv"] * f["inv"] * f["kappa"])
    grads.append((z[SF] - z[SH]) * f["inv_f1"])
    return grads


def local_gradients(observed, shadow, view_ids, points, frames, params, power, pos, cameras):
    lights, pixels = shadow.shape
    hbm = pl.BlockSpec(memory_space=pltpu.HBM)
    vmem = pl.BlockSpec(memory_space=pltpu.VMEM)
    return pl.pallas_call(
        gradient_kernel,
        in_specs=[pl.BlockSpec(memory_space=pltpu.SMEM)] + [hbm] * 6 + [vmem] * 2,
        out_specs=[vmem, vmem],
        out_shape=[
            jax.ShapeDtypeStruct((pixels // LANES * ROWS, LANES), jnp.float32),
            jax.ShapeDtypeStruct((2, LANES), jnp.float32),
        ],
        scratch_shapes=[
            pltpu.VMEM(observed.shape, observed.dtype),
            pltpu.VMEM(shadow.shape, jnp.int32),
            pltpu.VMEM((pixels // LANES, LANES), jnp.int32),
            pltpu.VMEM(points.shape, jnp.float32),
            pltpu.VMEM(frames.shape, jnp.float32),
            pltpu.VMEM(params.shape, jnp.float32),
            pltpu.VMEM((CHUNKS * RAW, LANES), jnp.float32),
            pltpu.VMEM((TABLE, CHUNKS, LANES), jnp.float32),
            pltpu.VMEM((SUMS * CHUNKS * SUM_PITCH, LANES), jnp.float32),
            pltpu.VMEM((lights, DEPTH), jnp.bfloat16),
            pltpu.VMEM((BLOCKS * CHUNKS * PITCH, LANES), jnp.float32),
            pltpu.VMEM((lights, BLOCKS * LANES), jnp.float32),
            pltpu.VMEM((lights, BLOCKS * LANES), jnp.float32),
            pltpu.VMEM((CHUNKS, DEPTH, BLOCKS * LANES), jnp.bfloat16),
            pltpu.VMEM((3, lights, LANES), jnp.float32),
            pltpu.VMEM((3, lights, LANES), jnp.float32),
            pltpu.VMEM((lights, 16), jnp.float32),
            pltpu.VMEM((SUBS, LANES), jnp.float32),
            pltpu.SemaphoreType.DMA((2, 6)),
        ],
        compiler_params=pltpu.CompilerParams(vmem_limit_bytes=16 << 20),
        name="pair_gradients",
    )(
        *(
            pltpu.with_memory_space_constraint(x, pltpu.HBM)
            for x in (
                cameras, observed, shadow, view_ids.reshape(pixels // LANES, LANES),
                points, frames, params, power, pos,
            )
        )
    )


def share_kernel(mark, arrived_ref, light_ref, share_ref, spread_ref):
    parts, rows = arrived_ref.shape[:2]
    squares = jnp.zeros((SUBS, LANES), jnp.float32)
    for at in range(0, rows, SUBS):
        pieces = [arrived_ref[i, at : at + SUBS, :] for i in range(parts)]
        while len(pieces) > 1:
            pieces = [a + b for a, b in zip(pieces[::2], pieces[1::2])]
        share_ref[at : at + SUBS, :] = pieces[0]
        squares = squares + pieces[0] * pieces[0]
    lane = lax.broadcasted_iota(jnp.int32, (2, LANES), 1)
    deep = lax.broadcasted_iota(jnp.int32, (2, LANES), 0)
    tile = jnp.where((lane == mark) & (deep == 1), whole(squares), light_ref[...])
    for i in range(spread_ref.shape[0]):
        spread_ref[i] = tile


def join_kernel(mark, share_ref, light_parts_ref, out_ref, light_ref):
    tile = light_parts_ref[0]
    for i in range(1, light_parts_ref.shape[0]):
        tile = tile + light_parts_ref[i]
    light_ref[...] = tile
    lane = lax.broadcasted_iota(jnp.int32, (2, LANES), 1)
    light_sq = whole(jnp.where(lane < mark, tile * tile, 0.0))
    deep = lax.broadcasted_iota(jnp.int32, (SUBS, LANES), 0)
    wide = lax.broadcasted_iota(jnp.int32, (SUBS, LANES), 1)
    tail = jnp.where(wide == 0, light_sq, 0.0)
    tail = jnp.where(wide == 1, tile[0:1, mark : mark + 1], tail)
    tail = jnp.where(wide == 2, tile[1:2, mark : mark + 1], tail)
    tail = jnp.where(deep == 0, tail, 0.0)
    rows = share_ref.shape[0]
    for at in range(0, rows, SUBS):
        value = share_ref[at : at + SUBS, :]
        for i in range(out_ref.shape[0]):
            out_ref[i, at : at + SUBS, :] = value
    for i in range(out_ref.shape[0]):
        out_ref[i, rows : rows + SUBS, :] = tail


def step_kernel(
    pixel_total, light_total, gathered_ref, light_ref, params_ref, power_ref, pos_ref,
    new_params_ref, new_power_ref, new_pos_ref, loss_ref,
):
    parts, rows = gathered_ref.shape[0], gathered_ref.shape[1] - SUBS
    tail = gathered_ref[0, rows : rows + SUBS, :]
    for i in range(1, parts):
        tail = tail + gathered_ref[i, rows : rows + SUBS, :]
    light_scale = STRIDE * lax.rsqrt(tail[0:1, 0:1] / (6 * light_total) + EPS)
    pixel_scale = STRIDE * lax.rsqrt(tail[0:1, 2:3] / (ROWS * pixel_total) + EPS)
    loss_ref[...] = tail[0:1, 1:2] / (3.0 * light_total * pixel_total)
    lights = power_ref.shape[1]
    for c in range(3):
        cut = slice(c * lights, (c + 1) * lights)
        new_power_ref[c : c + 1, :] = power_ref[c : c + 1, :] - light_ref[0:1, cut] * light_scale
        new_pos_ref[c : c + 1, :] = pos_ref[c : c + 1, :] - light_ref[1:2, cut] * light_scale
    chunks = rows // ROWS
    for i in range(parts):
        for k in range(chunks):
            cut = slice((i * chunks + k) * LANES, (i * chunks + k + 1) * LANES)
            grad = gathered_ref[i, k * ROWS : (k + 1) * ROWS, :]
            new_params_ref[:, cut] = params_ref[:, cut] - grad * pixel_scale


def broadcast_exchange(x, axes):
    return lax.all_to_all(x, axes, split_axis=0, concat_axis=0, tiled=True)


def shards(observed, shadow, view_ids, points, frames, params, power, pos, cameras):
    lights, pixels = shadow.shape
    px_size, lt_size = lax.axis_size(PX), lax.axis_size(LT)
    grads, light_tile = local_gradients(
        observed, shadow, view_ids, points, frames, params, power, pos, cameras
    )
    share_rows = grads.shape[0] // lt_size
    mark = 3 * lights
    small = pltpu.CompilerParams(vmem_limit_bytes=8 << 20)
    arrived = broadcast_exchange(grads.reshape(lt_size, share_rows, LANES), SHARES)
    share, spread = pl.pallas_call(
        functools.partial(share_kernel, mark),
        out_shape=(
            jax.ShapeDtypeStruct((share_rows, LANES), jnp.float32),
            jax.ShapeDtypeStruct((px_size, 2, LANES), jnp.float32),
        ),
        compiler_params=small,
        name="share_sum",
    )(arrived, light_tile)
    light_parts = broadcast_exchange(spread, BLOCK_SUMS)
    joined, own_lights = pl.pallas_call(
        functools.partial(join_kernel, mark),
        out_shape=(
            jax.ShapeDtypeStruct((lt_size, share_rows + SUBS, LANES), jnp.float32),
            jax.ShapeDtypeStruct((2, LANES), jnp.float32),
        ),
        compiler_params=small,
        name="join",
    )(share, light_parts)
    gathered = broadcast_exchange(joined, SHARES)
    new_params, new_power, new_pos, loss = pl.pallas_call(
        functools.partial(step_kernel, pixels * px_size, lights * lt_size),
        out_shape=(
            jax.ShapeDtypeStruct(params.shape, jnp.float32),
            jax.ShapeDtypeStruct(power.shape, jnp.float32),
            jax.ShapeDtypeStruct(pos.shape, jnp.float32),
            jax.ShapeDtypeStruct((1, 1), jnp.float32),
        ),
        compiler_params=small,
        name="step",
    )(gathered, own_lights, params, power, pos)
    return new_params, new_power, new_pos, loss.reshape(())


def solution(mesh):
    torus = Mesh(mesh.devices.reshape(4, 4, 2, 8, 2), PX + LT)
    placed = (
        P(None, LT, PX),
        P(LT, PX),
        P(PX),
        P(None, PX),
        P(None, PX),
        P(None, PX),
        P(None, LT),
        P(None, LT),
        P(),
    )
    return jax.shard_map(
        shards,
        mesh=torus,
        in_specs=placed,
        out_specs=(P(None, PX), P(None, LT), P(None, LT), P()),
        check_vma=False,
    )
```

```python
import functools
import math

import jax
import jax.numpy as jnp
from jax import lax
from jax.experimental import pallas as pl
from jax.experimental.pallas import tpu as pltpu
from jax.sharding import Mesh
from jax.sharding import PartitionSpec as P

PX = ("px_0", "px_1", "px_2")
LT = ("lt_0", "lt_1")
SHARES = ("lt_1", "lt_0")
BLOCK_SUMS = ("px_2", "px_1", "px_0")

SOFT = 0.01
EPS = 1e-06
STRIDE = 0.2
LANES = 128
SUBS = 8
ROWS = 12
BLOCK = 2048
CHUNKS = BLOCK // LANES
RAW = 25
DEPTH = 16
PITCH = 17
SUM_PITCH = 9
UNROLL = 16

(VT, VB, VN, AX2, AY2, IX2, IY2, F0, F1, K5, KD0, KD1, KD2, KS0, KS1, KS2) = range(16)
TABLE = 16
(SD0, SD1, SD2, SS0, SS1, SS2, SF, SH, V11, V22, V12, V13, V23, U11, U22, U12, TX, TY) = range(18)
SUMS = 18
LEFT = (0, 0, 1)
RIGHT = (0, 1, 0)
COMPS = 5
BLOCKS = 5
SQUARED = 3


def inner_three(first, second):
    return first[0] * second[0] + first[1] * second[1] + first[2] * second[2]


def pixel_frame(row, ids, camera_ref):
    azimuth = 2.0 * math.pi * row(17)
    ca, sa = jnp.cos(row(16)), jnp.sin(row(16))
    cz, sz = jnp.cos(azimuth), jnp.sin(azimuth)
    base_n = [sa * cz, sa * sz, ca]
    base_t = [ca * cz, ca * sz, -sa]
    base_b = [-sz, cz]
    u, v, spin = row(8), row(9), row(10)
    cs, sn = jnp.cos(spin), jnp.sin(spin)
    kappa = lax.rsqrt(1.0 + u * u + v * v)
    along = kappa * (u * cs + v * sn)
    inv = lax.rsqrt(1.0 - along * along)
    n_loc = [kappa, kappa * u, kappa * v]
    t_loc = [-along * n_loc[0] * inv, (cs - along * n_loc[1]) * inv, (sn - along * n_loc[2]) * inv]
    kb = kappa * inv
    b_loc = [kb * (u * sn - v * cs), -kb * sn, kb * cs]

    def world(loc):
        return [
            loc[0] * base_n[0] + loc[1] * base_t[0] + loc[2] * base_b[0],
            loc[0] * base_n[1] + loc[1] * base_t[1] + loc[2] * base_b[1],
            loc[0] * base_n[2] + loc[1] * base_t[2],
        ]

    tangent, bitangent, normal = world(t_loc), world(b_loc), world(n_loc)
    point = [row(12), row(13), row(14)]
    camera = [jnp.full_like(u, camera_ref[c, 0]) for c in range(3)]
    for view in range(1, camera_ref.shape[1]):
        chosen = ids == view
        camera = [jnp.where(chosen, camera_ref[c, view], camera[c]) for c in range(3)]
    toward = [camera[c] - point[c] for c in range(3)]
    scale = lax.rsqrt(inner_three(toward, toward))
    view_dir = [toward[c] * scale for c in range(3)]
    vt, vb, vn = (inner_three(view_dir, f) for f in (tangent, bitangent, normal))
    ax, ay = jnp.exp(row(6)), jnp.exp(row(7))
    ax2, ay2 = ax * ax, ay * ay
    ix2, iy2 = 1.0 / ax2, 1.0 / ay2
    vroot = lax.rsqrt(vn * vn + SOFT)
    cv = 0.5 * (vn + (vn * vn + SOFT) * vroot)
    wv2 = cv * cv + ax2 * vt * vt + ay2 * vb * vb
    rwv = lax.rsqrt(wv2)
    rcv = 1.0 / (cv + wv2 * rwv)
    return dict(
        tangent=tangent, bitangent=bitangent, normal=normal, point=point, view_dir=view_dir,
        vt=vt, vb=vb, vn=vn, ax=ax, ay=ay, ax2=ax2, ay2=ay2, ix2=ix2, iy2=iy2,
        inv_f1=1.0 / (1.0 - row(11)), lobe=16.0 * rcv / (math.pi * ax * ay), vroot=vroot, cv=cv, rwv=rwv, rcv=rcv, kappa=kappa, inv=inv, along=along,
        t_loc=t_loc, b_loc=b_loc,
    )


def pair_terms(px, offsets, pw, visible, measured):
    ot, ob, on, d2, ov = offsets
    r = lax.rsqrt(d2)
    id2 = r * r
    lt, lb, ln, lv = ot * r, ob * r, on * r, ov * r
    m = 0.5 * lv + 0.5
    a1, a2, a3 = lt + px(VT), lb + px(VB), ln + px(VN)
    b1, b2 = a1 * px(IX2), a2 * px(IY2)
    rq = lax.rsqrt(b1 * a1 + b2 * a2 + a3 * a3)
    rq = rq * rq
    rm = lax.rsqrt(m)
    om = 1.0 - m * rm
    om2 = om * om
    om4 = om2 * om2
    s5 = om4 * om
    fresnel = px(F0) + px(F1) * s5
    rf = lax.rsqrt(fresnel)
    lsq = ln * ln + SOFT
    rs = lax.rsqrt(lsq)
    cn = ln + lsq * rs
    xt, xb = lt * px(AX2), lb * px(AY2)
    wsq = cn * cn + (xt * lt + xb * lb)
    rw = lax.rsqrt(wsq)
    rc = lax.rsqrt(cn + wsq * rw)
    rc = rc * rc
    cni = cn * (id2 * visible)
    mq = m * rq
    gi = (mq * mq) * (rc * cni) * fresnel
    sums = [None] * SUMS
    power_terms = []
    squares = h = s = None
    for c in range(3):
        diffuse, glossy = pw[c] * cni, pw[c] * gi
        res = px(KD0 + c) * diffuse + px(KS0 + c) * glossy - measured[c]
        squares = res * res if c == 0 else squares + res * res
        sums[SD0 + c], sums[SS0 + c] = res * diffuse, res * glossy
        part = px(KS0 + c) * sums[SS0 + c]
        term = px(KD0 + c) * sums[SD0 + c] + part
        power_terms.append(term)
        h = part if c == 0 else h + part
        s = term if c == 0 else s + term
    squares = squares * visible
    x = (h * rf) * rf
    nm = rm * ((x * om4) * px(K5) - h * rm)
    hw = h * rw
    uu = hw * rc
    ww = rs * (s - hw * cn)
    v4 = (4.0 * h) * rq
    p1, p2 = uu * xt, uu * xb
    q1, q2, q3 = v4 * b1, v4 * b2, v4 * a3
    sums[SF] = x
    sums[SH] = h
    sums[V11], sums[V22], sums[V12] = q1 * a1, q2 * a2, q1 * a2
    sums[V13], sums[V23] = q1 * a3, q2 * a3
    sums[U11], sums[U22], sums[U12] = p1 * lt, p2 * lb, p1 * lb
    sums[TX], sums[TY] = p2 * ln + ww * lb, p1 * ln + ww * lt
    g1, g2, g3 = p1 + q1, p2 + q2, q3 - ww
    inner = (lt * g1 + lb * g2) + (ln * g3 + lv * nm)
    cots = [r * g1, r * g2, r * g3, id2 * (s - 0.5 * inner), r * nm]
    return sums, power_terms, squares, cots


def whole(x):
    return jnp.sum(jnp.sum(x, axis=0, keepdims=True), axis=1, keepdims=True)


def rounded(x):
    return x.astype(jnp.bfloat16).astype(jnp.float32)


def split_two(x):
    first = rounded(x)
    return [first, x - first]


def gradient_kernel(
    camera_ref, observed_hbm, shadow_hbm, ids_hbm, points_hbm, frames_hbm, params_hbm, power_ref, pos_ref,
    grads_ref, light_ref,
    observed_ref, shadow_ref, ids_ref, points_ref, frames_ref, params_ref,
    raw, table, sums_ref, left, right, offsets, spread_ref, frames_packed, power_wide, power_sum, pos_sum,
    square_sum, sems,
):
    lights, pixels = shadow_hbm.shape
    groups = lights // SUBS
    steps = pixels // BLOCK

    def copies(first, count):
        cut = slice(first * BLOCK, (first + count) * BLOCK)
        tile = slice(first * CHUNKS, (first + count) * CHUNKS)
        slot = min(first, 1)
        pairs = [
            (params_hbm.at[:, cut], params_ref.at[:, cut]),
            (points_hbm.at[:, cut], points_ref.at[:, cut]),
            (frames_hbm.at[:, cut], frames_ref.at[:, cut]),
            (ids_hbm.at[tile, :], ids_ref.at[tile, :]),
            (shadow_hbm.at[:, cut], shadow_ref.at[:, cut]),
            (observed_hbm.at[:, :, cut], observed_ref.at[:, :, cut]),
        ]
        return [pltpu.make_async_copy(a, b, sems.at[slot, i]) for i, (a, b) in enumerate(pairs)]

    stages = [copies(0, 1), copies(1, steps - 1)]
    for copy in stages[0]:
        copy.start()

    power_sum[...] = jnp.zeros_like(power_sum)
    pos_sum[...] = jnp.zeros_like(pos_sum)
    square_sum[...] = jnp.zeros_like(square_sum)
    spread_ref[...] = jnp.zeros_like(spread_ref)
    frames_packed[...] = jnp.zeros_like(frames_packed)
    right[...] = jnp.zeros_like(right)

    def piece(b):
        return slice(b * LANES, (b + 1) * LANES)

    def right_rows(b, q):
        return pl.ds(b * CHUNKS * PITCH + q, CHUNKS, stride=PITCH)

    for i, part in enumerate(RIGHT):
        if part == 0:
            right[right_rows(SQUARED, i * COMPS + 4), :] = jnp.ones((CHUNKS, LANES), jnp.float32)
    lane = lax.broadcasted_iota(jnp.int32, (SUBS, lights), 1)
    sub = lax.broadcasted_iota(jnp.int32, (SUBS, lights), 0)

    def column(source, c, g):
        picked = jnp.where(lane == sub + g * SUBS, source[c : c + 1, :], 0.0)
        return jnp.sum(picked, axis=1, keepdims=True)

    deep_lane = lax.broadcasted_iota(jnp.int32, (SUBS, DEPTH), 1)
    one = jnp.ones((SUBS, DEPTH), jnp.float32)
    zero = jnp.zeros((SUBS, DEPTH), jnp.float32)
    tiles = []
    for g in range(groups):
        at = slice(g * SUBS, (g + 1) * SUBS)
        for c in range(3):
            power_wide[c, at, :] = jnp.broadcast_to(column(power_ref, c, g), (SUBS, LANES))
        pos = [jnp.broadcast_to(column(pos_ref, c, g), (SUBS, DEPTH)) for c in range(3)]
        splits = [split_two(x) for x in pos] + [[one, zero], split_two(inner_three(pos, pos))]
        tile = zero
        for i, part in enumerate(LEFT):
            for c in range(COMPS):
                tile = jnp.where(deep_lane == i * COMPS + c, splits[c][part], tile)
        tiles.append(tile)
    left[...] = jnp.concatenate(tiles, axis=0).astype(jnp.bfloat16)

    def product(k):
        frame = jnp.concatenate(
            [right[pl.ds((b * CHUNKS + k) * PITCH, DEPTH), :] for b in range(BLOCKS)], axis=1
        ).astype(jnp.bfloat16)
        frames_packed[k] = frame
        return jnp.dot(left[...], frame, preferred_element_type=jnp.float32)

    def gather_positions(k):
        pos_sum[...] += lax.dot_general(
            spread_ref[...].astype(jnp.bfloat16), frames_packed[k], (((1,), (1,)), ((), ())),
            preferred_element_type=jnp.float32,
        )

    for copy in stages[0][:4]:
        copy.wait()
    for stage in stages[1:]:
        for copy in stage:
            copy.start()

    def arrive(step, first, some):
        for i, stage in enumerate(stages[first:], first):

            @pl.when(step == i)
            def _(stage=stage):
                for copy in stage[some]:
                    copy.wait()

    def block(step, _):
        arrive(step, 1, slice(0, 4))

        base = pl.multiple_of(step * BLOCK, BLOCK)
        for k in range(CHUNKS):
            cut = pl.ds(pl.multiple_of(base + k * LANES, LANES), LANES)
            raw[k * RAW : k * RAW + 12, :] = params_ref[:, cut]
            raw[k * RAW + 12 : k * RAW + 15, :] = points_ref[:, cut]
            raw[k * RAW + 16 : k * RAW + 18, :] = frames_ref[:, cut]

        def row(q):
            return raw[pl.ds(q, CHUNKS, stride=RAW), :]

        ids = ids_ref[pl.ds(pl.multiple_of(step * CHUNKS, CHUNKS), CHUNKS), :]
        f = pixel_frame(row, ids, camera_ref)
        point = f["point"]
        columns = [
            [*vec, -inner_three(point, vec)] for vec in (f["tangent"], f["bitangent"], f["normal"])
        ]
        columns.append([-2.0 * point[c] for c in range(3)] + [inner_three(point, point)])
        columns.append([*f["view_dir"], -inner_three(point, f["view_dir"])])
        for b, column_of in enumerate(columns):
            for c, value in enumerate(column_of):
                parts = [value, value - rounded(value)]
                for i, part in enumerate(RIGHT):
                    right[right_rows(b, i * COMPS + c), :] = parts[part]
        entries = {
            AX2: 4.0 * f["ax2"], AY2: 4.0 * f["ay2"], IX2: f["ix2"], IY2: f["iy2"],
            VT: f["vt"], VB: f["vb"], VN: f["vn"],
            F0: row(11), F1: 1.0 - row(11), K5: 1.25 - 1.25 * row(11),
        }
        for c in range(3):
            entries[KD0 + c] = row(c) * (0.5 / math.pi)
            entries[KS0 + c] = row(3 + c) * f["lobe"]
        for q, value in entries.items():
            table[q] = value
        offsets[...] = product(0)

        def chunk(k, _):
            cut = pl.ds(pl.multiple_of(base + k * LANES, LANES), LANES)

            def px(q):
                return jnp.broadcast_to(table[q, pl.ds(k, 1), :], (SUBS, LANES))

            following = product(jnp.minimum(k + 1, CHUNKS - 1))
            gather_positions(jnp.where(k == 0, CHUNKS, k) - 1)
            total = squares = None
            for g in range(groups):
                at = slice(g * SUBS, (g + 1) * SUBS)
                visible = shadow_ref[at, cut].astype(jnp.float32)
                measured = [observed_ref[c, at, cut].astype(jnp.float32) for c in range(3)]
                sums, power_terms, square, cot = pair_terms(
                    px, [offsets[at, piece(b)] for b in range(BLOCKS)],
                    [power_wide[c, at, :] for c in range(3)], visible, measured,
                )
                total = sums if total is None else [a + b for a, b in zip(total, sums)]
                squares = square if squares is None else squares + square
                for b in range(BLOCKS):
                    spread_ref[at, piece(b)] = cot[b]
                for c in range(3):
                    power_sum[c, at, :] += power_terms[c]
            square_sum[...] += squares
            for q in range(SUMS):
                sums_ref[pl.ds((q * CHUNKS + k) * SUM_PITCH, SUBS), :] = total[q]
            offsets[...] = following
            return 0

        arrive(step, 0, slice(4, 6))
        lax.fori_loop(0, CHUNKS, chunk, 0, unroll=UNROLL)
        grads = block_gradients(f, sums_ref)
        for q in range(ROWS):
            grads_ref[pl.ds(step * (CHUNKS * ROWS) + q, CHUNKS, stride=ROWS), :] = grads[q]
        return 0

    lax.fori_loop(0, steps, block, 0)

    gather_positions(CHUNKS - 1)
    wide = lax.broadcasted_iota(jnp.int32, (SUBS, LANES), 1)
    deep = lax.broadcasted_iota(jnp.int32, (SUBS, LANES), 0)
    lines = []
    for kind in range(2):
        spread = jnp.zeros((SUBS, LANES), jnp.float32)
        for c in range(3):
            for g in range(groups):
                at = slice(g * SUBS, (g + 1) * SUBS)
                if kind == 0:
                    line = jnp.sum(power_sum[c, at, :], axis=1, keepdims=True) / column(power_ref, c, g)
                else:
                    line = -pos_sum[at, c : c + 1] - 2.0 * column(pos_ref, c, g) * pos_sum[at, 4:5]
                spread = jnp.where(wide == deep + (g * SUBS + c * lights), line, spread)
        lines.append(jnp.sum(spread, axis=0, keepdims=True))
    first = lax.broadcasted_iota(jnp.int32, (1, LANES), 1)
    light_ref[0:1, :] = jnp.where(first == 3 * lights, whole(square_sum[...]), lines[0])
    light_ref[1:2, :] = lines[1]


def block_gradients(f, sums_ref):
    def summed(q):
        start = q * CHUNKS * SUM_PITCH
        parts = [sums_ref[pl.ds(start + i, CHUNKS, stride=SUM_PITCH), :] for i in range(SUBS)]
        while len(parts) > 1:
            parts = [a + b for a, b in zip(parts[::2], parts[1::2])]
        return parts[0]

    z = [summed(q) for q in range(SUMS)]
    vt, vb, vn = f["vt"], f["vb"], f["vn"]
    uv = z[SH] * f["rwv"] * f["rcv"]
    wv = -z[SH] * f["rwv"] * f["cv"] * f["vroot"]
    ax2, ay2, ix2, iy2 = f["ax2"], f["ay2"], f["ix2"], f["iy2"]
    pt, pb = uv * vt * ax2, uv * vb * ay2
    tau_x = (ay2 - 1.0) * z[V23] - z[TX] - (pb * vn + wv * vb)
    tau_y = (1.0 - ax2) * z[V13] + z[TY] + (pt * vn + wv * vt)
    tau_z = (iy2 * ax2 - 1.0) * z[V12] + (ay2 * ix2 - 1.0) * (z[U12] + pt * vb)
    turned = tau_x + f["inv"] * f["along"] * tau_z
    grads = [z[SD0 + c] * (0.5 / math.pi) for c in range(3)]
    grads += [z[SS0 + c] * f["lobe"] for c in range(3)]
    grads.append(z[V11] - (z[U11] + pt * vt) - z[SH])
    grads.append(z[V22] - (z[U22] + pb * vb) - z[SH])
    grads.append(f["kappa"] * (f["t_loc"][1] * tau_y - f["b_loc"][1] * turned))
    grads.append(f["kappa"] * (f["t_loc"][2] * tau_y - f["b_loc"][2] * turned))
    grads.append(tau_z * f["inv"] * f["inv"] * f["kappa"])
    grads.append((z[SF] - z[SH]) * f["inv_f1"])
    return grads


def local_gradients(observed, shadow, view_ids, points, frames, params, power, pos, cameras):
    lights, pixels = shadow.shape
    hbm = pl.BlockSpec(memory_space=pltpu.HBM)
    vmem = pl.BlockSpec(memory_space=pltpu.VMEM)
    return pl.pallas_call(
        gradient_kernel,
        in_specs=[pl.BlockSpec(memory_space=pltpu.SMEM)] + [hbm] * 6 + [vmem] * 2,
        out_specs=[vmem, vmem],
        out_shape=[
            jax.ShapeDtypeStruct((pixels // LANES * ROWS, LANES), jnp.float32),
            jax.ShapeDtypeStruct((2, LANES), jnp.float32),
        ],
        scratch_shapes=[
            pltpu.VMEM(observed.shape, observed.dtype),
            pltpu.VMEM(shadow.shape, jnp.int32),
            pltpu.VMEM((pixels // LANES, LANES), jnp.int32),
            pltpu.VMEM(points.shape, jnp.float32),
            pltpu.VMEM(frames.shape, jnp.float32),
            pltpu.VMEM(params.shape, jnp.float32),
            pltpu.VMEM((CHUNKS * RAW, LANES), jnp.float32),
            pltpu.VMEM((TABLE, CHUNKS, LANES), jnp.float32),
            pltpu.VMEM((SUMS * CHUNKS * SUM_PITCH, LANES), jnp.float32),
            pltpu.VMEM((lights, DEPTH), jnp.bfloat16),
            pltpu.VMEM((BLOCKS * CHUNKS * PITCH, LANES), jnp.float32),
            pltpu.VMEM((lights, BLOCKS * LANES), jnp.float32),
            pltpu.VMEM((lights, BLOCKS * LANES), jnp.float32),
            pltpu.VMEM((CHUNKS, DEPTH, BLOCKS * LANES), jnp.bfloat16),
            pltpu.VMEM((3, lights, LANES), jnp.float32),
            pltpu.VMEM((3, lights, LANES), jnp.float32),
            pltpu.VMEM((lights, 16), jnp.float32),
            pltpu.VMEM((SUBS, LANES), jnp.float32),
            pltpu.SemaphoreType.DMA((2, 6)),
        ],
        compiler_params=pltpu.CompilerParams(vmem_limit_bytes=16 << 20),
        name="pair_gradients",
    )(
        *(
            pltpu.with_memory_space_constraint(x, pltpu.HBM)
            for x in (
                cameras, observed, shadow, view_ids.reshape(pixels // LANES, LANES),
                points, frames, params, power, pos,
            )
        )
    )


def share_kernel(mark, arrived_ref, light_ref, share_ref, spread_ref):
    parts, rows = arrived_ref.shape[:2]
    squares = jnp.zeros((SUBS, LANES), jnp.float32)
    for at in range(0, rows, SUBS):
        pieces = [arrived_ref[i, at : at + SUBS, :] for i in range(parts)]
        while len(pieces) > 1:
            pieces = [a + b for a, b in zip(pieces[::2], pieces[1::2])]
        share_ref[at : at + SUBS, :] = pieces[0]
        squares = squares + pieces[0] * pieces[0]
    lane = lax.broadcasted_iota(jnp.int32, (2, LANES), 1)
    deep = lax.broadcasted_iota(jnp.int32, (2, LANES), 0)
    tile = jnp.where((lane == mark) & (deep == 1), whole(squares), light_ref[...])
    for i in range(spread_ref.shape[0]):
        spread_ref[i] = tile


def join_kernel(mark, share_ref, light_parts_ref, out_ref, light_ref):
    tile = light_parts_ref[0]
    for i in range(1, light_parts_ref.shape[0]):
        tile = tile + light_parts_ref[i]
    light_ref[...] = tile
    lane = lax.broadcasted_iota(jnp.int32, (2, LANES), 1)
    light_sq = whole(jnp.where(lane < mark, tile * tile, 0.0))
    deep = lax.broadcasted_iota(jnp.int32, (SUBS, LANES), 0)
    wide = lax.broadcasted_iota(jnp.int32, (SUBS, LANES), 1)
    tail = jnp.where(wide == 0, light_sq, 0.0)
    tail = jnp.where(wide == 1, tile[0:1, mark : mark + 1], tail)
    tail = jnp.where(wide == 2, tile[1:2, mark : mark + 1], tail)
    tail = jnp.where(deep == 0, tail, 0.0)
    rows = share_ref.shape[0]
    for at in range(0, rows, SUBS):
        value = share_ref[at : at + SUBS, :]
        for i in range(out_ref.shape[0]):
            out_ref[i, at : at + SUBS, :] = value
    for i in range(out_ref.shape[0]):
        out_ref[i, rows : rows + SUBS, :] = tail


def step_kernel(
    pixel_total, light_total, gathered_ref, light_ref, params_ref, power_ref, pos_ref,
    new_params_ref, new_power_ref, new_pos_ref, loss_ref,
):
    parts, rows = gathered_ref.shape[0], gathered_ref.shape[1] - SUBS
    tail = gathered_ref[0, rows : rows + SUBS, :]
    for i in range(1, parts):
        tail = tail + gathered_ref[i, rows : rows + SUBS, :]
    light_scale = STRIDE * lax.rsqrt(tail[0:1, 0:1] / (6 * light_total) + EPS)
    pixel_scale = STRIDE * lax.rsqrt(tail[0:1, 2:3] / (ROWS * pixel_total) + EPS)
    loss_ref[...] = tail[0:1, 1:2] / (3.0 * light_total * pixel_total)
    lights = power_ref.shape[1]
    for c in range(3):
        cut = slice(c * lights, (c + 1) * lights)
        new_power_ref[c : c + 1, :] = power_ref[c : c + 1, :] - light_ref[0:1, cut] * light_scale
        new_pos_ref[c : c + 1, :] = pos_ref[c : c + 1, :] - light_ref[1:2, cut] * light_scale
    chunks = rows // ROWS
    for i in range(parts):
        for k in range(chunks):
            cut = slice((i * chunks + k) * LANES, (i * chunks + k + 1) * LANES)
            grad = gathered_ref[i, k * ROWS : (k + 1) * ROWS, :]
            new_params_ref[:, cut] = params_ref[:, cut] - grad * pixel_scale


def broadcast_exchange(x, axes):
    return lax.all_to_all(x, axes, split_axis=0, concat_axis=0, tiled=True)


def shards(observed, shadow, view_ids, points, frames, params, power, pos, cameras):
    lights, pixels = shadow.shape
    px_size, lt_size = lax.axis_size(PX), lax.axis_size(LT)
    grads, light_tile = local_gradients(
        observed, shadow, view_ids, points, frames, params, power, pos, cameras
    )
    share_rows = grads.shape[0] // lt_size
    mark = 3 * lights
    small = pltpu.CompilerParams(vmem_limit_bytes=8 << 20)
    arrived = broadcast_exchange(grads.reshape(lt_size, share_rows, LANES), SHARES)
    share, spread = pl.pallas_call(
        functools.partial(share_kernel, mark),
        out_shape=(
            jax.ShapeDtypeStruct((share_rows, LANES), jnp.float32),
            jax.ShapeDtypeStruct((px_size, 2, LANES), jnp.float32),
        ),
        compiler_params=small,
        name="share_sum",
    )(arrived, light_tile)
    light_parts = broadcast_exchange(spread, BLOCK_SUMS)
    joined, own_lights = pl.pallas_call(
        functools.partial(join_kernel, mark),
        out_shape=(
            jax.ShapeDtypeStruct((lt_size, share_rows + SUBS, LANES), jnp.float32),
            jax.ShapeDtypeStruct((2, LANES), jnp.float32),
        ),
        compiler_params=small,
        name="join",
    )(share, light_parts)
    gathered = broadcast_exchange(joined, SHARES)
    new_params, new_power, new_pos, loss = pl.pallas_call(
        functools.partial(step_kernel, pixels * px_size, lights * lt_size),
        out_shape=(
            jax.ShapeDtypeStruct(params.shape, jnp.float32),
            jax.ShapeDtypeStruct(power.shape, jnp.float32),
            jax.ShapeDtypeStruct(pos.shape, jnp.float32),
            jax.ShapeDtypeStruct((1, 1), jnp.float32),
        ),
        compiler_params=small,
        name="step",
    )(gathered, own_lights, params, power, pos)
    return new_params, new_power, new_pos, loss.reshape(())


def solution(mesh):
    torus = Mesh(mesh.devices.reshape(4, 4, 2, 8, 2), PX + LT)
    placed = (
        P(None, LT, PX),
        P(LT, PX),
        P(PX),
        P(None, PX),
        P(None, PX),
        P(None, PX),
        P(None, LT),
        P(None, LT),
        P(),
    )
    return jax.shard_map(
        shards,
        mesh=torus,
        in_specs=placed,
        out_specs=(P(None, PX), P(None, LT), P(None, LT), P()),
        check_vma=False,
    )
```
